32 devices in a mesh: dp: 8 (over z, y), mp: 4 (over x, core).
Axes of the slice: x: 2, y: 2, z: 4, core: 2. Of those that a mesh axis runs over, the one named last changes fastest.
Arguments:
- x_in: bfloat16 [8192, 768], P(('dp', 'mp')), may hold values from -6 to 6
- out_grad: bfloat16 [8192, 768], P(('dp', 'mp')), may hold values from -6 to 6
- doc_lengths: int32 [8, 8], P('dp'), may hold values from 1 to 512, 1024 in all within a row
- keep_layer: int32 [8], P('dp'), may hold values 0 or 1
- w_qkv: float32 [2, 3, 768, 768], P(None, None, 'dp', 'mp'), may hold values from -0.21875 to 0.21875
- w_o: float32 [2, 768, 768], P(None, 'mp', 'dp'), may hold values from -0.625 to 0.625
- w_in: float32 [2, 768, 3072], P(None, 'dp', 'mp'), may hold values from -0.21875 to 0.21875
- w_out: float32 [2, 3072, 768], P(None, 'mp', 'dp'), may hold values from -0.109375 to 0.109375
- b_qv: float32 [2, 2, 768], P(None, None, 'mp'), may hold values from -1.2 to 1.2
- b_in: float32 [2, 3072], P(None, 'mp'), may hold values from -1.2 to 1.2
- ln_gain: float32 [2, 2, 768], replicated, may hold values from 0.5 to 1.5
- shifts: float32 [2, 4, 768], replicated, may hold values from -1.2 to 1.2
- m_qkv: float32 [2, 3, 768, 768], P(None, None, 'dp', 'mp'), may hold values from -3 to 3
- m_o: float32 [2, 768, 768], P(None, 'mp', 'dp'), may hold values from -3 to 3
- m_in: float32 [2, 768, 3072], P(None, 'dp', 'mp'), may hold values from -3 to 3
- m_out: float32 [2, 3072, 768], P(None, 'mp', 'dp'), may hold values from -3 to 3
- m_qv: float32 [2, 2, 768], P(None, None, 'mp'), may hold values from -6 to 6
- m_bin: float32 [2, 3072], P(None, 'mp'), may hold values from -6 to 6
- m_gain: float32 [2, 2, 768], replicated, may hold values from -6 to 6
- m_shift: float32 [2, 4, 768], replicated, may hold values from -6 to 6
- e_qkv: float32 [8, 2, 3, 768, 768], P('dp', None, None, None, 'mp'), may hold values from -30 to 30
- e_o: float32 [8, 2, 768, 768], P('dp', None, 'mp'), may hold values from -30 to 30
- e_in: float32 [8, 2, 768, 3072], P('dp', None, None, 'mp'), may hold values from -30 to 30
- e_out: float32 [8, 2, 3072, 768], P('dp', None, 'mp'), may hold values from -30 to 30
- q_qkv: float32 [2, 3, 768, 8], P(None, None, 'mp'), may hold values from -6 to 6
- q_o: float32 [2, 3072, 8], P(None, 'mp'), may hold values from -6 to 6
- q_in: float32 [2, 3072, 8], P(None, 'mp'), may hold values from -6 to 6
- q_out: float32 [2, 3072, 8], P(None, 'mp'), may hold values from -6 to 6
Outputs:
- block_output: float32 [8192, 768], P(('dp', 'mp'))
- input_gradient: float32 [8192, 768], P(('dp', 'mp'))
- new_w_qkv: float32 [2, 3, 768, 768], P(None, None, 'dp', 'mp')
- new_w_o: float32 [2, 768, 768], P(None, 'mp', 'dp')
- new_w_in: float32 [2, 768, 3072], P(None, 'dp', 'mp')
- new_w_out: float32 [2, 3072, 768], P(None, 'mp', 'dp')
- new_b_qv: float32 [2, 2, 768], P(None, None, 'mp')
- new_b_in: float32 [2, 3072], P(None, 'mp')
- new_gain: float32 [2, 2, 768], replicated
- new_shifts: float32 [2, 4, 768], replicated
- new_m_qkv: float32 [2, 3, 768, 768], P(None, None, 'dp', 'mp')
- new_m_o: float32 [2, 768, 768], P(None, 'mp', 'dp')
- new_m_in: float32 [2, 768, 3072], P(None, 'dp', 'mp')
- new_m_out: float32 [2, 3072, 768], P(None, 'mp', 'dp')
- new_m_qv: float32 [2, 2, 768], P(None, None, 'mp')
- new_m_bin: float32 [2, 3072], P(None, 'mp')
- new_m_gain: float32 [2, 2, 768], replicated
- new_m_shift: float32 [2, 4, 768], replicated
- new_e_qkv: float32 [8, 2, 3, 768, 768], P('dp', None, None, None, 'mp')
- new_e_o: float32 [8, 2, 768, 768], P('dp', None, 'mp')
- new_e_in: float32 [8, 2, 768, 3072], P('dp', None, None, 'mp')
- new_e_out: float32 [8, 2, 3072, 768], P('dp', None, 'mp')
- p_qkv: float32 [2, 3, 3072, 8], P(None, None, 'mp')
- p_o: float32 [2, 768, 8], P(None, 'mp')
- p_in: float32 [2, 3072, 8], P(None, 'mp')
- p_out: float32 [2, 3072, 8], P(None, 'mp')
- new_q_qkv: float32 [2, 3, 768, 8], P(None, None, 'mp')
- new_q_o: float32 [2, 3072, 8], P(None, 'mp')
- new_q_in: float32 [2, 3072, 8], P(None, 'mp')
- new_q_out: float32 [2, 3072, 8], P(None, 'mp')
The draws below stay inside these ranges and needn't reach their ends.
Inputs may be any that keep to these rules, and one draw needn't show every extreme that they name: `doc_lengths`: each row holds the 8 document lengths of one replica, which sum to 1024; the longest document of every replica has exactly 512 tokens.
All inputs are finite; a program needn't handle non-finite values. No bound on the sum of `keep_layer` on one device may be relied on, other than what follows from the above.
Results may differ from the reference program's by a relative error of at most 0.02.
Values may be sent and summed in bfloat16 or wider, within the bound.
No kernel may reach another device: no remote copies, remote signals or barrier semaphores. Data moves between devices by JAX's collectives and lax.ppermute only.
A program may use at most 192 MiB of HBM per device.

```python
import math
import jax
import jax.numpy as jnp
import numpy as np
from jax import lax

D = 768
H = 12
HD = 64
FF = 3072
HH = 768
RANK = 8
TOK = 1024
LONG = 512
SLOTS = 8
TOKENS = 8192
DM = 3072
N_DP = 8
N_MP = 4


def place_ends(entries, rng, smallest, top_value):
    spot = [jax.random.randint(jax.random.fold_in(rng, axis), (), 0, length) for axis, length in enumerate(entries.shape)]
    widest = entries.shape.index(max(entries.shape))
    beside = spot[:widest] + [(spot[widest] + 1) % entries.shape[widest]] + spot[widest + 1:]
    return entries.at[tuple(spot)].set(smallest).at[tuple(beside)].set(top_value)


def levels(rng, shape, split, smallest, top_value):
    def one(position, shards_of):
        draws = jax.random.uniform(jax.random.fold_in(jax.random.fold_in(rng, 6), position), (shards_of,), jnp.float32, smallest / len(split), top_value / len(split))
        return jnp.repeat(jnp.exp(draws), shape[position] // shards_of).reshape((-1,) + (1,) * (len(shape) - position - 1))

    level = one(*split[0])
    for cut in split[1:]:
        level = level * one(*cut)
    return level


def split_up(number_of, total, reach, lean):
    loads = [(1 << 20) // math.isqrt(standing ** lean) + 1 for standing in range(2, number_of + 1)]
    spare, holding = total - reach - (number_of - 1), [1] * (number_of - 1)
    while spare > 0:
        free = [i for i in range(number_of - 1) if holding[i] < reach]
        whole, remaining = sum([loads[i] for i in free]), spare
        for i in free:
            more = min(reach - holding[i], max(1, remaining * loads[i] // whole), spare)
            holding[i] = holding[i] + more
            spare = spare - more
    return np.array([reach] + holding)


def uneven(rng, count, total, most, lean):
    if count == 2:
        one = jax.random.randint(rng, (), max(1, total - most), min(most, total - 1) + 1)
        return jnp.stack([one, total - one])
    sizes = jnp.asarray(split_up(count, total, most, lean), jnp.int32)
    twos = (count - 1) // 2
    giver, receiver = sizes[1:1 + 2 * twos:2], sizes[2:2 + 2 * twos:2]
    margin = jnp.minimum(giver - 1, most - receiver)
    moved = jax.random.randint(jax.random.fold_in(rng, 1), (twos,), 0, 1 << 20) % (margin + 1)
    sizes = sizes.at[1:1 + 2 * twos:2].set(giver - moved).at[2:2 + 2 * twos:2].set(receiver + moved)
    return sizes[jax.random.permutation(jax.random.fold_in(rng, 2), count)]


def normal_values(key, dims, scale, bound, cuts=(), kind=jnp.bfloat16):
    result = scale * jax.random.normal(key, dims, jnp.float32)
    if cuts:
        result = result * levels(key, dims, cuts, -0.22, 0.18)
    return jnp.clip(result, -bound, bound).astype(kind)


def setup_inputs(seed: int = 0) -> dict:
    arg_keys = jax.random.split(jax.random.key(seed), 29)
    return {
        "x_in": normal_values(arg_keys[0], (TOKENS, D), 1.0, 6.0, ((0, 32),)),
        "out_grad": normal_values(arg_keys[1], (TOKENS, D), 1.0, 6.0, ((0, 32),)),
        "doc_lengths": jax.vmap(lambda own: uneven(own, SLOTS, TOK, LONG, 2))(jax.random.split(arg_keys[2], N_DP)).reshape((N_DP, SLOTS)).astype(jnp.int32),
        "keep_layer": place_ends((jax.random.randint(arg_keys[3], (N_DP,), 0, 2) < 1).astype(jnp.int32), jax.random.fold_in(arg_keys[3], 1), 0, 1),
        "w_qkv": normal_values(arg_keys[4], (2, 3, D, HH), D ** -0.5, 0.21875, ((2, 8), (3, 4)), jnp.float32),
        "w_o": normal_values(arg_keys[5], (2, HH, D), (HH // 8) ** -0.5, 0.625, ((1, 4), (2, 8)), jnp.float32),
        "w_in": normal_values(arg_keys[6], (2, D, FF), D ** -0.5, 0.21875, ((1, 8), (2, 4)), jnp.float32),
        "w_out": normal_values(arg_keys[7], (2, FF, D), FF ** -0.5, 0.109375, ((1, 4), (2, 8)), jnp.float32),
        "b_qv": normal_values(arg_keys[8], (2, 2, HH), 0.2, 1.2, ((2, 4),), jnp.float32),
        "b_in": normal_values(arg_keys[9], (2, FF), 0.2, 1.2, ((1, 4),), jnp.float32),
        "ln_gain": jnp.clip(1.0 + 0.1 * jax.random.normal(arg_keys[10], (2, 2, D), jnp.float32), 0.5, 1.5),
        "shifts": normal_values(arg_keys[11], (2, 4, D), 0.2, 1.2, (), jnp.float32),
        "m_qkv": normal_values(arg_keys[12], (2, 3, D, HH), 0.5, 3.0, ((2, 8), (3, 4)), jnp.float32),
        "m_o": normal_values(arg_keys[13], (2, HH, D), 0.5, 3.0, ((1, 4), (2, 8)), jnp.float32),
        "m_in": normal_values(arg_keys[14], (2, D, FF), 0.5, 3.0, ((1, 8), (2, 4)), jnp.float32),
        "m_out": normal_values(arg_keys[15], (2, FF, D), 0.5, 3.0, ((1, 4), (2, 8)), jnp.float32),
        "m_qv": normal_values(arg_keys[16], (2, 2, HH), 1.0, 6.0, ((2, 4),), jnp.float32),
        "m_bin": normal_values(arg_keys[17], (2, FF), 1.0, 6.0, ((1, 4),), jnp.float32),
        "m_gain": normal_values(arg_keys[18], (2, 2, D), 1.0, 6.0, (), jnp.float32),
        "m_shift": normal_values(arg_keys[19], (2, 4, D), 1.0, 6.0, (), jnp.float32),
        "e_qkv": normal_values(arg_keys[20], (N_DP, 2, 3, D, HH), (1.0 + TOK // 256), 30.0, ((0, 8), (4, 4)), jnp.float32),
        "e_o": normal_values(arg_keys[21], (N_DP, 2, HH, D), (1.0 + TOK // 256), 30.0, ((0, 8), (2, 4)), jnp.float32),
        "e_in": normal_values(arg_keys[22], (N_DP, 2, D, FF), (1.0 + TOK // 256), 30.0, ((0, 8), (3, 4)), jnp.float32),
        "e_out": normal_values(arg_keys[23], (N_DP, 2, FF, D), (1.0 + TOK // 256), 30.0, ((0, 8), (2, 4)), jnp.float32),
        "q_qkv": normal_values(arg_keys[24], (2, 3, HH, RANK), 1.0, 6.0, ((2, 4),), jnp.float32),
        "q_o": normal_values(arg_keys[25], (2, DM, RANK), 1.0, 6.0, ((1, 4),), jnp.float32),
        "q_in": normal_values(arg_keys[26], (2, FF, RANK), 1.0, 6.0, ((1, 4),), jnp.float32),
        "q_out": normal_values(arg_keys[27], (2, DM, RANK), 1.0, 6.0, ((1, 4),), jnp.float32),
    }


NORM_EPS = 1e-05
ORTHO_EPS = 1e-06
MOMENTUM = 0.9
RATE = 0.05
MASKED = -1000000000.0
ROOT_HALF = 0.7071067811865476
HIGHEST = lax.Precision.HIGHEST

@jax.custom_vjp
def low(v):
    return lax.optimization_barrier(v.astype(jnp.bfloat16)).astype(jnp.float32)

@jax.custom_vjp
def low_back(v):
    return v

def low_keep(v):
    return (low(v), None)

def low_pass(kept, grad):
    return (grad,)

def back_keep(v):
    return (v, None)

def back_low(kept, grad):
    return (low(grad),)
low.defvjp(low_keep, low_pass)
low_back.defvjp(back_keep, back_low)

def rounded_both(value):
    return low_back(low(value))

def matmul(left, right):
    return jnp.dot(left, right, precision=HIGHEST, preferred_element_type=jnp.float32)

def gelu_value(upper):
    return 0.5 * upper * (1.0 + lax.erf(upper * ROOT_HALF))

def layer_norm(rows_in, gain, shift):
    centred = rows_in - lax.optimization_barrier(jnp.mean(rows_in, axis=-1, keepdims=True))
    inverse = lax.rsqrt(lax.optimization_barrier(jnp.mean(centred * centred, axis=-1, keepdims=True)) + NORM_EPS)
    return centred * inverse * gain + shift

def doc_positions(lengths, count):
    ends = jnp.cumsum(lengths)
    places = jnp.arange(count, dtype=jnp.int32)
    return lax.optimization_barrier(jnp.sum((places[:, None] >= ends[None, :]).astype(jnp.int32), axis=1))

def orthogonal(factor):
    rank = factor.shape[-1]
    for column in range(rank):
        vector = factor[..., column:column + 1]
        vector = vector * lax.rsqrt(lax.optimization_barrier(jnp.sum(vector * vector, axis=-2, keepdims=True)) + ORTHO_EPS)
        remain = factor[..., column + 1:]
        remain = remain - vector * lax.optimization_barrier(jnp.sum(vector * remain, axis=-2, keepdims=True))
        factor = jnp.concatenate([factor[..., :column], vector, remain], axis=-1)
    return factor

def attention(query, keys, values, docs):
    count = query.shape[0]
    same = docs[:, None] == docs[None, :]
    scale = HD ** (-0.5)

    def one_head(inputs):
        query_head, key_head, value_head = inputs
        scores = low_back(matmul(query_head, key_head.T) * scale)
        scores = jnp.where(same, scores, MASKED)
        probs = low(jax.nn.softmax(scores, axis=-1))
        return matmul(probs, value_head)

    def split_heads(matrix):
        return matrix.reshape(count, H, HD).transpose(1, 0, 2)
    mixed = lax.map(jax.checkpoint(one_head), (split_heads(query), split_heads(keys), split_heads(values)))
    return mixed.transpose(1, 0, 2).reshape(count, H * HD)

def layer(resid, params, docs):
    w_proj, w_back, w_up, w_down, b_proj, b_up, gains, shift_rows = params
    low_in = low(resid)
    query = rounded_both(matmul(low_in, w_proj[0]) + b_proj[0])
    keys = rounded_both(matmul(low_in, w_proj[1]))
    values = rounded_both(matmul(low_in, w_proj[2]) + b_proj[1])
    attended = rounded_both(attention(query, keys, values, docs))
    mixed_one = low_back(matmul(attended, w_back)) + shift_rows[0] + resid
    hidden = layer_norm(mixed_one, gains[0], shift_rows[1])
    low_hidden = low(hidden)
    upper = low_back(matmul(low_hidden, w_up) + b_up)
    activated = low(gelu_value(upper))
    mixed_two = low_back(matmul(activated, w_down)) + shift_rows[2] + hidden
    return layer_norm(mixed_two, gains[1], shift_rows[3])

def forward(params, resid, docs, keep):
    w_qkv, w_o, w_in, w_out, b_qv, b_in, ln_gain, shifts = params
    w_qkv = low(w_qkv)
    w_o = low(w_o)
    w_in = low(w_in)
    w_out = low(w_out)
    first = layer(resid, (w_qkv[0], w_o[0], w_in[0], w_out[0], b_qv[0], b_in[0], ln_gain[0], shifts[0]), docs)
    second = layer(first, (w_qkv[1], w_o[1], w_in[1], w_out[1], b_qv[1], b_in[1], ln_gain[1], shifts[1]), docs)
    return jnp.where(keep > 0, second, first)

def compress_blocks(totals, starts):
    firsts = lax.optimization_barrier(jnp.sum(jnp.einsum('...mn,...nr->...mr', totals, starts[None], precision=HIGHEST), axis=0))
    bases = orthogonal(firsts)
    seconds = lax.optimization_barrier(jnp.sum(jnp.einsum('...mn,...mr->...nr', totals, bases[None], precision=HIGHEST), axis=0))
    approx = jnp.einsum('...mr,...nr->...mn', bases, seconds, precision=HIGHEST) / N_DP
    return (bases, seconds, approx, totals - approx[None])

def reference(x_in, out_grad, doc_lengths, keep_layer, w_qkv, w_o, w_in, w_out, b_qv, b_in, ln_gain, shifts, m_qkv, m_o, m_in, m_out, m_qv, m_bin, m_gain, m_shift, e_qkv, e_o, e_in, e_out, q_qkv, q_o, q_in, q_out):
    params = (w_qkv, w_o, w_in, w_out, b_qv, b_in, ln_gain, shifts)
    inputs = x_in.astype(jnp.float32).reshape(N_DP, TOK, D)
    cotangents = out_grad.astype(jnp.float32).reshape(N_DP, TOK, D)

    def replica(inputs_one):
        resid, cotangent, lengths, keep = inputs_one
        docs = doc_positions(lengths, TOK)

        def apply(weights, rows_in):
            return forward(weights, rows_in, docs, keep)
        output, pullback = jax.vjp(apply, params, resid)
        weight_grads, input_grad = pullback(cotangent)
        return (output, input_grad, weight_grads)
    outputs, input_grads, grads = lax.map(replica, (inputs, cotangents, doc_lengths, keep_layer))
    head_cols = HH // N_MP
    unit_cols = FF // N_MP
    totals = (grads[0] + e_qkv).reshape(N_DP, 2, 3, D, N_MP, head_cols).transpose(0, 1, 2, 4, 3, 5)
    bases, seconds, approx, errors = compress_blocks(totals, q_qkv.reshape(2, 3, N_MP, head_cols, RANK))
    approx_qkv = approx.transpose(0, 1, 3, 2, 4).reshape(2, 3, D, HH)
    new_e_qkv = errors.transpose(0, 1, 2, 4, 3, 5).reshape(N_DP, 2, 3, D, HH)
    p_qkv = bases.reshape(2, 3, N_MP * D, RANK)
    new_q_qkv = seconds.reshape(2, 3, HH, RANK)
    totals = (grads[1] + e_o).reshape(N_DP, 2, N_MP, head_cols, D)
    bases, seconds, approx, errors = compress_blocks(totals, q_o.reshape(2, N_MP, D, RANK))
    approx_o = approx.reshape(2, HH, D)
    new_e_o = errors.reshape(N_DP, 2, HH, D)
    p_o = bases.reshape(2, HH, RANK)
    new_q_o = seconds.reshape(2, N_MP * D, RANK)
    totals = (grads[2] + e_in).reshape(N_DP, 2, D, N_MP, unit_cols).transpose(0, 1, 3, 2, 4)
    bases, seconds, approx, errors = compress_blocks(totals, q_in.reshape(2, N_MP, unit_cols, RANK))
    approx_in = approx.transpose(0, 2, 1, 3).reshape(2, D, FF)
    new_e_in = errors.transpose(0, 1, 3, 2, 4).reshape(N_DP, 2, D, FF)
    p_in = bases.reshape(2, N_MP * D, RANK)
    new_q_in = seconds.reshape(2, FF, RANK)
    totals = (grads[3] + e_out).reshape(N_DP, 2, N_MP, unit_cols, D)
    bases, seconds, approx, errors = compress_blocks(totals, q_out.reshape(2, N_MP, D, RANK))
    approx_out = approx.reshape(2, FF, D)
    new_e_out = errors.reshape(N_DP, 2, FF, D)
    p_out = bases.reshape(2, FF, RANK)
    new_q_out = seconds.reshape(2, N_MP * D, RANK)
    new_m_qkv = MOMENTUM * m_qkv + approx_qkv
    new_m_o = MOMENTUM * m_o + approx_o
    new_m_in = MOMENTUM * m_in + approx_in
    new_m_out = MOMENTUM * m_out + approx_out
    new_m_qv = MOMENTUM * m_qv + lax.optimization_barrier(jnp.sum(grads[4], axis=0)) / N_DP
    new_m_bin = MOMENTUM * m_bin + lax.optimization_barrier(jnp.sum(grads[5], axis=0)) / N_DP
    new_m_gain = MOMENTUM * m_gain + lax.optimization_barrier(jnp.sum(grads[6], axis=0)) / N_DP
    new_m_shift = MOMENTUM * m_shift + lax.optimization_barrier(jnp.sum(grads[7], axis=0)) / N_DP
    return (outputs.reshape(N_DP * TOK, D), input_grads.reshape(N_DP * TOK, D), w_qkv - RATE * new_m_qkv, w_o - RATE * new_m_o, w_in - RATE * new_m_in, w_out - RATE * new_m_out, b_qv - RATE * new_m_qv, b_in - RATE * new_m_bin, ln_gain - RATE * new_m_gain, shifts - RATE * new_m_shift, new_m_qkv, new_m_o, new_m_in, new_m_out, new_m_qv, new_m_bin, new_m_gain, new_m_shift, new_e_qkv, new_e_o, new_e_in, new_e_out, p_qkv, p_o, p_in, p_out, new_q_qkv, new_q_o, new_q_in, new_q_out)
```

```python
import jax
import jax.numpy as jnp
from jax import lax
from jax.sharding import PartitionSpec as P

HD = 64


NORM_EPS = 1e-05
ORTHO_EPS = 1e-06
MOMENTUM = 0.9
RATE = 0.05
MASKED = -1000000000.0
ROOT_HALF = 0.7071067811865476
INV_ROOT_TWO_PI = 0.3989422804014327
HIGHEST = lax.Precision.HIGHEST
LOW = jnp.bfloat16
F32 = jnp.float32


def dot(left, right, left_dim, right_dim, precision=None):
    return lax.dot_general(
        left,
        right,
        (((left_dim,), (right_dim,)), ((), ())),
        preferred_element_type=F32,
        precision=precision,
    )


def swap(value, axis, bit):
    size = lax.axis_size(axis)
    return lax.ppermute(value, axis, [(i, i ^ bit) for i in range(size)])


def gelu_parts(upper):
    cdf = 0.5 * (1.0 + lax.erf(upper * ROOT_HALF))
    slope = cdf + upper * jnp.exp(-0.5 * upper * upper) * INV_ROOT_TWO_PI
    return upper * cdf, slope


def norm_forward(rows_in, gain, shift):
    centred = rows_in - jnp.mean(rows_in, axis=-1, keepdims=True)
    inverse = lax.rsqrt(jnp.mean(centred * centred, axis=-1, keepdims=True) + NORM_EPS)
    normed = centred * inverse
    return (normed * gain + shift, normed, inverse)


def norm_backward(grad, normed, inverse, gain):
    scaled = grad * gain
    inner = jnp.mean(scaled * normed, axis=-1, keepdims=True)
    return inverse * (scaled - jnp.mean(scaled, axis=-1, keepdims=True) - normed * inner)


def doc_index(lengths, places):
    slots = jnp.arange(lengths.shape[0])
    ends = jnp.sum(jnp.where(slots[:, None] <= slots[None, :], lengths[:, None], 0), axis=0)
    return jnp.sum((places[:, None] >= ends[None, :]).astype(jnp.int32), axis=1)


def orthogonal_rows(factor):
    rank = factor.shape[-2]
    done = []
    for row in range(rank):
        vector = factor[..., :1, :]
        vector = vector * lax.rsqrt(jnp.sum(vector * vector, axis=-1, keepdims=True) + ORTHO_EPS)
        done.append(vector)
        if row + 1 < rank:
            remain = factor[..., 1:, :]
            factor = remain - vector * jnp.sum(vector * remain, axis=-1, keepdims=True)
    return jnp.concatenate(done, axis=-2)


def attend(query, keys, values, docs):
    count, width = query.shape
    heads = width // HD
    scale = HD ** (-0.5)
    same = docs[:, None] == docs[None, :]
    outs, logsums = [], []
    for head in range(heads):
        cols = slice(head * HD, (head + 1) * HD)
        scores = dot(query[:, cols], keys[:, cols], 1, 1) * scale
        scores = jnp.where(same, scores, MASKED)
        highest = jnp.max(scores, axis=-1, keepdims=True)
        logsum = highest + jnp.log(jnp.sum(jnp.exp(scores - highest), axis=-1, keepdims=True))
        probs = jnp.exp(scores - logsum).astype(LOW)
        outs.append(dot(probs, values[:, cols], 1, 0))
        logsums.append(logsum)
    return jnp.concatenate(outs, axis=1), logsums


def attend_back(query, keys, values, grad_out, logsums, docs):
    count, width = query.shape
    heads = width // HD
    scale = HD ** (-0.5)
    same = docs[:, None] == docs[None, :]
    dq, dk, dv = [], [], []
    for head in range(heads):
        cols = slice(head * HD, (head + 1) * HD)
        scores = dot(query[:, cols], keys[:, cols], 1, 1) * scale
        scores = jnp.where(same, scores, MASKED)
        probs = jnp.exp(scores - logsums[head])
        prob_grad = dot(grad_out[:, cols], values[:, cols], 1, 1)
        inner = jnp.sum(probs * prob_grad, axis=-1, keepdims=True)
        score_grad = (probs * (prob_grad - inner)).astype(LOW)
        dq.append(dot(score_grad, keys[:, cols], 1, 0) * scale)
        dk.append(dot(score_grad, query[:, cols], 0, 0) * scale)
        dv.append(dot(probs.astype(LOW), grad_out[:, cols], 0, 0))
    return jnp.concatenate(dq + dk + dv, axis=1).astype(LOW)


def core_sum(partial):
    half = partial.shape[0] // 2
    arrived = swap(partial[half:].astype(LOW), "mp", 1)
    return partial[:half] + arrived.astype(F32)


def chip_sum(part):
    arrived = swap(part.astype(LOW), "mp", 2).astype(F32)
    half = part.shape[0] // 2
    return part + jnp.concatenate([arrived[half:], arrived[:half]], axis=0)


def group_sum(partial):
    return chip_sum(core_sum(partial))


def core_whole(low_rows):
    return jnp.concatenate([low_rows, swap(low_rows, "mp", 1)], axis=0)


def layer_forward(resid, whole_in, params, docs):
    w_proj, w_back_t, w_up, w_down_t, b_proj, b_up, gains, shift_rows = params
    width = w_back_t.shape[1]
    projected = (dot(whole_in, w_proj, 1, 0) + b_proj).astype(LOW)
    query = projected[:, :width]
    keys = projected[:, width : 2 * width]
    values = projected[:, 2 * width :]
    attended, logsums = attend(query, keys, values, docs)
    attended = attended.astype(LOW)
    mixed_one = group_sum(dot(attended, w_back_t, 1, 1)) + shift_rows[0] + resid
    hidden, normed_one, inverse_one = norm_forward(mixed_one, gains[0], shift_rows[1])
    whole_hidden = core_whole(hidden.astype(LOW))
    upper = dot(whole_hidden, w_up, 1, 0) + b_up
    activated, slope = gelu_parts(upper)
    activated = activated.astype(LOW)
    mixed_two = group_sum(dot(activated, w_down_t, 1, 1)) + shift_rows[2] + hidden
    output, normed_two, inverse_two = norm_forward(mixed_two, gains[1], shift_rows[3])
    saved = (
        whole_in, query, keys, values, attended, logsums, normed_one, inverse_one,
        whole_hidden, slope, activated, normed_two, inverse_two,
    )
    return output, saved


def own_sum(rows):
    return jnp.sum(rows[: rows.shape[0] // 2], axis=0)


def layer_backward(grad_out, saved, params, docs):
    (
        whole_in, query, keys, values, attended, logsums, normed_one, inverse_one,
        whole_hidden, slope, activated, normed_two, inverse_two,
    ) = saved
    w_proj, w_back_t, w_up, w_down_t, b_proj, b_up, gains, shift_rows = params
    width = w_back_t.shape[1]
    mixed_two_grad = norm_backward(grad_out, normed_two, inverse_two, gains[1])
    piece = core_whole(mixed_two_grad.astype(LOW))
    upper_grad = (dot(piece, w_down_t, 1, 0) * slope).astype(LOW)
    hidden_part = dot(upper_grad, w_up, 1, 1)
    hidden_grad = group_sum(hidden_part) + mixed_two_grad
    down_grad = dot(activated, piece, 0, 0)
    up_grad = dot(whole_hidden, upper_grad, 0, 0)
    mixed_one_grad = norm_backward(hidden_grad, normed_one, inverse_one, gains[0])
    piece_one = core_whole(mixed_one_grad.astype(LOW))
    attended_grad = dot(piece_one, w_back_t, 1, 0).astype(LOW)
    proj_low = attend_back(query, keys, values, attended_grad, logsums, docs)
    back_grad = dot(attended, piece_one, 0, 0)
    proj_grad = dot(proj_low, whole_in, 0, 0)
    resid_part = dot(proj_low, w_proj, 1, 1)
    bias_sums = jnp.sum(proj_low.astype(F32), axis=0)
    grads = (
        proj_grad.reshape(3, width, -1),
        back_grad,
        up_grad,
        down_grad,
        jnp.stack([bias_sums[:width], bias_sums[2 * width :]]),
        jnp.sum(upper_grad.astype(F32), axis=0),
        jnp.stack([own_sum(hidden_grad * normed_one), own_sum(grad_out * normed_two)]),
        jnp.stack([own_sum(mixed_one_grad), own_sum(hidden_grad), own_sum(mixed_two_grad), own_sum(grad_out)]),
    )
    return grads, resid_part, mixed_one_grad


def sum_over(value, axis):
    bit = 1
    while bit < lax.axis_size(axis):
        value = value + swap(value, axis, bit)
        bit *= 2
    return value


def flat_rows(parts):
    return jnp.concatenate([part.reshape(-1) for part in parts])


def sum_many(parts, axes):
    total = flat_rows(parts)
    size = total.shape[0]
    total = jnp.pad(total, (0, -size % 1024)).reshape(-1, 128)
    for axis in axes:
        total = sum_over(total, axis)
    total = total.reshape(-1)
    outs, start = [], 0
    for part in parts:
        outs.append(total[start : start + part.size].reshape(part.shape))
        start += part.size
    return outs


def first_factors(totals, starts):
    mt_proj, m_back, m_up, m_down = totals
    s_proj, s_back, s_up, s_down = starts
    return [
        jnp.einsum("jnm,jrn->jrm", mt_proj, s_proj, precision=HIGHEST),
        dot(s_back, m_back, 1, 1, HIGHEST),
        dot(s_up, m_up, 1, 1, HIGHEST),
        dot(s_down, m_down, 1, 1, HIGHEST),
    ]


def second_factors(totals, bases):
    mt_proj, m_back, m_up, m_down = totals
    p_proj, p_back, p_up, p_down = bases
    return [
        jnp.einsum("jnm,jrm->jrn", mt_proj, p_proj, precision=HIGHEST),
        dot(p_back, m_back, 1, 0, HIGHEST),
        dot(p_up, m_up, 1, 0, HIGHEST),
        dot(p_down, m_down, 1, 0, HIGHEST),
    ]


def flip(value):
    return jnp.swapaxes(value, -1, -2)


def per_device(
    x_in, out_grad, doc_lengths, keep_layer, w_qkv, w_o, w_in, w_out, b_qv, b_in, ln_gain, shifts,
    m_qkv, m_o, m_in, m_out, m_qv, m_bin, m_gain, m_shift, e_qkv, e_o, e_in, e_out, q_qkv, q_o, q_in, q_out,
):
    own_rows = x_in.shape[0]
    replicas = lax.axis_size("dp")
    index = lax.axis_index("dp")
    place = lax.axis_index("mp")
    width = w_o.shape[1]

    def gather(piece):
        return lax.all_gather(piece, "dp", axis=0, tiled=True)

    def pieces(layer):
        return (
            jnp.concatenate([w_qkv[layer, 0], w_qkv[layer, 1], w_qkv[layer, 2], flip(w_o[layer])], axis=1).astype(LOW),
            w_in[layer].astype(LOW),
            flip(w_out[layer]).astype(LOW),
        )

    order = [0, 2, 1, 3]
    places = jnp.concatenate([(place ^ v) * own_rows + jnp.arange(own_rows) for v in order])
    docs = doc_index(doc_lengths[0], places)

    one = [gather(piece) for piece in pieces(0)]
    two = [gather(piece) for piece in pieces(1)]

    def params_of(layer, whole):
        b_proj = jnp.concatenate([b_qv[layer, 0], jnp.zeros((width,), F32), b_qv[layer, 1]])
        return (
            whole[0][:, : 3 * width], whole[0][:, 3 * width :], whole[1], whole[2],
            b_proj, b_in[layer], ln_gain[layer], shifts[layer],
        )

    set_in = jnp.concatenate([x_in, swap(x_in, "mp", 2)], axis=0)
    set_grad = jnp.concatenate([out_grad, swap(out_grad, "mp", 2)], axis=0)
    layer_one = params_of(0, one)
    layer_two = params_of(1, two)
    first, saved_one = layer_forward(set_in.astype(F32), core_whole(set_in), layer_one, docs)
    second, saved_two = layer_forward(first, core_whole(first.astype(LOW)), layer_two, docs)
    keep = keep_layer[0] > 0
    output = jnp.where(keep, second[:own_rows], first[:own_rows])
    grad = set_grad.astype(F32)
    grads_two, part_two, rest_two = layer_backward(jnp.where(keep, grad, 0.0), saved_two, layer_two, docs)
    back_two = group_sum(part_two) + rest_two

    errors = (flip(e_qkv[0]), e_o[0], e_in[0], e_out[0])
    starts = tuple(flip(q) for q in (q_qkv, q_o, q_in, q_out))

    def totals_of(grads, layer):
        return [grads[member] + errors[member][layer] for member in range(4)]

    def starts_of(layer):
        return [start[layer] for start in starts]

    totals_two = totals_of(grads_two, 1)
    firsts_two = first_factors(totals_two, starts_of(1))
    sums_two = sum_many(firsts_two + [grads_two[4], grads_two[5]], ("dp",))
    bases_two = [orthogonal_rows(f) for f in sums_two[:4]]
    seconds_two = second_factors(totals_two, bases_two)

    grads_one, part_one, rest_one = layer_backward(jnp.where(keep, back_two, grad), saved_one, layer_one, docs)
    last = core_sum(part_one)
    back_one = last[:own_rows] + swap(last[own_rows:].astype(LOW), "mp", 2).astype(F32) + rest_one[:own_rows]

    totals_one = totals_of(grads_one, 0)
    firsts_one = first_factors(totals_one, starts_of(0))
    sums_one = sum_many(firsts_one + [grads_one[4], grads_one[5]] + seconds_two, ("dp",))
    bases_one = [orthogonal_rows(f) for f in sums_one[:4]]
    seconds_one = second_factors(totals_one, bases_one)
    sums_last = sum_many(seconds_one, ("dp",))
    wide = [jnp.stack([grads_one[6], grads_two[6]]), jnp.stack([grads_one[7], grads_two[7]])]
    gain_sum, shift_sum = sum_many(wide, ("mp", "dp"))

    bases = (bases_one, bases_two)
    seconds = (sums_last, sums_one[6:])
    totals = (totals_one, totals_two)
    member_errors = []
    scaled = [[second / replicas for second in seconds[layer]] for layer in range(2)]

    def approx_of(layer, member):
        base, second = bases[layer][member], scaled[layer][member]
        if member == 0:
            return jnp.einsum("jrn,jrm->jnm", second, base, precision=HIGHEST)
        return dot(base, second, 0, 0, HIGHEST)

    for member in range(4):
        member_errors.append(
            jnp.stack([totals[layer][member] - approx_of(layer, member) for layer in range(2)])[None]
        )
    member_errors[0] = flip(member_errors[0])

    def part_of(value, axis):
        rows = value.shape[axis] // replicas
        return lax.dynamic_slice_in_dim(value, index * rows, rows, axis)

    def update_qkv(layer):
        base = part_of(bases[layer][0], 2)
        return jnp.einsum("jrm,jrn->jmn", base, scaled[layer][0], precision=HIGHEST)

    def update_o(layer):
        return dot(bases[layer][1], part_of(scaled[layer][1], 1), 0, 0, HIGHEST)

    def update_in(layer):
        return dot(part_of(bases[layer][2], 1), scaled[layer][2], 0, 0, HIGHEST)

    def update_out(layer):
        return flip(dot(part_of(scaled[layer][3], 1), bases[layer][3], 0, 0, HIGHEST))

    def renew(weight, moment, update):
        moment_new = MOMENTUM * moment + jnp.stack([update(0), update(1)])
        return weight - RATE * moment_new, moment_new

    new_w_qkv, new_m_qkv = renew(w_qkv, m_qkv, update_qkv)
    new_w_o, new_m_o = renew(w_o, m_o, update_o)
    new_w_in, new_m_in = renew(w_in, m_in, update_in)
    new_w_out, new_m_out = renew(w_out, m_out, update_out)
    new_m_qv = MOMENTUM * m_qv + jnp.stack([sums_one[4], sums_two[4]]) / replicas
    new_m_bin = MOMENTUM * m_bin + jnp.stack([sums_one[5], sums_two[5]]) / replicas
    new_m_gain = MOMENTUM * m_gain + gain_sum / replicas
    new_m_shift = MOMENTUM * m_shift + shift_sum / replicas
    outer = [flip(jnp.stack([bases_one[member], bases_two[member]])) for member in range(4)]
    inner = [flip(jnp.stack([seconds[0][member], seconds[1][member]])) for member in range(4)]
    return (
        output, back_one, new_w_qkv, new_w_o, new_w_in, new_w_out,
        b_qv - RATE * new_m_qv, b_in - RATE * new_m_bin, ln_gain - RATE * new_m_gain, shifts - RATE * new_m_shift,
        new_m_qkv, new_m_o, new_m_in, new_m_out, new_m_qv, new_m_bin, new_m_gain, new_m_shift,
        *member_errors, *outer, *inner,
    )


def solution(mesh):
    in_specs = (
        P(("dp", "mp"), None), P(("dp", "mp"), None), P("dp", None), P("dp"),
        P(None, None, "dp", "mp"), P(None, "mp", "dp"), P(None, "dp", "mp"), P(None, "mp", "dp"),
        P(None, None, "mp"), P(None, "mp"), P(), P(),
        P(None, None, "dp", "mp"), P(None, "mp", "dp"), P(None, "dp", "mp"), P(None, "mp", "dp"),
        P(None, None, "mp"), P(None, "mp"), P(), P(),
        P("dp", None, None, None, "mp"), P("dp", None, "mp", None), P("dp", None, None, "mp"), P("dp", None, "mp", None),
        P(None, None, "mp", None), P(None, "mp", None), P(None, "mp", None), P(None, "mp", None),
    )
    out_specs = (
        P(("dp", "mp"), None), P(("dp", "mp"), None),
        P(None, None, "dp", "mp"), P(None, "mp", "dp"), P(None, "dp", "mp"), P(None, "mp", "dp"),
        P(None, None, "mp"), P(None, "mp"), P(), P(),
        P(None, None, "dp", "mp"), P(None, "mp", "dp"), P(None, "dp", "mp"), P(None, "mp", "dp"),
        P(None, None, "mp"), P(None, "mp"), P(), P(),
        P("dp", None, None, None, "mp"), P("dp", None, "mp", None), P("dp", None, None, "mp"), P("dp", None, "mp", None),
        P(None, None, "mp", None), P(None, "mp", None), P(None, "mp", None), P(None, "mp", None),
        P(None, None, "mp", None), P(None, "mp", None), P(None, "mp", None), P(None, "mp", None),
    )
    return jax.shard_map(per_device, mesh=mesh, in_specs=in_specs, out_specs=out_specs, check_vma=False)
```

```python
import jax
import jax.numpy as jnp
from jax import lax
from jax.experimental import pallas as pl
from jax.experimental.pallas import tpu as pltpu
from jax.sharding import PartitionSpec as P

HD = 64


NORM_EPS = 1e-05
ORTHO_EPS = 1e-06
MOMENTUM = 0.9
RATE = 0.05
MASKED = -1000000000.0
ROOT_HALF = 0.7071067811865476
INV_ROOT_TWO_PI = 0.3989422804014327
HIGHEST = lax.Precision.HIGHEST
LOW = jnp.bfloat16
F32 = jnp.float32


def dot(left, right, left_dim, right_dim, precision=None):
    return lax.dot_general(
        left,
        right,
        (((left_dim,), (right_dim,)), ((), ())),
        preferred_element_type=F32,
        precision=precision,
    )


def swap(value, axis, bit):
    size = lax.axis_size(axis)
    return lax.ppermute(value, axis, [(i, i ^ bit) for i in range(size)])


def gelu_parts(upper):
    cdf = 0.5 * (1.0 + lax.erf(upper * ROOT_HALF))
    slope = cdf + upper * jnp.exp(-0.5 * upper * upper) * INV_ROOT_TWO_PI
    return upper * cdf, slope


def after(value, *marks):
    return lax.optimization_barrier((value, *marks))[0]


def rows_sum(part, arrived):
    half = part.shape[0] // 2
    part, arrived = part.astype(F32), arrived.astype(F32)
    return jnp.concatenate([part[:half] + arrived[half:], part[half:] + arrived[:half]], axis=0)


def normal(rows_in):
    centred = rows_in - jnp.mean(rows_in, axis=-1, keepdims=True)
    inverse = lax.rsqrt(jnp.mean(centred * centred, axis=-1, keepdims=True) + NORM_EPS)
    return centred * inverse, inverse


def normal_back(grad, normed, inverse, gain):
    scaled = grad * gain
    inner = jnp.mean(scaled * normed, axis=-1, keepdims=True)
    return inverse * (scaled - jnp.mean(scaled, axis=-1, keepdims=True) - normed * inner)


def call(kernel, outs, args, name, flops, limit=24, scalars=None):
    specs = [pl.BlockSpec(a.shape, lambda n=a.ndim: (0,) * n) for a in args]
    operands = list(args)
    if scalars is not None:
        specs = [pl.BlockSpec(memory_space=pltpu.SMEM)] + specs
        operands = [scalars] + operands
    shapes = [jax.ShapeDtypeStruct(shape, kind) for shape, kind in outs]
    moved = sum(a.size * a.dtype.itemsize for a in list(args) + shapes)
    return pl.pallas_call(
        kernel,
        in_specs=specs,
        out_shape=shapes,
        cost_estimate=cost(flops, moved),
        compiler_params=params(limit),
        name=name,
    )(*operands)


def project(low, wq_ref, wkv_ref, bias_ref, q_ref, kv_ref):
    width = wq_ref.shape[1]
    q_ref[...] = (dot(low, wq_ref[...], 1, 0) + bias_ref[:, :width]).astype(LOW)
    kv_ref[...] = (dot(low, wkv_ref[...], 1, 0) + bias_ref[:, width:]).astype(LOW)


def project_kernel(x_ref, wq_ref, wkv_ref, bias_ref, q_ref, kv_ref):
    project(x_ref[...], wq_ref, wkv_ref, bias_ref, q_ref, kv_ref)


def first_norm(rows, vec_ref):
    return normal(rows)[0] * vec_ref[0:1, :] + vec_ref[2:3, :]


def second_norm(rows, vec_ref):
    return normal(rows)[0] * vec_ref[1:2, :] + vec_ref[3:4, :]


def norm_project_kernel(
    sent_ref, arrived_ref, rows_ref, vec_ref, wq_ref, wkv_ref, bias_ref, out_ref, low_ref, q_ref, kv_ref
):
    rows = rows_sum(sent_ref[...], arrived_ref[...]) + vec_ref[5:6, :] + first_norm(rows_ref[...], vec_ref)
    out_ref[...] = rows
    low = second_norm(rows, vec_ref).astype(LOW)
    low_ref[...] = low
    project(low, wq_ref, wkv_ref, bias_ref, q_ref, kv_ref)


def pick(flag, first, second):
    return jnp.where(flag, first.astype(F32), second.astype(F32)).astype(LOW)


def attend_kernel(flags_ref, q_ref, k0_ref, k1_ref, k2_ref, k3_ref, place_ref, bound_ref, wo_ref,
                  keep_ref, give_ref, logsum_ref, sent_ref):
    rows, width = q_ref.shape
    pieces = (k0_ref, k1_ref, k2_ref, k3_ref)
    lanes = lax.broadcasted_iota(jnp.int32, (1, 128), 1)
    low, high = bound_ref[:, :1], bound_ref[:, 1:2]
    masks = []
    for index, ref in enumerate(pieces):
        place = place_ref[:, index * ref.shape[0] : (index + 1) * ref.shape[0]]
        masks.append(jnp.where((place >= low) & (place < high), 0.0, MASKED))
    logsums = jnp.zeros((rows, 128), F32)
    tiles = []
    for tile in range(width // 128):
        cols = slice(tile * 128, tile * 128 + 128)
        other = slice(width + tile * 128, width + tile * 128 + 128)
        query = q_ref[:, cols]
        out = None
        for side in range(2):
            here = (lanes >= side * HD) & (lanes < side * HD + HD)
            lone = jnp.where(here, query.astype(F32) * HD ** (-0.5), 0.0).astype(LOW)
            scores = [dot(lone, ref[:, cols], 1, 1) + mask for ref, mask in zip(pieces, masks)]
            highest = jnp.max(scores[0], axis=-1, keepdims=True)
            for score in scores[1:]:
                highest = jnp.maximum(highest, jnp.max(score, axis=-1, keepdims=True))
            powers = [jnp.exp(score - highest) for score in scores]
            total = sum(jnp.sum(power, axis=-1, keepdims=True) for power in powers)
            inverse = 1.0 / total
            head = sum(dot((power * inverse).astype(LOW), ref[:, other], 1, 0) for power, ref in zip(powers, pieces))
            head = jnp.where(here, head, 0.0)
            out = head if out is None else out + head
            logsums = jnp.where(lanes == 2 * tile + side, highest + jnp.log(total), logsums)
        tiles.append(out.astype(LOW))
    logsum_ref[...] = logsums
    mixed = jnp.concatenate(tiles, axis=1)
    half = width // 2
    keep_ref[...] = pick(flags_ref[0] == 0, mixed[:, :half], mixed[:, half:])
    give_ref[...] = pick(flags_ref[0] == 0, mixed[:, half:], mixed[:, :half])
    sent_ref[...] = dot(mixed, wo_ref[...], 1, 1).astype(LOW)


def attend_back_kernel(first, *refs):
    q_ref, k0_ref, k1_ref, k2_ref, k3_ref, grad_ref, logsum_ref, place_ref, bound_ref = refs[:9]
    held_refs = () if first else refs[9:13]
    dq_ref, *sums_refs = refs[9 + len(held_refs) :]
    rows, width = q_ref.shape
    pieces = (k0_ref, k1_ref, k2_ref, k3_ref)
    lanes = lax.broadcasted_iota(jnp.int32, (1, 128), 1)
    low, high = bound_ref[:, :1], bound_ref[:, 1:2]
    scale = HD ** (-0.5)
    masks = []
    for index, ref in enumerate(pieces):
        place = place_ref[:, index * ref.shape[0] : (index + 1) * ref.shape[0]]
        masks.append(jnp.where((place >= low) & (place < high), 0.0, MASKED))
    for tile in range(width // 128):
        cols = slice(tile * 128, tile * 128 + 128)
        other = slice(width + tile * 128, width + tile * 128 + 128)
        query, grad = q_ref[:, cols].astype(F32), grad_ref[:, cols].astype(F32)
        dq = None
        dk, dv = [None] * 4, [None] * 4
        for side in range(2):
            here = (lanes >= side * HD) & (lanes < side * HD + HD)
            lone = jnp.where(here, query * scale, 0.0).astype(LOW)
            lone_grad = jnp.where(here, grad, 0.0).astype(LOW)
            logsum = jnp.sum(jnp.where(lanes == 2 * tile + side, logsum_ref[...], 0.0), axis=-1, keepdims=True)
            probs, prob_grads = [], []
            inner = None
            for ref, mask in zip(pieces, masks):
                prob = jnp.exp(dot(lone, ref[:, cols], 1, 1) + mask - logsum)
                prob_grad = dot(lone_grad, ref[:, other], 1, 1)
                probs.append(prob)
                prob_grads.append(prob_grad)
                piece = jnp.sum(prob * prob_grad, axis=-1, keepdims=True)
                inner = piece if inner is None else inner + piece
            for index, ref in enumerate(pieces):
                score = (probs[index] * (prob_grads[index] - inner)).astype(LOW)
                back = dot(score, ref[:, cols], 1, 0)
                back = jnp.where(here, back * scale, 0.0)
                dq = back if dq is None else dq + back
                key = dot(score, lone, 0, 0)
                value = dot(probs[index].astype(LOW), lone_grad, 0, 0)
                dk[index] = key if dk[index] is None else dk[index] + key
                dv[index] = value if dv[index] is None else dv[index] + value
        dq_ref[:, cols] = dq.astype(LOW)
        for index in range(4):
            key, value = dk[index], dv[index]
            if held_refs:
                key = key + held_refs[index][:, cols]
                value = value + held_refs[index][:, other]
            sums_refs[index][:, cols] = key.astype(sums_refs[index].dtype)
            sums_refs[index][:, other] = value.astype(sums_refs[index].dtype)


def feed_kernel(is_first, sent_ref, arrived_ref, resid_ref, vec_ref, before_ref, feed0_ref, feed1_ref, bias_ref,
                rows_ref, give_ref, act_ref, slope_ref, out_ref):
    resid = resid_ref[...].astype(F32) if is_first else second_norm(resid_ref[...], before_ref)
    rows = rows_sum(sent_ref[...], arrived_ref[...]) + vec_ref[4:5, :] + resid
    rows_ref[...] = rows
    low = first_norm(rows, vec_ref).astype(LOW)
    cols = low.shape[1]
    units = feed0_ref.shape[1] // 2
    give_ref[:, :cols] = low
    act, slope = gelu_parts(dot(low, feed0_ref[:, :units], 1, 0) + bias_ref[0:1, :])
    act = act.astype(LOW)
    act_ref[...] = act
    slope_ref[:, :units] = slope.astype(LOW)
    part = dot(act, feed0_ref[:, units:], 1, 1)
    act, slope = gelu_parts(dot(low, feed1_ref[:, :units], 1, 0) + bias_ref[1:2, :])
    act = act.astype(LOW)
    give_ref[:, cols:] = act
    slope_ref[:, units:] = slope.astype(LOW)
    out_ref[...] = (part + dot(act, feed1_ref[:, units:], 1, 1)).astype(LOW)


def put_sums(sums_ref, lists):
    half = lists[0].shape[0] // 2
    for index, rows in enumerate(lists):
        sums_ref[index : index + 1, :] = jnp.sum(rows[:half], axis=0, keepdims=True)
    sums_ref[len(lists) :, :] = jnp.zeros((8 - len(lists), lists[0].shape[1]), F32)


def back_feed(grad, normed, inverse, gain, slope_ref, feed0_ref, feed1_ref, rest_ref, give_ref, keep_ref, out_ref, sums_ref):
    back = normal_back(grad, normed, inverse, gain)
    rest_ref[...] = back
    put_sums(sums_ref, [grad * normed, grad, back])
    low = back.astype(LOW)
    cols = low.shape[1]
    units = feed0_ref.shape[1] // 2
    give_ref[:, :cols] = low
    upper = (dot(low, feed0_ref[:, units:], 1, 0) * slope_ref[:, :units].astype(F32)).astype(LOW)
    keep_ref[...] = upper
    part = dot(upper, feed0_ref[:, :units], 1, 1)
    upper = (dot(low, feed1_ref[:, units:], 1, 0) * slope_ref[:, units:].astype(F32)).astype(LOW)
    give_ref[:, cols:] = upper
    out_ref[...] = (part + dot(upper, feed1_ref[:, :units], 1, 1)).astype(LOW)


def top_kernel(flags_ref, sent_ref, arrived_ref, rows_ref, grad_ref, before_rows_ref, before_ref, vec_ref, slope_ref,
               feed0_ref, feed1_ref, y_ref, rest_ref, give_ref, keep_ref, out_ref, sums_ref):
    rows = rows_sum(sent_ref[...], arrived_ref[...]) + vec_ref[5:6, :] + first_norm(rows_ref[...], vec_ref)
    normed, inverse = normal(rows)
    half = normed.shape[0] // 2
    y = normed[:half] * vec_ref[1:2, :] + vec_ref[3:4, :]
    on = flags_ref[1] > 0
    y_ref[...] = jnp.where(on, y, second_norm(before_rows_ref[:half, :], before_ref))
    grad = jnp.where(on, grad_ref[...].astype(F32), 0.0)
    back_feed(grad, normed, inverse, vec_ref[1:2, :], slope_ref, feed0_ref, feed1_ref,
              rest_ref, give_ref, keep_ref, out_ref, sums_ref)


def under_kernel(flags_ref, sent_ref, arrived_ref, resid_ref, grad_ref, rows_ref, vec_ref, slope_ref,
                 feed0_ref, feed1_ref, rest_ref, give_ref, keep_ref, out_ref, sums_ref):
    grad = rows_sum(sent_ref[...], arrived_ref[...]) + resid_ref[...]
    grad = jnp.where(flags_ref[1] > 0, grad, grad_ref[...].astype(F32))
    normed, inverse = normal(rows_ref[...])
    back_feed(grad, normed, inverse, vec_ref[1:2, :], slope_ref, feed0_ref, feed1_ref,
              rest_ref, give_ref, keep_ref, out_ref, sums_ref)


def back_norm_kernel(sent_ref, arrived_ref, resid_ref, rows_ref, vec_ref, wo_ref, rest_ref, low_ref, grad_ref, sums_ref):
    grad = rows_sum(sent_ref[...], arrived_ref[...]) + resid_ref[...]
    normed, inverse = normal(rows_ref[...])
    back = normal_back(grad, normed, inverse, vec_ref[0:1, :])
    rest_ref[...] = back
    put_sums(sums_ref, [grad * normed, grad, back])
    low = back.astype(LOW)
    low_ref[...] = low
    grad_ref[...] = dot(low, wo_ref[...], 1, 0).astype(LOW)


def back_project_kernel(flags_ref, dq_ref, own_ref, arrived_ref, wq_ref, wkv_ref, keep_ref, give_ref, sent_ref):
    dq = dq_ref[...]
    dkv = (own_ref[...] + arrived_ref[...].astype(F32)).astype(LOW)
    sent_ref[...] = (dot(dq, wq_ref[...], 1, 1) + dot(dkv, wkv_ref[...], 1, 1)).astype(LOW)
    half = dq.shape[1] // 2
    groups = (dq, dkv[:, : 2 * half], dkv[:, 2 * half :])
    front = flags_ref[0] == 0
    keep_ref[...] = jnp.concatenate([pick(front, g[:, :half], g[:, half:]) for g in groups], axis=1)
    give_ref[...] = jnp.concatenate([pick(front, g[:, half:], g[:, :half]) for g in groups], axis=1)

def sum_over(value, axis):
    bit = 1
    while bit < lax.axis_size(axis):
        value = value + swap(value, axis, bit)
        bit *= 2
    return value


def split(value):
    high = value.astype(LOW)
    return high, (value - high.astype(F32)).astype(LOW)


def split_dot(small, large, small_dim, large_dim):
    high, rest = split(large)
    lead, tail = split(small)
    rows = small.shape[0]
    both = dot(jnp.concatenate([lead, tail], axis=0), high, small_dim, large_dim)
    return both[:rows] + both[rows:] + dot(lead, rest, small_dim, large_dim)


def dot_chunks(lefts, rights):
    total = None
    for left, right in zip(lefts, rights):
        part = dot(left[...], right[...], 0, 0)
        total = part if total is None else total + part
    return total


def rows_total_kernel(chunks, *refs):
    lefts, rights = refs[:chunks], refs[chunks : 2 * chunks]
    error_ref, start_ref, total_ref, first_ref, bias_ref = refs[2 * chunks :]
    total = dot_chunks(lefts, rights) + error_ref[...]
    total_ref[...] = total
    first_ref[...] = split_dot(start_ref[...], total, 1, 1)

    @pl.when(pl.program_id(0) == 0)
    def _():
        bias = sum(jnp.sum(ref[...].astype(F32), axis=0, keepdims=True) for ref in rights)
        bias_ref[...] = jnp.concatenate([bias, jnp.zeros((7, bias.shape[1]), F32)], axis=0)


def params(limit, **more):
    return pltpu.CompilerParams(vmem_limit_bytes=limit << 20, **more)


def cost(flops, moved):
    return pl.CostEstimate(flops=int(flops), bytes_accessed=int(moved), transcendentals=0)


def rows_total(lefts, rights, errors, starts, layer):
    rows, cols = errors.shape[-2:]
    tokens = lefts[0][0].shape[0]
    rank = starts.shape[1]
    step = 256
    chunks = len(lefts)
    return pl.pallas_call(
        lambda *refs: rows_total_kernel(chunks, *refs),
        grid=(rows // step,),
        in_specs=[pl.BlockSpec((tokens, step), lambda i, at=at: (0, i + at * (rows // step))) for _, at in lefts]
        + [pl.BlockSpec((tokens, cols), lambda i, at=at: (0, at)) for _, at in rights]
        + [
            pl.BlockSpec((None, None, step, cols), lambda i: (0, layer, i, 0)),
            pl.BlockSpec((None, rank, cols), lambda i: (layer, 0, 0)),
        ],
        out_specs=[
            pl.BlockSpec((step, cols), lambda i: (i, 0)),
            pl.BlockSpec((rank, step), lambda i: (0, i)),
            pl.BlockSpec((rank, cols), lambda i: (0, 0)),
        ],
        out_shape=[
            jax.ShapeDtypeStruct((rows, cols), F32),
            jax.ShapeDtypeStruct((rank, rows), F32),
            jax.ShapeDtypeStruct((rank, cols), F32),
        ],
        cost_estimate=cost(2 * chunks * tokens * rows * cols, 8 * rows * cols + 4 * chunks * tokens * rows),
        compiler_params=params(24),
        name="rows_total",
    )(*[array for array, _ in lefts], *[array for array, _ in rights], errors, starts)


def mixed_total_kernel(chunks, *refs):
    proj_refs, whole_refs = refs[:chunks], refs[chunks : 2 * chunks]
    attended_refs, piece_refs = refs[2 * chunks : 3 * chunks], refs[3 * chunks : 4 * chunks]
    e_proj_ref, e_back_ref, s_proj_ref, s_back_ref, total_ref, first_ref = refs[4 * chunks :]
    width = e_back_ref.shape[0]
    grads = dot_chunks(proj_refs, whole_refs)
    for member in range(3):
        rows = slice(member * width, (member + 1) * width)
        total = grads[rows] + e_proj_ref[member]
        total_ref[rows, :] = total
        first_ref[8 * member : 8 * member + 8, :] = split_dot(s_proj_ref[member], total, 1, 0)
    total = dot_chunks(attended_refs, piece_refs) + e_back_ref[...]
    total_ref[3 * width :, :] = total
    first_ref[24:, :] = jnp.zeros((8, total.shape[1]), F32)
    first_ref[24:, :width] = split_dot(s_back_ref[...], total, 1, 1)
    sums = sum(jnp.sum(ref[...].astype(F32), axis=0, keepdims=True) for ref in proj_refs)
    first_ref[24:25, 256 : 256 + width] = sums[:, :width]
    first_ref[24:25, 512 : 512 + width] = sums[:, 2 * width :]


def mixed_total(proj_low, whole_in, attended, piece, e_proj, e_back, s_proj, s_back, layer):
    tokens, width = attended[0].shape
    cols = whole_in[0].shape[1]
    rank = s_back.shape[1]
    chunks = len(attended)
    return pl.pallas_call(
        lambda *refs: mixed_total_kernel(chunks, *refs),
        grid=(1,),
        in_specs=[pl.BlockSpec((tokens, 3 * width), lambda i: (0, 0))] * chunks
        + [pl.BlockSpec((tokens, cols), lambda i: (0, 0))] * chunks
        + [pl.BlockSpec((tokens, width), lambda i: (0, 0))] * chunks
        + [pl.BlockSpec((tokens, cols), lambda i: (0, 0))] * chunks
        + [
            pl.BlockSpec((None, None, 3, width, cols), lambda i: (0, layer, 0, 0, 0)),
            pl.BlockSpec((None, None, width, cols), lambda i: (0, layer, 0, 0)),
            pl.BlockSpec((None, 3, rank, width), lambda i: (layer, 0, 0, 0)),
            pl.BlockSpec((None, rank, cols), lambda i: (layer, 0, 0)),
        ],
        out_specs=[
            pl.BlockSpec((4 * width, cols), lambda i: (0, 0)),
            pl.BlockSpec((4 * rank, cols), lambda i: (0, 0)),
        ],
        out_shape=[jax.ShapeDtypeStruct((4 * width, cols), F32), jax.ShapeDtypeStruct((4 * rank, cols), F32)],
        cost_estimate=cost(2 * chunks * tokens * 4 * width * cols, 32 * width * cols + 6 * chunks * tokens * cols),
        compiler_params=params(32),
        name="mixed_total",
    )(*proj_low, *whole_in, *attended, *piece, e_proj, e_back, s_proj, s_back)


def ortho_rows(factor):
    rank = factor.shape[0]
    index = lax.broadcasted_iota(jnp.int32, (rank, 1), 0)
    for row in range(rank):
        vector = factor[row : row + 1, :]
        inner = jnp.sum(factor * vector, axis=1, keepdims=True)
        scale = lax.rsqrt(inner[row : row + 1] + ORTHO_EPS)
        vector = vector * scale
        factor = jnp.where(
            index < row, factor, jnp.where(index == row, vector, factor - vector * (inner * scale))
        )
    return factor


def feed_second_kernel(sums_ref, up_ref, down_ref, base_ref, second_ref):
    for member, total_ref in enumerate((up_ref, down_ref)):
        rows = slice(8 * member, 8 * member + 8)
        base = ortho_rows(sums_ref[rows, :])
        base_ref[rows, :] = base
        second_ref[rows, :] = split_dot(base, total_ref[...], 1, 0)


def feed_second(sums, m_up, m_down):
    cols = m_up.shape[1]
    return pl.pallas_call(
        feed_second_kernel,
        out_shape=[jax.ShapeDtypeStruct((16, cols), F32)] * 2,
        cost_estimate=cost(96 * m_up.size, 8 * m_up.size),
        compiler_params=params(24),
        name="feed_second",
    )(sums, m_up, m_down)


def mixed_second_kernel(width, sums_ref, total_ref, base_ref, second_ref):
    second_ref[...] = jnp.zeros(second_ref.shape, F32)
    for member in range(3):
        rows = slice(8 * member, 8 * member + 8)
        base = ortho_rows(sums_ref[rows, :])
        base_ref[rows, :] = base
        second_ref[:8, 256 * member : 256 * member + width] = split_dot(
            base, total_ref[member * width : (member + 1) * width, :], 1, 1
        )
    base = ortho_rows(sums_ref[24:32, :width])
    base_ref[24:32, :width] = base
    second_ref[8:, :] = split_dot(base, total_ref[3 * width :, :], 1, 0)


def mixed_second(sums, m_mixed, width):
    cols = m_mixed.shape[1]
    return pl.pallas_call(
        lambda *refs: mixed_second_kernel(width, *refs),
        out_shape=[jax.ShapeDtypeStruct((32, cols), F32), jax.ShapeDtypeStruct((16, cols), F32)],
        cost_estimate=cost(48 * m_mixed.size, 4 * m_mixed.size),
        compiler_params=params(16),
        name="mixed_second",
    )(sums, m_mixed)


def low_rank(base, second):
    b_high, b_rest = split(base)
    s_high, s_rest = split(second)
    left = jnp.concatenate([b_high, b_rest, b_high], axis=0)
    right = jnp.concatenate([s_high, s_high, s_rest], axis=0)
    return dot(left, right, 0, 0)


def feed_error_kernel(layer, replicas, base_ref, second_ref, up_ref, down_ref, *refs):
    up_out, down_out = refs[-2:]
    seconds = second_ref[...] * (1.0 / replicas)
    up_out[...] = up_ref[...] - low_rank(base_ref[:8, :], seconds[:8])
    down_out[...] = down_ref[...] - low_rank(base_ref[8:16, :], seconds[8:16])


def feed_error(base, second, m_up, m_down, layer, replicas, held):
    rows, cols = m_up.shape
    rank2 = base.shape[0]
    step = 256
    shape = jax.ShapeDtypeStruct((1, 2, rows, cols), F32)
    out_spec = pl.BlockSpec((None, None, step, cols), lambda i: (0, layer, i, 0))
    extra = {} if held is None else {"input_output_aliases": {4: 0, 5: 1}}
    return pl.pallas_call(
        lambda *refs: feed_error_kernel(layer, replicas, *refs),
        grid=(rows // step,),
        in_specs=[
            pl.BlockSpec((rank2, step), lambda i: (0, i)),
            pl.BlockSpec((rank2, cols), lambda i: (0, 0)),
            pl.BlockSpec((step, cols), lambda i: (i, 0)),
            pl.BlockSpec((step, cols), lambda i: (i, 0)),
        ] + ([] if held is None else [pl.BlockSpec(memory_space=pl.ANY)] * 2),
        out_specs=[out_spec, out_spec],
        out_shape=[shape, shape],
        cost_estimate=cost(100 * m_up.size, 16 * m_up.size),
        compiler_params=params(16),
        name="feed_error",
        **extra,
    )(base, second, m_up, m_down, *(() if held is None else held))


def mixed_error_kernel(replicas, base_ref, second_ref, total_ref, *refs):
    proj_out, back_out = refs[-2:]
    width = back_out.shape[0]
    seconds = second_ref[...] * (1.0 / replicas)
    for member in range(3):
        approx = low_rank(seconds[:8, 256 * member : 256 * member + width], base_ref[8 * member : 8 * member + 8, :])
        proj_out[member] = total_ref[member * width : (member + 1) * width, :] - approx
    back_out[...] = total_ref[3 * width :, :] - low_rank(base_ref[24:32, :width], seconds[8:])


def mixed_error(base, second, m_mixed, layer, replicas, held):
    rows, cols = m_mixed.shape
    width = rows // 4
    extra = {} if held is None else {"input_output_aliases": {3: 0, 4: 1}}
    return pl.pallas_call(
        lambda *refs: mixed_error_kernel(replicas, *refs),
        grid=(1,),
        in_specs=[
            pl.BlockSpec(base.shape, lambda i: (0, 0)),
            pl.BlockSpec(second.shape, lambda i: (0, 0)),
            pl.BlockSpec((rows, cols), lambda i: (0, 0)),
        ] + ([] if held is None else [pl.BlockSpec(memory_space=pl.ANY)] * 2),
        out_specs=[
            pl.BlockSpec((None, None, 3, width, cols), lambda i: (0, layer, 0, 0, 0)),
            pl.BlockSpec((None, None, width, cols), lambda i: (0, layer, 0, 0)),
        ],
        out_shape=[
            jax.ShapeDtypeStruct((1, 2, 3, width, cols), F32), jax.ShapeDtypeStruct((1, 2, width, cols), F32)
        ],
        cost_estimate=cost(50 * m_mixed.size, 8 * m_mixed.size),
        compiler_params=params(24),
        name="mixed_error",
        **extra,
    )(base, second, m_mixed, *(() if held is None else held))


def flip(value):
    return jnp.swapaxes(value, -1, -2)


def per_device(
    x_in, out_grad, doc_lengths, keep_layer, w_qkv, w_o, w_in, w_out, b_qv, b_in, ln_gain, shifts,
    m_qkv, m_o, m_in, m_out, m_qv, m_bin, m_gain, m_shift, e_qkv, e_o, e_in, e_out, q_qkv, q_o, q_in, q_out,
):
    own_rows, cols = x_in.shape
    replicas = lax.axis_size("dp")
    index = lax.axis_index("dp")
    place = lax.axis_index("mp")
    width = w_o.shape[1]
    front = lax.rem(place, 2) == 0
    flags = jnp.stack([lax.rem(place, 2), keep_layer[0]]).astype(jnp.int32)
    chunks = 2
    step = own_rows // chunks
    size = 2 * step
    pair = range(chunks)

    def core(value):
        return swap(value, "mp", 1)

    def chip(value):
        return swap(value, "mp", 2)

    def gather(piece):
        return lax.all_gather(piece, "dp", axis=0, tiled=True)

    def join(own, other, axis):
        return jnp.where(
            front, jnp.concatenate([own, other], axis=axis), jnp.concatenate([other, own], axis=axis)
        )

    def mixed_piece(layer):
        return jnp.concatenate(
            [w_qkv[layer, 0], w_qkv[layer, 1], w_qkv[layer, 2], flip(w_o[layer])], axis=1
        ).astype(LOW)

    def feed_piece(layer):
        return jnp.concatenate([w_in[layer], flip(w_out[layer])], axis=1).astype(LOW)

    def spread(piece):
        if replicas != 8:
            return gather(piece)
        order = [0]
        for bit in (4, 2, 1):
            piece = jnp.concatenate([piece, swap(piece, "dp", bit)], axis=0)
            order = order + [v ^ bit for v in order]
        spots = jnp.asarray([order.index(v) for v in range(replicas)], jnp.int32)
        rows = piece.shape[0] // replicas
        parts = [lax.dynamic_slice_in_dim(piece, spots[index ^ k] * rows, rows, 0) for k in range(replicas)]
        return jnp.concatenate(parts, axis=0)

    def by_chunk(rows, arrived):
        return [
            jnp.concatenate([rows[j * step : (j + 1) * step], arrived[j * step : (j + 1) * step]], axis=0) for j in pair
        ]

    mixed_whole = [spread(mixed_piece(0)), None]
    set_in = by_chunk(x_in, chip(x_in))
    feed_whole = [gather(feed_piece(0)), None]
    whole_other = [core(rows) for rows in set_in]
    feed_late, *whole_other = lax.optimization_barrier((feed_piece(1), *whole_other))
    feed_whole[1] = gather(feed_late)
    set_grad = by_chunk(out_grad, chip(after(out_grad, *set_in)))
    mixed_whole[1] = spread(after(mixed_piece(1), mixed_whole[0]))
    small = jnp.concatenate([b_qv.reshape(-1), b_in.reshape(-1)]).reshape(-1, 128)
    small = core(small).reshape(-1)
    other_qv = small[: b_qv.size].reshape(b_qv.shape)
    other_in = small[b_qv.size :].reshape(b_in.shape)

    ends = jnp.sum(
        jnp.where(
            jnp.arange(doc_lengths.shape[1])[:, None] <= jnp.arange(doc_lengths.shape[1])[None, :],
            doc_lengths[0][:, None], 0,
        ),
        axis=0,
    )

    def places_of(device, j):
        steps = jnp.arange(step, dtype=jnp.int32) + j * step
        return jnp.concatenate([device * own_rows + steps, (device ^ 2) * own_rows + steps])

    mine = [places_of(place, j) for j in pair]
    all_places = jnp.concatenate(mine + [places_of(place ^ 1, j) for j in pair])[None, :]

    def bounds_of(places):
        passed = places[:, None] >= ends[None, :]
        low = jnp.max(jnp.where(passed, ends[None, :], 0), axis=1)
        high = jnp.min(jnp.where(passed, 1 << 30, ends[None, :]), axis=1)
        return jnp.stack([low, high], axis=1)

    bounds = [bounds_of(places) for places in mine]

    vecs, feeds, proj_bias, feed_bias = [], [], [], []
    for layer in range(2):
        gain, shift = ln_gain[layer], shifts[layer]
        vecs.append(
            jnp.concatenate(
                [gain, shift[1:2], shift[3:4], shift[0:1], shift[2:3], jnp.zeros((2, cols), F32)], axis=0
            )
        )
        proj_bias.append(
            jnp.concatenate(
                [
                    join(b_qv[layer, 0], other_qv[layer, 0], 0),
                    jnp.zeros((2 * width,), F32),
                    join(b_qv[layer, 1], other_qv[layer, 1], 0),
                ]
            )[None]
        )
        feed_bias.append(jnp.stack([b_in[layer], other_in[layer]]))

    full = [(size, cols), F32]
    full_low = [(size, cols), LOW]
    thin = [(size, 128), F32]
    half_low = [(size, 2 * width), LOW]
    one_low = [(size, width), LOW]
    kv_low = [(size, 4 * width), LOW]
    units = cols

    def mixed_weights(own):
        other = core(own)
        keys = join(own[:, width : 2 * width], other[:, width : 2 * width], 1)
        values = join(own[:, 2 * width : 3 * width], other[:, 2 * width : 3 * width], 1)
        return (
            join(own[:, :width], other[:, :width], 1), jnp.concatenate([keys, values], axis=1),
            join(own[:, 3 * width :], other[:, 3 * width :], 1),
        )

    def attention(layer, q, kv):
        pieces = kv + [core(part) for part in kv]
        return pieces, [
            call(
                attend_kernel, [one_low, one_low, thin, full_low],
                [q[j], *pieces, all_places, bounds[j], wo[layer]], "attend",
                2 * size * (4 * size) * 4 * width + 2 * size * 2 * width * cols, 32, flags,
            )
            for j in pair
        ]

    def feed_all(layer, outs, resid):
        return [
            call(
                lambda *refs: feed_kernel(layer == 0, *refs),
                [full, [(size, cols + units), LOW], [(size, units), LOW], [(size, 2 * units), LOW], full_low],
                [outs[j][3], chip(outs[j][3]), resid[j], vecs[layer], vecs[0], *feeds[layer], feed_bias[layer]],
                "feed", 8 * size * cols * units, 32,
            )
            for j in pair
        ]

    wq, wkv, wo = ([part] for part in mixed_weights(mixed_whole[0]))
    first = [
        call(
            project_kernel, [half_low, kv_low], [set_in[j], wq[0], wkv[0], proj_bias[0]],
            "project", 2 * size * cols * 6 * width,
        )
        for j in pair
    ]
    q_one = [out[0] for out in first]
    pieces_one, mixed_out_one = attention(0, q_one, [out[1] for out in first])
    vecs[0] = after(vecs[0], *set_grad)
    whole = after(feed_whole[0], mixed_out_one[0][3])
    feeds.append((whole, core(whole)))
    feed_out_one = feed_all(0, mixed_out_one, set_in)
    for held, part in zip((wq, wkv, wo), mixed_weights(after(mixed_whole[1], feed_out_one[0][4]))):
        held.append(part)
    second = [
        call(
            norm_project_kernel, [full, full_low, half_low, kv_low],
            [feed_out_one[j][4], chip(feed_out_one[j][4]), feed_out_one[j][0], vecs[0], wq[1], wkv[1], proj_bias[1]],
            "norm_project", 2 * size * cols * 6 * width,
        )
        for j in pair
    ]
    q_two = [out[2] for out in second]
    pieces_two, mixed_out_two = attention(1, q_two, [out[3] for out in second])
    whole = after(feed_whole[1], mixed_out_two[0][3])
    feeds.append((whole, core(whole)))
    feed_out_two = feed_all(1, mixed_out_two, [out[0] for out in second])

    wide_outs = [full, [(size, cols + units), LOW], [(size, units), LOW], full_low, [(8, cols), F32]]
    top = [
        call(
            top_kernel, [[(step, cols), F32]] + wide_outs,
            [
                feed_out_two[j][4], chip(feed_out_two[j][4]), feed_out_two[j][0], set_grad[j], second[j][0], vecs[0],
                vecs[1], feed_out_two[j][3], *feeds[1],
            ],
            "top", 8 * size * cols * units, 32, flags,
        )
        for j in pair
    ]
    output = jnp.concatenate([out[0] for out in top], axis=0)

    def back_norm(layer, outs, feed_out):
        return [
            call(
                back_norm_kernel, [full, full_low, half_low, [(8, cols), F32]],
                [outs[j][3], chip(outs[j][3]), outs[j][0], feed_out[j][0], vecs[layer], wo[layer]],
                "back_norm", 4 * size * cols * width,
            )
            for j in pair
        ]

    def attention_back(layer, q, pieces, grads, outs):
        held, dqs = [], []
        for j in pair:
            kinds = [full] * 4 if j + 1 < chunks else [full, full, full_low, full_low]
            dq, *held = call(
                lambda *refs, j=j: attend_back_kernel(j == 0, *refs), [half_low] + kinds,
                [q[j], *pieces, grads[j], outs[j][2], all_places, bounds[j], *held], "attend_back",
                5 * size * (4 * size) * 4 * width, 40,
            )
            dqs.append(dq)
        return [
            call(
                back_project_kernel, [[(size, 3 * width), LOW], [(size, 3 * width), LOW], full_low],
                [dqs[j], held[j], core(held[2 + j]), wq[layer], wkv[layer]], "back_project",
                2 * size * cols * 6 * width, 32, flags,
            )
            for j in pair
        ]

    top_tail = [out[1:] for out in top]
    norm_two = back_norm(1, top_tail, feed_out_two)
    back_two = attention_back(1, q_two, pieces_two, [out[2] for out in norm_two], mixed_out_two)
    under = [
        call(
            under_kernel, wide_outs,
            [
                back_two[j][2], chip(back_two[j][2]), norm_two[j][0], set_grad[j], second[j][0],
                vecs[0], feed_out_one[j][3], *feeds[0],
            ],
            "under", 8 * size * cols * units, 32, flags,
        )
        for j in pair
    ]
    norm_one = back_norm(0, under, feed_out_one)
    back_one = attention_back(0, q_one, pieces_one, [out[2] for out in norm_one], mixed_out_one)
    input_gradient = jnp.concatenate(
        [
            back_one[j][2][:step].astype(F32) + chip(back_one[j][2][step:]).astype(F32) + norm_one[j][0][:step]
            for j in pair
        ],
        axis=0,
    )

    e_proj, s_proj = flip(e_qkv), flip(q_qkv)
    s_back, s_up, s_down = flip(q_o), flip(q_in), flip(q_out)

    def feed_first(layer, feed_out, tails):
        give_up = [out[1] for out in feed_out]
        give_down = [out[1] for out in tails]
        their_up = [core(rows) for rows in give_up]
        their_down = [core(rows) for rows in give_down]
        m_up, f_up, bias = rows_total(
            [(rows, 0) for rows in give_up + their_up],
            [(out[2], 0) for out in tails] + [(rows, 1) for rows in their_down], e_in, s_up, layer,
        )
        m_down, f_down, _ = rows_total(
            [(out[2], 0) for out in feed_out] + [(rows, 1) for rows in their_up],
            [(rows, 0) for rows in give_down + their_down], e_out, s_down, layer,
        )
        return (m_up, m_down), jnp.concatenate([f_up, f_down, bias], axis=0)

    def mixed_first(layer, low, back, mixed, norm):
        return mixed_total(
            [out[0] for out in back] + [core(out[1]) for out in back],
            low,
            [out[0] for out in mixed] + [core(out[1]) for out in mixed],
            [out[1] for out in norm] + [core(out[1]) for out in norm],
            e_proj, e_o, s_proj, s_back, layer,
        )

    def total_over(value, axes):
        for axis in axes:
            value = sum_over(value, axis)
        return value

    def norm_sums(tails, norm):
        upper = sum(out[4] for out in tails)
        lower = sum(out[3] for out in norm)
        return jnp.stack([lower[0], upper[0], lower[2], lower[1], upper[2], upper[1]])

    s_up, s_down = after(s_up, top[1][4]), after(s_down, back_two[1][2])
    s_proj = after(s_proj, back_two[1][2])
    feed_two, send_two = feed_first(1, feed_out_two, top_tail)
    low_two = [out[1] for out in second]
    mixed_two, send_mixed_two = mixed_first(1, low_two + [core(rows) for rows in low_two], back_two, mixed_out_two, norm_two)
    sums_two = total_over(jnp.concatenate([send_two, send_mixed_two], axis=0), ("dp",))
    base_feed_two, second_feed_two = feed_second(sums_two[:24], *feed_two)
    base_mixed_two, second_mixed_two = mixed_second(sums_two[24:], mixed_two, width)
    seconds_two = total_over(jnp.concatenate([second_feed_two, second_mixed_two], axis=0), ("dp",))
    held_feed = feed_error(base_feed_two, seconds_two[:16], *feed_two, 1, replicas, None)
    held_mixed = mixed_error(base_mixed_two, seconds_two[16:], mixed_two, 1, replicas, None)

    wide = jnp.concatenate(
        [norm_sums(under, norm_one), norm_sums(top_tail, norm_two), jnp.zeros((4, cols), F32)], axis=0
    )
    wide = total_over(wide, ("mp",))
    s_up, s_down = after(s_up, under[1][3]), after(s_down, under[1][3])
    feed_one, send_one = feed_first(0, feed_out_one, under)
    sums_feed_one = total_over(jnp.concatenate([send_one, wide], axis=0), ("dp",))
    wide = sums_feed_one[24:36].reshape(2, 6, cols)
    gain_sum, shift_sum = wide[:, :2], wide[:, 2:]
    base_feed_one, second_feed_one = feed_second(sums_feed_one, *feed_one)
    seconds_feed_one = total_over(second_feed_one, ("dp",))
    new_e_in, new_e_out = feed_error(base_feed_one, seconds_feed_one, *feed_one, 0, replicas, held_feed)

    mixed_one, send_mixed_one = mixed_first(0, set_in + whole_other, back_one, mixed_out_one, norm_one)
    sums_mixed_one = total_over(send_mixed_one, ("dp",))
    base_mixed_one, second_mixed_one = mixed_second(sums_mixed_one, mixed_one, width)
    seconds_mixed_one = total_over(second_mixed_one, ("dp",))
    new_e_qkv, new_e_o = mixed_error(base_mixed_one, seconds_mixed_one, mixed_one, 0, replicas, held_mixed)
    member_errors = [flip(new_e_qkv), new_e_o, new_e_in, new_e_out]

    def unpack_bases(feed, mixed):
        return [mixed[:24].reshape(3, 8, -1), mixed[24:, :width], feed[:8], feed[8:16]]

    def unpack_seconds(feed, mixed):
        proj = jnp.stack([mixed[:8, 256 * member : 256 * member + width] for member in range(3)])
        return [proj, mixed[8:], feed[:8], feed[8:16]]

    bases = (unpack_bases(base_feed_one, base_mixed_one), unpack_bases(base_feed_two, base_mixed_two))
    seconds = (unpack_seconds(seconds_feed_one, seconds_mixed_one), unpack_seconds(seconds_two[:16], seconds_two[16:]))
    scaled = [[second / replicas for second in seconds[layer]] for layer in range(2)]
    bias_rows = (sums_mixed_one[24], sums_two[48])
    bias_qv = jnp.stack([jnp.stack([row[256 : 256 + width], row[512 : 512 + width]]) for row in bias_rows])
    bias_in = jnp.stack([sums_feed_one[16], sums_two[16]])

    def part_of(value, axis):
        rows = value.shape[axis] // replicas
        return lax.dynamic_slice_in_dim(value, index * rows, rows, axis)

    def update_qkv(layer):
        base = part_of(bases[layer][0], 2)
        return jnp.einsum("jrm,jrn->jmn", base, scaled[layer][0], precision=HIGHEST)

    def update_o(layer):
        return dot(bases[layer][1], part_of(scaled[layer][1], 1), 0, 0, HIGHEST)

    def update_in(layer):
        return dot(part_of(bases[layer][2], 1), scaled[layer][2], 0, 0, HIGHEST)

    def update_out(layer):
        return flip(dot(part_of(scaled[layer][3], 1), bases[layer][3], 0, 0, HIGHEST))

    def renew(weight, moment, update):
        moment_new = MOMENTUM * moment + jnp.stack([update(0), update(1)])
        return weight - RATE * moment_new, moment_new

    new_w_qkv, new_m_qkv = renew(w_qkv, m_qkv, update_qkv)
    new_w_o, new_m_o = renew(w_o, m_o, update_o)
    new_w_in, new_m_in = renew(w_in, m_in, update_in)
    new_w_out, new_m_out = renew(w_out, m_out, update_out)
    new_m_qv = MOMENTUM * m_qv + bias_qv / replicas
    new_m_bin = MOMENTUM * m_bin + bias_in / replicas
    new_m_gain = MOMENTUM * m_gain + gain_sum / replicas
    new_m_shift = MOMENTUM * m_shift + shift_sum / replicas
    outer = [flip(jnp.stack([bases[0][member], bases[1][member]])) for member in range(4)]
    inner = [flip(jnp.stack([seconds[0][member], seconds[1][member]])) for member in range(4)]
    return (
        output, input_gradient, new_w_qkv, new_w_o, new_w_in, new_w_out,
        b_qv - RATE * new_m_qv, b_in - RATE * new_m_bin, ln_gain - RATE * new_m_gain, shifts - RATE * new_m_shift,
        new_m_qkv, new_m_o, new_m_in, new_m_out, new_m_qv, new_m_bin, new_m_gain, new_m_shift,
        *member_errors, *outer, *inner,
    )


def solution(mesh):
    in_specs = (
        P(("dp", "mp"), None), P(("dp", "mp"), None), P("dp", None), P("dp"),
        P(None, None, "dp", "mp"), P(None, "mp", "dp"), P(None, "dp", "mp"), P(None, "mp", "dp"),
        P(None, None, "mp"), P(None, "mp"), P(), P(),
        P(None, None, "dp", "mp"), P(None, "mp", "dp"), P(None, "dp", "mp"), P(None, "mp", "dp"),
        P(None, None, "mp"), P(None, "mp"), P(), P(),
        P("dp", None, None, None, "mp"), P("dp", None, "mp", None), P("dp", None, None, "mp"), P("dp", None, "mp", None),
        P(None, None, "mp", None), P(None, "mp", None), P(None, "mp", None), P(None, "mp", None),
    )
    out_specs = (
        P(("dp", "mp"), None), P(("dp", "mp"), None),
        P(None, None, "dp", "mp"), P(None, "mp", "dp"), P(None, "dp", "mp"), P(None, "mp", "dp"),
        P(None, None, "mp"), P(None, "mp"), P(), P(),
        P(None, None, "dp", "mp"), P(None, "mp", "dp"), P(None, "dp", "mp"), P(None, "mp", "dp"),
        P(None, None, "mp"), P(None, "mp"), P(), P(),
        P("dp", None, None, None, "mp"), P("dp", None, "mp", None), P("dp", None, None, "mp"), P("dp", None, "mp", None),
        P(None, None, "mp", None), P(None, "mp", None), P(None, "mp", None), P(None, "mp", None),
        P(None, None, "mp", None), P(None, "mp", None), P(None, "mp", None), P(None, "mp", None),
    )
    return jax.shard_map(per_device, mesh=mesh, in_specs=in_specs, out_specs=out_specs, check_vma=False)
```

```python
import jax
import jax.numpy as jnp
from jax import lax
from jax.experimental import pallas as pl
from jax.experimental.pallas import tpu as pltpu
from jax.sharding import PartitionSpec as P

HD = 64


NORM_EPS = 1e-05
ORTHO_EPS = 1e-06
MOMENTUM = 0.9
RATE = 0.05
MASKED = -1000000000.0
ROOT_HALF = 0.7071067811865476
INV_ROOT_TWO_PI = 0.3989422804014327
HIGHEST = lax.Precision.HIGHEST
LOW = jnp.bfloat16
F32 = jnp.float32


def dot(left, right, left_dim, right_dim, precision=None):
    return lax.dot_general(
        left,
        right,
        (((left_dim,), (right_dim,)), ((), ())),
        preferred_element_type=F32,
        precision=precision,
    )


def swap(value, axis, bit):
    size = lax.axis_size(axis)
    return lax.ppermute(value, axis, [(i, i ^ bit) for i in range(size)])


def gelu_parts(upper):
    cdf = 0.5 * (1.0 + lax.erf(upper * ROOT_HALF))
    slope = cdf + upper * jnp.exp(-0.5 * upper * upper) * INV_ROOT_TWO_PI
    return upper * cdf, slope


def after(value, *marks):
    return lax.optimization_barrier((value, *marks))[0]


def rows_sum(part, arrived):
    half = part.shape[0] // 2
    part, arrived = part.astype(F32), arrived.astype(F32)
    return jnp.concatenate([part[:half] + arrived[half:], part[half:] + arrived[:half]], axis=0)


def normal(rows_in):
    centred = rows_in - jnp.mean(rows_in, axis=-1, keepdims=True)
    inverse = lax.rsqrt(jnp.mean(centred * centred, axis=-1, keepdims=True) + NORM_EPS)
    return centred * inverse, inverse


def normal_back(grad, normed, inverse, gain):
    scaled = grad * gain
    inner = jnp.mean(scaled * normed, axis=-1, keepdims=True)
    return inverse * (scaled - jnp.mean(scaled, axis=-1, keepdims=True) - normed * inner)


class Arriving:
    def __init__(self, source, local, mark):
        self.local, self.shape, self.dtype, self.waited = local, local.shape, local.dtype, False
        self.copy = pltpu.make_async_copy(source, local, mark)
        self.copy.start()

    def __getitem__(self, index):
        self.settle()
        return self.local[index]

    def settle(self):
        if not self.waited:
            self.copy.wait()
            self.waited = True


class Leaving:
    def __init__(self, target, local, mark):
        self.local, self.shape, self.dtype, self.written = local, local.shape, local.dtype, 0
        self.copy = pltpu.make_async_copy(local, target, mark)

    def __setitem__(self, index, value):
        self.local[index] = value
        self.written += value.size
        if self.written == self.local.size:
            self.copy.start()

    def __getitem__(self, index):
        return self.local[index]

    def settle(self):
        assert self.written == self.local.size
        self.copy.wait()


def call(kernel, outs, args, name, flops, limit=24, scalars=None, far=(), far_outs=()):
    lead = 0 if scalars is None else 1
    inputs, results = len(args), len(outs)
    parts = {i: a[1] for i, a in enumerate(args) if isinstance(a, tuple)}
    kinds = [jax.ShapeDtypeStruct(a[0].shape[len(a[1]) :], a[0].dtype) if isinstance(a, tuple) else a for a in args]
    args = [a[0] if isinstance(a, tuple) else a for a in args]
    moved_in, moved_out = [kinds[i] for i in far], [outs[i] for i in far_outs]

    def body(*refs):
        refs = list(refs)
        scratch = refs[lead + inputs + results :]
        late = []
        for spot, i in enumerate(far):
            source = refs[lead + i].at[parts[i]] if i in parts else refs[lead + i]
            refs[lead + i] = Arriving(source, scratch[spot], scratch[-1].at[spot])
            late.append(refs[lead + i])
        for spot, i in enumerate(far_outs):
            spot += len(far)
            at = lead + inputs + i
            refs[at] = Leaving(refs[at], scratch[spot], scratch[-1].at[spot])
            late.append(refs[at])
        kernel(*refs[: lead + inputs + results])
        for item in late:
            item.settle()

    near = lambda shape: pl.BlockSpec(shape, lambda n=len(shape): (0,) * n)
    elsewhere = pl.BlockSpec(memory_space=pltpu.HBM)
    specs = [elsewhere if i in far else near(a.shape) for i, a in enumerate(args)]
    out_specs = [elsewhere if i in far_outs else near(shape) for i, (shape, _) in enumerate(outs)]
    scratch = [pltpu.VMEM(a.shape, a.dtype) for a in moved_in] + [pltpu.VMEM(shape, kind) for shape, kind in moved_out]
    if scratch:
        scratch.append(pltpu.SemaphoreType.DMA((len(scratch),)))
    operands = list(args)
    if lead:
        specs = [pl.BlockSpec(memory_space=pltpu.SMEM)] + specs
        operands = [scalars] + operands
    shapes = [jax.ShapeDtypeStruct(shape, kind) for shape, kind in outs]
    moved = sum(a.size * a.dtype.itemsize for a in [*kinds, *shapes])
    return pl.pallas_call(
        body,
        in_specs=specs,
        out_specs=out_specs,
        out_shape=shapes,
        scratch_shapes=scratch,
        cost_estimate=cost(flops, moved),
        compiler_params=params(limit),
        name=name,
    )(*operands)


def join_kernel(order, flags_ref, own_ref, other_ref, q_ref, kv_ref, out_ref):
    width = q_ref.shape[1] // 2
    rows = own_ref.shape[0] // len(order)
    front = flags_ref[0] == 0
    for spot, v in enumerate(order):
        here = slice(spot * rows, (spot + 1) * rows)
        there = here if len(order) == 1 else pl.ds(pl.multiple_of((flags_ref[2] ^ v) * rows, 16), rows)
        groups = []
        for part in range(4):
            lanes = slice(part * width, (part + 1) * width)
            own, other = own_ref[here, lanes].astype(F32), other_ref[here, lanes].astype(F32)
            left, right = jnp.where(front, own, other), jnp.where(front, other, own)
            groups.append(jnp.concatenate([left, right], axis=1).astype(LOW))
        q_ref[there, :] = groups[0]
        kv_ref[there, : 2 * width] = groups[1]
        kv_ref[there, 2 * width :] = groups[2]
        out_ref[there, :] = groups[3]


def project(low, wq_ref, wkv_ref, bias_ref, q_ref, kv_ref):
    width = wq_ref.shape[1]
    q_ref[...] = (dot(low, wq_ref[...], 1, 0) + bias_ref[:, :width]).astype(LOW)
    kv_ref[...] = (dot(low, wkv_ref[...], 1, 0) + bias_ref[:, width:]).astype(LOW)


def project_kernel(x_ref, wq_ref, wkv_ref, bias_ref, q_ref, kv_ref):
    project(x_ref[...], wq_ref, wkv_ref, bias_ref, q_ref, kv_ref)


def first_norm(rows, vec_ref):
    return normal(rows)[0] * vec_ref[0:1, :] + vec_ref[2:3, :]


def second_norm(rows, vec_ref):
    return normal(rows)[0] * vec_ref[1:2, :] + vec_ref[3:4, :]


def norm_project_kernel(
    sent_ref, arrived_ref, rows_ref, vec_ref, wq_ref, wkv_ref, bias_ref, out_ref, low_ref, q_ref, kv_ref
):
    rows = rows_sum(sent_ref[...], arrived_ref[...]) + vec_ref[5:6, :] + first_norm(rows_ref[...], vec_ref)
    out_ref[...] = rows
    low = second_norm(rows, vec_ref).astype(LOW)
    low_ref[...] = low
    project(low, wq_ref, wkv_ref, bias_ref, q_ref, kv_ref)


def pick(flag, first, second):
    return jnp.where(flag, first.astype(F32), second.astype(F32)).astype(LOW)


def attend_kernel(flags_ref, q_ref, k0_ref, k1_ref, k2_ref, k3_ref, place_ref, bound_ref, wo_ref,
                  keep_ref, give_ref, logsum_ref, sent_ref):
    rows, width = q_ref.shape
    pieces = (k0_ref, k1_ref, k2_ref, k3_ref)
    lanes = lax.broadcasted_iota(jnp.int32, (1, 128), 1)
    low, high = bound_ref[:, :1], bound_ref[:, 1:2]
    masks = []
    for index, ref in enumerate(pieces):
        place = place_ref[:, index * ref.shape[0] : (index + 1) * ref.shape[0]]
        masks.append(jnp.where((place >= low) & (place < high), 0.0, MASKED))
    logsums = jnp.zeros((rows, 128), F32)
    tiles = []
    for tile in range(width // 128):
        cols = slice(tile * 128, tile * 128 + 128)
        other = slice(width + tile * 128, width + tile * 128 + 128)
        query = q_ref[:, cols]
        out = None
        for side in range(2):
            here = (lanes >= side * HD) & (lanes < side * HD + HD)
            lone = jnp.where(here, query.astype(F32) * HD ** (-0.5), 0.0).astype(LOW)
            scores = [dot(lone, ref[:, cols], 1, 1) + mask for ref, mask in zip(pieces, masks)]
            highest = jnp.max(scores[0], axis=-1, keepdims=True)
            for score in scores[1:]:
                highest = jnp.maximum(highest, jnp.max(score, axis=-1, keepdims=True))
            powers = [jnp.exp(score - highest) for score in scores]
            total = sum(jnp.sum(power, axis=-1, keepdims=True) for power in powers)
            inverse = 1.0 / total
            head = sum(dot((power * inverse).astype(LOW), ref[:, other], 1, 0) for power, ref in zip(powers, pieces))
            head = jnp.where(here, head, 0.0)
            out = head if out is None else out + head
            logsums = jnp.where(lanes == 2 * tile + side, highest + jnp.log(total), logsums)
        tiles.append(out.astype(LOW))
    logsum_ref[...] = logsums
    mixed = jnp.concatenate(tiles, axis=1)
    half = width // 2
    keep_ref[...] = pick(flags_ref[0] == 0, mixed[:, :half], mixed[:, half:])
    give_ref[...] = pick(flags_ref[0] == 0, mixed[:, half:], mixed[:, :half])
    sent_ref[...] = dot(mixed, wo_ref[...], 1, 1).astype(LOW)


def attend_all_kernel(flags_ref, kinds, *refs):
    pieces, place_ref, wo_ref, rest = refs[:4], refs[4], refs[5], refs[6:]
    chunks = len(rest) // (kinds + 2)
    for j in range(chunks):
        outs = rest[2 * chunks + j * kinds : 2 * chunks + (j + 1) * kinds]
        attend_kernel(flags_ref, rest[j], *pieces, place_ref, rest[chunks + j], wo_ref, *outs)


def attend_back_kernel(first, *refs):
    rows_ref, wo_ref, q_ref, k0_ref, k1_ref, k2_ref, k3_ref, logsum_ref, resid_ref = refs[:9]
    sent_ref, arrived_ref, vec_ref, place_ref, bound_ref = refs[9:14]
    held_refs = () if first else refs[14:18]
    rest_ref, low_ref, norm_sums_ref, dq_ref, *sums_refs = refs[14 + len(held_refs) :]
    grad = rows_sum(sent_ref[...], arrived_ref[...]) + resid_ref[...]
    normed, inverse = normal(rows_ref[...])
    back = normal_back(grad, normed, inverse, vec_ref[0:1, :])
    rest_ref[...] = back
    put_sums(norm_sums_ref, [grad * normed, grad, back], 3)
    low_back = back.astype(LOW)
    low_ref[...] = low_back
    mixed_grad = dot(low_back, wo_ref[...], 1, 0).astype(LOW).astype(F32)
    rows, width = q_ref.shape
    pieces = (k0_ref, k1_ref, k2_ref, k3_ref)
    lanes = lax.broadcasted_iota(jnp.int32, (1, 128), 1)
    low, high = bound_ref[:, :1], bound_ref[:, 1:2]
    scale = HD ** (-0.5)
    masks = []
    for index, ref in enumerate(pieces):
        place = place_ref[:, index * ref.shape[0] : (index + 1) * ref.shape[0]]
        masks.append(jnp.where((place >= low) & (place < high), 0.0, MASKED))
    for tile in range(width // 128):
        cols = slice(tile * 128, tile * 128 + 128)
        other = slice(width + tile * 128, width + tile * 128 + 128)
        query, grad = q_ref[:, cols].astype(F32), mixed_grad[:, cols]
        dq = None
        dk, dv = [None] * 4, [None] * 4
        for side in range(2):
            here = (lanes >= side * HD) & (lanes < side * HD + HD)
            lone = jnp.where(here, query * scale, 0.0).astype(LOW)
            lone_grad = jnp.where(here, grad, 0.0).astype(LOW)
            logsum = jnp.sum(jnp.where(lanes == 2 * tile + side, logsum_ref[...], 0.0), axis=-1, keepdims=True)
            probs, prob_grads = [], []
            inner = None
            for ref, mask in zip(pieces, masks):
                prob = jnp.exp(dot(lone, ref[:, cols], 1, 1) + mask - logsum)
                prob_grad = dot(lone_grad, ref[:, other], 1, 1)
                probs.append(prob)
                prob_grads.append(prob_grad)
                piece = jnp.sum(prob * prob_grad, axis=-1, keepdims=True)
                inner = piece if inner is None else inner + piece
            for index, ref in enumerate(pieces):
                score = (probs[index] * (prob_grads[index] - inner)).astype(LOW)
                back = dot(score, ref[:, cols], 1, 0)
                back = jnp.where(here, back * scale, 0.0)
                dq = back if dq is None else dq + back
                key = dot(score, lone, 0, 0)
                value = dot(probs[index].astype(LOW), lone_grad, 0, 0)
                dk[index] = key if dk[index] is None else dk[index] + key
                dv[index] = value if dv[index] is None else dv[index] + value
        dq_ref[:, cols] = dq.astype(LOW)
        for index in range(4):
            key, value = dk[index], dv[index]
            if held_refs:
                key = key + held_refs[index][:, cols]
                value = value + held_refs[index][:, other]
            sums_refs[index][:, cols] = key.astype(sums_refs[index].dtype)
            sums_refs[index][:, other] = value.astype(sums_refs[index].dtype)


def feed_kernel(is_first, sent_ref, arrived_ref, resid_ref, vec_ref, before_ref, feed0_ref, feed1_ref, bias_ref,
                rows_ref, give_ref, act_ref, slope_ref, out_ref):
    resid = resid_ref[...].astype(F32) if is_first else second_norm(resid_ref[...], before_ref)
    rows = rows_sum(sent_ref[...], arrived_ref[...]) + vec_ref[4:5, :] + resid
    rows_ref[...] = rows
    low = first_norm(rows, vec_ref).astype(LOW)
    cols = low.shape[1]
    units = feed0_ref.shape[0]
    top = feed0_ref.shape[1] - units
    base = top - units
    give_ref[:, :cols] = low
    act, slope = gelu_parts(dot(low, feed0_ref[:, base:top], 1, 0) + bias_ref[0:1, :])
    act = act.astype(LOW)
    act_ref[...] = act
    slope_ref[:, :units] = slope.astype(LOW)
    part = dot(act, feed0_ref[:, top:], 1, 1)
    act, slope = gelu_parts(dot(low, feed1_ref[:, base:top], 1, 0) + bias_ref[1:2, :])
    act = act.astype(LOW)
    give_ref[:, cols:] = act
    slope_ref[:, units:] = slope.astype(LOW)
    out_ref[...] = (part + dot(act, feed1_ref[:, top:], 1, 1)).astype(LOW)


def put_sums(sums_ref, lists, start):
    half = lists[0].shape[0] // 2
    sums_ref[...] = jnp.zeros(sums_ref.shape, F32)
    for index, rows in enumerate(lists):
        sums_ref[start + index : start + index + 1, :] = jnp.sum(rows[:half], axis=0, keepdims=True)


def back_feed(grad, normed, inverse, gain, slope_ref, feed0_ref, feed1_ref, rest_ref, give_ref, keep_ref, out_ref, sums_ref):
    back = normal_back(grad, normed, inverse, gain)
    rest_ref[...] = back
    put_sums(sums_ref, [grad * normed, grad, back], 0)
    low = back.astype(LOW)
    cols = low.shape[1]
    units = feed0_ref.shape[0]
    top = feed0_ref.shape[1] - units
    base = top - units
    give_ref[:, :cols] = low
    upper = (dot(low, feed0_ref[:, top:], 1, 0) * slope_ref[:, :units].astype(F32)).astype(LOW)
    keep_ref[...] = upper
    part = dot(upper, feed0_ref[:, base:top], 1, 1)
    upper = (dot(low, feed1_ref[:, top:], 1, 0) * slope_ref[:, units:].astype(F32)).astype(LOW)
    give_ref[:, cols:] = upper
    out_ref[...] = (part + dot(upper, feed1_ref[:, base:top], 1, 1)).astype(LOW)


def top_kernel(flags_ref, sent_ref, arrived_ref, rows_ref, grad_ref, before_rows_ref, before_ref, vec_ref, slope_ref,
               feed0_ref, feed1_ref, y_ref, rest_ref, give_ref, keep_ref, out_ref, sums_ref):
    rows = rows_sum(sent_ref[...], arrived_ref[...]) + vec_ref[5:6, :] + first_norm(rows_ref[...], vec_ref)
    normed, inverse = normal(rows)
    half = normed.shape[0] // 2
    y = normed[:half] * vec_ref[1:2, :] + vec_ref[3:4, :]
    on = flags_ref[1] > 0
    y_ref[...] = jnp.where(on, y, second_norm(before_rows_ref[:half, :], before_ref))
    grad = jnp.where(on, grad_ref[...].astype(F32), 0.0)
    back_feed(grad, normed, inverse, vec_ref[1:2, :], slope_ref, feed0_ref, feed1_ref,
              rest_ref, give_ref, keep_ref, out_ref, sums_ref)


def under_kernel(flags_ref, sent_ref, arrived_ref, resid_ref, grad_ref, rows_ref, vec_ref, slope_ref,
                 feed0_ref, feed1_ref, rest_ref, give_ref, keep_ref, out_ref, sums_ref):
    grad = rows_sum(sent_ref[...], arrived_ref[...]) + resid_ref[...]
    grad = jnp.where(flags_ref[1] > 0, grad, grad_ref[...].astype(F32))
    normed, inverse = normal(rows_ref[...])
    back_feed(grad, normed, inverse, vec_ref[1:2, :], slope_ref, feed0_ref, feed1_ref,
              rest_ref, give_ref, keep_ref, out_ref, sums_ref)


def back_project_kernel(flags_ref, dq_ref, own_ref, arrived_ref, wq_ref, wkv_ref, keep_ref, give_ref, sent_ref):
    dq = dq_ref[...]
    dkv = (own_ref[...] + arrived_ref[...].astype(F32)).astype(LOW)
    sent_ref[...] = (dot(dq, wq_ref[...], 1, 1) + dot(dkv, wkv_ref[...], 1, 1)).astype(LOW)
    half = dq.shape[1] // 2
    groups = (dq, dkv[:, : 2 * half], dkv[:, 2 * half :])
    front = flags_ref[0] == 0
    keep_ref[...] = jnp.concatenate([pick(front, g[:, :half], g[:, half:]) for g in groups], axis=1)
    give_ref[...] = jnp.concatenate([pick(front, g[:, half:], g[:, :half]) for g in groups], axis=1)

def split(value):
    high = value.astype(LOW)
    return high, (value - high.astype(F32)).astype(LOW)


def split_dot(small, large, small_dim, large_dim):
    high, rest = split(large)
    lead, tail = split(small)
    rows = small.shape[0]
    both = dot(jnp.concatenate([lead, tail], axis=0), high, small_dim, large_dim)
    return both[:rows] + both[rows:] + dot(lead, rest, small_dim, large_dim)


def dot_chunks(lefts, rights):
    total = None
    for left, right in zip(lefts, rights):
        part = dot(left[...], right[...], 0, 0)
        total = part if total is None else total + part
    return total


def rows_total_kernel(chunks, *refs):
    lefts, rights = refs[:chunks], refs[chunks : 2 * chunks]
    error_ref, start_ref, total_ref, first_ref, bias_ref = refs[2 * chunks :]
    total = dot_chunks(lefts, rights) + error_ref[...]
    total_ref[...] = total
    first_ref[...] = split_dot(start_ref[...], total, 1, 1)

    @pl.when(pl.program_id(0) == 0)
    def _():
        bias = sum(jnp.sum(ref[...].astype(F32), axis=0, keepdims=True) for ref in rights)
        bias_ref[...] = jnp.concatenate([bias, jnp.zeros((7, bias.shape[1]), F32)], axis=0)


def params(limit, **more):
    return pltpu.CompilerParams(vmem_limit_bytes=limit << 20, **more)


def cost(flops, moved):
    return pl.CostEstimate(flops=int(flops), bytes_accessed=int(moved), transcendentals=0)


def rows_total(lefts, rights, errors, starts, layer):
    rows, cols = errors.shape[-2:]
    tokens = lefts[0][0].shape[0]
    rank = starts.shape[1]
    step = 256
    chunks = len(lefts)
    return pl.pallas_call(
        lambda *refs: rows_total_kernel(chunks, *refs),
        grid=(rows // step,),
        in_specs=[pl.BlockSpec((tokens, step), lambda i, at=at: (0, i + at * (rows // step))) for _, at in lefts]
        + [pl.BlockSpec((tokens, cols), lambda i, at=at: (0, at)) for _, at in rights]
        + [
            pl.BlockSpec((None, None, step, cols), lambda i: (0, layer, i, 0)),
            pl.BlockSpec((None, rank, cols), lambda i: (layer, 0, 0)),
        ],
        out_specs=[
            pl.BlockSpec((step, cols), lambda i: (i, 0)),
            pl.BlockSpec((rank, step), lambda i: (0, i)),
            pl.BlockSpec((rank, cols), lambda i: (0, 0)),
        ],
        out_shape=[
            jax.ShapeDtypeStruct((rows, cols), F32),
            jax.ShapeDtypeStruct((rank, rows), F32),
            jax.ShapeDtypeStruct((rank, cols), F32),
        ],
        cost_estimate=cost(2 * chunks * tokens * rows * cols, 8 * rows * cols + 4 * chunks * tokens * rows),
        compiler_params=params(24),
        name="rows_total",
    )(*[array for array, _ in lefts], *[array for array, _ in rights], errors, starts)


def mixed_total_kernel(chunks, *refs):
    proj_refs, whole_refs = refs[:chunks], refs[chunks : 2 * chunks]
    attended_refs, piece_refs = refs[2 * chunks : 3 * chunks], refs[3 * chunks : 4 * chunks]
    e_proj_ref, e_back_ref, s_proj_ref, s_back_ref, total_ref, first_ref = refs[4 * chunks :]
    width = e_back_ref.shape[0]
    grads = dot_chunks(proj_refs, whole_refs)
    for member in range(3):
        rows = slice(member * width, (member + 1) * width)
        total = grads[rows] + e_proj_ref[member]
        total_ref[rows, :] = total
        first_ref[8 * member : 8 * member + 8, :] = split_dot(s_proj_ref[member], total, 1, 0)
    total = dot_chunks(attended_refs, piece_refs) + e_back_ref[...]
    total_ref[3 * width :, :] = total
    first_ref[24:, :] = jnp.zeros((8, total.shape[1]), F32)
    first_ref[24:, :width] = split_dot(s_back_ref[...], total, 1, 1)
    sums = sum(jnp.sum(ref[...].astype(F32), axis=0, keepdims=True) for ref in proj_refs)
    first_ref[24:25, 256 : 256 + width] = sums[:, :width]
    first_ref[24:25, 512 : 512 + width] = sums[:, 2 * width :]


def mixed_total(proj_low, whole_in, attended, piece, e_proj, e_back, s_proj, s_back, layer):
    tokens, width = attended[0].shape
    cols = whole_in[0].shape[1]
    rank = s_back.shape[1]
    chunks = len(attended)
    args = [*proj_low, *whole_in, *attended, *piece, (e_proj, (0, layer)), (e_back, (0, layer)), s_proj[layer], s_back[layer]]
    return call(
        lambda *refs: mixed_total_kernel(chunks, *refs),
        [[(4 * width, cols), F32], [(4 * rank, cols), F32]],
        args, "mixed_total", 2 * chunks * tokens * 4 * width * cols, 24, None, range(4 * chunks + 2),
    )


def ortho_rows(factor):
    rank = factor.shape[0]
    index = lax.broadcasted_iota(jnp.int32, (rank, 1), 0)
    for row in range(rank):
        vector = factor[row : row + 1, :]
        inner = jnp.sum(factor * vector, axis=1, keepdims=True)
        scale = lax.rsqrt(inner[row : row + 1] + ORTHO_EPS)
        vector = vector * scale
        factor = jnp.where(
            index < row, factor, jnp.where(index == row, vector, factor - vector * (inner * scale))
        )
    return factor


def feed_second_kernel(sums_ref, up_ref, down_ref, base_ref, second_ref):
    for member, total_ref in enumerate((up_ref, down_ref)):
        rows = slice(8 * member, 8 * member + 8)
        base = ortho_rows(sums_ref[rows, :])
        base_ref[rows, :] = base
        second_ref[rows, :] = split_dot(base, total_ref[...], 1, 0)


def feed_second(sums, m_up, m_down):
    cols = m_up.shape[1]
    return pl.pallas_call(
        feed_second_kernel,
        out_shape=[jax.ShapeDtypeStruct((16, cols), F32)] * 2,
        cost_estimate=cost(96 * m_up.size, 8 * m_up.size),
        compiler_params=params(24),
        name="feed_second",
    )(sums, m_up, m_down)


def mixed_second_kernel(width, sums_ref, total_ref, base_ref, second_ref):
    second_ref[...] = jnp.zeros(second_ref.shape, F32)
    for member in range(3):
        rows = slice(8 * member, 8 * member + 8)
        base = ortho_rows(sums_ref[rows, :])
        base_ref[rows, :] = base
        second_ref[:8, 256 * member : 256 * member + width] = split_dot(
            base, total_ref[member * width : (member + 1) * width, :], 1, 1
        )
    base = ortho_rows(sums_ref[24:32, :width])
    base_ref[24:32, :width] = base
    second_ref[8:, :] = split_dot(base, total_ref[3 * width :, :], 1, 0)


def mixed_second(sums, m_mixed, width):
    cols = m_mixed.shape[1]
    return pl.pallas_call(
        lambda *refs: mixed_second_kernel(width, *refs),
        out_shape=[jax.ShapeDtypeStruct((32, cols), F32), jax.ShapeDtypeStruct((16, cols), F32)],
        cost_estimate=cost(48 * m_mixed.size, 4 * m_mixed.size),
        compiler_params=params(16),
        name="mixed_second",
    )(sums, m_mixed)


def low_rank(base, second):
    b_high, b_rest = split(base)
    s_high, s_rest = split(second)
    left = jnp.concatenate([b_high, b_rest, b_high], axis=0)
    right = jnp.concatenate([s_high, s_high, s_rest], axis=0)
    return dot(left, right, 0, 0)


def feed_error_kernel(layer, replicas, base_ref, second_ref, up_ref, down_ref, *refs):
    up_out, down_out = refs[-2:]
    seconds = second_ref[...] * (1.0 / replicas)
    up_out[...] = up_ref[...] - low_rank(base_ref[:8, :], seconds[:8])
    down_out[...] = down_ref[...] - low_rank(base_ref[8:16, :], seconds[8:16])


def feed_error(base, second, m_up, m_down, layer, replicas, held):
    rows, cols = m_up.shape
    rank2 = base.shape[0]
    step = 256
    shape = jax.ShapeDtypeStruct((1, 2, rows, cols), F32)
    out_spec = pl.BlockSpec((None, None, step, cols), lambda i: (0, layer, i, 0))
    extra = {} if held is None else {"input_output_aliases": {4: 0, 5: 1}}
    return pl.pallas_call(
        lambda *refs: feed_error_kernel(layer, replicas, *refs),
        grid=(rows // step,),
        in_specs=[
            pl.BlockSpec((rank2, step), lambda i: (0, i)),
            pl.BlockSpec((rank2, cols), lambda i: (0, 0)),
            pl.BlockSpec((step, cols), lambda i: (i, 0)),
            pl.BlockSpec((step, cols), lambda i: (i, 0)),
        ] + ([] if held is None else [pl.BlockSpec(memory_space=pl.ANY)] * 2),
        out_specs=[out_spec, out_spec],
        out_shape=[shape, shape],
        cost_estimate=cost(100 * m_up.size, 16 * m_up.size),
        compiler_params=params(16),
        name="feed_error",
        **extra,
    )(base, second, m_up, m_down, *(() if held is None else held))


def mixed_error_kernel(replicas, base_ref, second_ref, total_ref, *refs):
    proj_out, back_out = refs[-2:]
    width = back_out.shape[0]
    seconds = second_ref[...] * (1.0 / replicas)
    for member in range(3):
        approx = low_rank(seconds[:8, 256 * member : 256 * member + width], base_ref[8 * member : 8 * member + 8, :])
        proj_out[member] = total_ref[member * width : (member + 1) * width, :] - approx
    back_out[...] = total_ref[3 * width :, :] - low_rank(base_ref[24:32, :width], seconds[8:])


def mixed_error(base, second, m_mixed, layer, replicas, held):
    rows, cols = m_mixed.shape
    width = rows // 4
    extra = {} if held is None else {"input_output_aliases": {3: 0, 4: 1}}
    return pl.pallas_call(
        lambda *refs: mixed_error_kernel(replicas, *refs),
        grid=(1,),
        in_specs=[
            pl.BlockSpec(base.shape, lambda i: (0, 0)),
            pl.BlockSpec(second.shape, lambda i: (0, 0)),
            pl.BlockSpec((rows, cols), lambda i: (0, 0)),
        ] + ([] if held is None else [pl.BlockSpec(memory_space=pl.ANY)] * 2),
        out_specs=[
            pl.BlockSpec((None, None, 3, width, cols), lambda i: (0, layer, 0, 0, 0)),
            pl.BlockSpec((None, None, width, cols), lambda i: (0, layer, 0, 0)),
        ],
        out_shape=[
            jax.ShapeDtypeStruct((1, 2, 3, width, cols), F32), jax.ShapeDtypeStruct((1, 2, width, cols), F32)
        ],
        cost_estimate=cost(50 * m_mixed.size, 8 * m_mixed.size),
        compiler_params=params(24),
        name="mixed_error",
        **extra,
    )(base, second, m_mixed, *(() if held is None else held))


def flip(value):
    return jnp.swapaxes(value, -1, -2)


def per_device(
    x_in, out_grad, doc_lengths, keep_layer, w_qkv, w_o, w_in, w_out, b_qv, b_in, ln_gain, shifts,
    m_qkv, m_o, m_in, m_out, m_qv, m_bin, m_gain, m_shift, e_qkv, e_o, e_in, e_out, q_qkv, q_o, q_in, q_out,
):
    own_rows, cols = x_in.shape
    replicas = lax.axis_size("dp")
    index = lax.axis_index("dp")
    place = lax.axis_index("mp")
    width = w_o.shape[1]
    front = lax.rem(place, 2) == 0
    flags = jnp.stack([lax.rem(place, 2), keep_layer[0], index]).astype(jnp.int32)
    chunks = 2
    step = own_rows // chunks
    size = 2 * step
    pair = range(chunks)

    def core(value):
        return swap(value, "mp", 1)

    def chip(value):
        return swap(value, "mp", 2)

    def gather(piece):
        return lax.all_gather(piece, "dp", axis=0, tiled=True)

    def join(own, other, axis):
        return jnp.where(
            front, jnp.concatenate([own, other], axis=axis), jnp.concatenate([other, own], axis=axis)
        )

    def mixed_piece(layer):
        return jnp.concatenate(
            [w_qkv[layer, 0], w_qkv[layer, 1], w_qkv[layer, 2], flip(w_o[layer])], axis=1
        ).astype(LOW)

    def feed_piece(layer):
        return jnp.concatenate([w_in[layer], flip(w_out[layer])], axis=1).astype(LOW)

    def by_chunk(rows, arrived):
        return [
            jnp.concatenate([rows[j * step : (j + 1) * step], arrived[j * step : (j + 1) * step]], axis=0) for j in pair
        ]

    small = jnp.concatenate([b_qv.reshape(-1), b_in.reshape(-1)]).reshape(-1, 128)
    small = core(small).reshape(-1)
    other_qv = small[: b_qv.size].reshape(b_qv.shape)
    other_in = small[b_qv.size :].reshape(b_in.shape)

    ends = jnp.sum(
        jnp.where(
            jnp.arange(doc_lengths.shape[1])[:, None] <= jnp.arange(doc_lengths.shape[1])[None, :],
            doc_lengths[0][:, None], 0,
        ),
        axis=0,
    )

    def places_of(device, j):
        steps = jnp.arange(step, dtype=jnp.int32) + j * step
        return jnp.concatenate([device * own_rows + steps, (device ^ 2) * own_rows + steps])

    mine = [places_of(place, j) for j in pair]
    all_places = jnp.concatenate(mine + [places_of(place ^ 1, j) for j in pair])[None, :]

    def bounds_of(places):
        passed = places[:, None] >= ends[None, :]
        low = jnp.max(jnp.where(passed, ends[None, :], 0), axis=1)
        high = jnp.min(jnp.where(passed, 1 << 30, ends[None, :]), axis=1)
        return jnp.stack([low, high], axis=1)

    bounds = [bounds_of(places) for places in mine]

    vecs, feeds, proj_bias, feed_bias = [], [], [], []
    for layer in range(2):
        gain, shift = ln_gain[layer], shifts[layer]
        vecs.append(
            jnp.concatenate(
                [gain, shift[1:2], shift[3:4], shift[0:1], shift[2:3], jnp.zeros((2, cols), F32)], axis=0
            )
        )
        proj_bias.append(
            jnp.concatenate(
                [
                    join(b_qv[layer, 0], other_qv[layer, 0], 0),
                    jnp.zeros((2 * width,), F32),
                    join(b_qv[layer, 1], other_qv[layer, 1], 0),
                ]
            )[None]
        )
        feed_bias.append(jnp.stack([b_in[layer], other_in[layer]]))

    set_in = by_chunk(x_in, chip(x_in))
    order = [0]
    bits = [4, 2, 1] if replicas == 8 else []
    for bit in bits:
        order = order + [v ^ bit for v in order]
    if not bits:
        order = order[:1]

    def doubled(piece, bit):
        return jnp.concatenate([piece, swap(piece, "dp", bit)], axis=0)

    feed_whole = jnp.concatenate([mixed_piece(1), feed_piece(0)], axis=1)
    whole_mixed = mixed_piece(0)
    if bits:
        feed_whole = gather(feed_whole)
        set_grad = by_chunk(out_grad, chip(after(out_grad, *set_in)))
        whole_mixed = doubled(doubled(whole_mixed, 4), 2)
        whole_mixed, all_places, flags, *rest = lax.optimization_barrier(
            (whole_mixed, all_places, flags, *bounds, *vecs, *proj_bias, *feed_bias, *set_in, *set_grad)
        )
        bounds, vecs, proj_bias, feed_bias = rest[:2], rest[2:4], rest[4:6], rest[6:8]
        set_in, set_grad = rest[8:10], rest[10:12]
        whole_mixed = doubled(whole_mixed, 1)
    else:
        set_grad = by_chunk(out_grad, chip(out_grad))
        whole_mixed = gather(whole_mixed)
        feed_whole = gather(feed_whole)
    feed_late, *set_in = lax.optimization_barrier((feed_piece(1), *set_in))
    feed_late = gather(feed_late)
    whole_other = [core(rows) for rows in set_in]

    full = [(size, cols), F32]
    full_low = [(size, cols), LOW]
    thin = [(size, 128), F32]
    half_low = [(size, 2 * width), LOW]
    one_low = [(size, width), LOW]
    kv_low = [(size, 4 * width), LOW]
    units = cols

    def mixed_weights(own, other, order):
        return call(
            lambda *refs: join_kernel(order, *refs), [[(cols, 2 * width), LOW], [(cols, 4 * width), LOW], [(cols, 2 * width), LOW]],
            [own, other], "join", 0, 16, flags,
        )

    def attention(layer, q, kv):
        pieces = kv + [core(part) for part in kv]
        kinds = [one_low, one_low, thin, full_low]
        outs = call(
            lambda flags_ref, *refs: attend_all_kernel(flags_ref, len(kinds), *refs), kinds * chunks,
            [*pieces, all_places, wo[layer], *q, *bounds], "attend",
            chunks * (2 * size * (4 * size) * 4 * width + 2 * size * 2 * width * cols), 20, flags,
        )
        return pieces, [outs[j * len(kinds) : (j + 1) * len(kinds)] for j in pair]

    def feed_all(layer, outs, resid):
        return [
            call(
                lambda *refs: feed_kernel(layer == 0, *refs),
                [full, [(size, cols + units), LOW], [(size, units), LOW], [(size, 2 * units), LOW], full_low],
                [outs[j][3], chip(outs[j][3]), resid[j], vecs[layer], vecs[0], *feeds[layer], feed_bias[layer]],
                "feed", 8 * size * cols * units, 24,
            )
            for j in pair
        ]

    e_proj, s_proj = flip(e_qkv), flip(q_qkv)
    e_proj, e_back, e_up, e_down = (
        pltpu.with_memory_space_constraint(value, pltpu.HBM) for value in (e_proj, e_o, e_in, e_out)
    )
    s_back, s_up, s_down = flip(q_o), flip(q_in), flip(q_out)

    def feed_up(layer, feed_out, tails, start):
        give_up = [out[1] for out in feed_out]
        give_down = [out[1] for out in tails]
        return rows_total(
            [(rows, 0) for rows in give_up + [core(rows) for rows in give_up]],
            [(out[2], 0) for out in tails] + [(core(rows), 1) for rows in give_down], e_up, start, layer,
        )

    def feed_down(layer, feed_out, tails, start):
        give_up = [out[1] for out in feed_out]
        give_down = [out[1] for out in tails]
        return rows_total(
            [(out[2], 0) for out in feed_out] + [(core(rows), 1) for rows in give_up],
            [(rows, 0) for rows in give_down + [core(rows) for rows in give_down]], e_down, start, layer,
        )

    def mixed_first(layer, low, back, mixed, norm, start):
        return mixed_total(
            [out[0] for out in back] + [core(out[1]) for out in back],
            low,
            [out[0] for out in mixed] + [core(out[1]) for out in mixed],
            [out[1] for out in norm] + [core(out[1]) for out in norm],
            e_proj, e_back, s_proj, start, layer,
        )

    def total_over(value, axis):
        bit = 1
        while bit < lax.axis_size(axis):
            value = value + swap(value, axis, bit)
            bit = 2 * bit
        return value

    class Total:
        def __init__(self, value):
            self.value, self.bit = value, 1

        def step(self, *marks):
            if self.bit < replicas:
                self.value = self.value + after(swap(self.value, "dp", self.bit), *marks)
                self.bit = 2 * self.bit

        def rest(self):
            while self.bit < replicas:
                self.value = self.value + swap(self.value, "dp", self.bit)
                self.bit = 2 * self.bit
            return self.value

    def norm_sums(tails, norm):
        return sum(out[4] for out in tails) + sum(out[3] for out in norm)

    wq, wkv, wo = ([part] for part in mixed_weights(whole_mixed, core(whole_mixed), order))
    first = [
        call(
            project_kernel, [half_low, kv_low], [set_in[j], wq[0], wkv[0], proj_bias[0]],
            "project", 2 * size * cols * 6 * width, 10,
        )
        for j in pair
    ]
    q_one = [out[0] for out in first]
    pieces_one, mixed_out_one = attention(0, q_one, [out[1] for out in first])
    feed_whole = after(feed_whole, mixed_out_one[0][2])
    feeds.append((feed_whole, core(feed_whole)))
    feed_out_one = feed_all(0, mixed_out_one, set_in)
    own_late = after(feed_whole, feed_out_one[1][4])
    for held, part in zip((wq, wkv, wo), mixed_weights(own_late, feeds[0][1], [0])):
        held.append(part)
    second = [
        call(
            norm_project_kernel, [full, full_low, half_low, kv_low],
            [feed_out_one[j][4], chip(feed_out_one[j][4]), feed_out_one[j][0], vecs[0], wq[1], wkv[1], proj_bias[1]],
            "norm_project", 2 * size * cols * 6 * width, 12,
        )
        for j in pair
    ]
    q_two = [out[2] for out in second]
    pieces_two, mixed_out_two = attention(1, q_two, [out[3] for out in second])
    feed_late = after(feed_late, mixed_out_two[1][2])
    other_late = core(feed_late)
    feeds.append((feed_late, other_late))
    feed_out_two = feed_all(1, mixed_out_two, [out[0] for out in second])

    wide_outs = [full, [(size, cols + units), LOW], [(size, units), LOW], full_low, [(8, cols), F32]]
    top = [
        call(
            top_kernel, [[(step, cols), F32]] + wide_outs,
            [
                feed_out_two[j][4], chip(feed_out_two[j][4]), feed_out_two[j][0], set_grad[j], second[j][0], vecs[0],
                vecs[1], feed_out_two[j][3], *feeds[1],
            ],
            "top", 8 * size * cols * units, 26, flags,
        )
        for j in pair
    ]
    output = jnp.concatenate([out[0] for out in top], axis=0)

    def attention_back(layer, outs, feed_out, q, pieces, mixed, vec, between, ending):
        held, dqs, norms = [], [], []
        for j in pair:
            kinds = [full] * 4 if j + 1 < chunks else [full, full, full_low, full_low]
            rest, low, sums, dq, *held = call(
                lambda *refs, j=j: attend_back_kernel(j == 0, *refs),
                [full, full_low, [(8, cols), F32], half_low] + kinds,
                [
                    feed_out[j][0], wo[layer], q[j], *pieces, mixed[j][2], outs[j][0],
                    outs[j][3], chip(outs[j][3]), vec, all_places, bounds[j], *held,
                ],
                "attend_back", 5 * size * (4 * size) * 4 * width, 26, None, range(8),
            )
            dqs.append(dq)
            norms.append((rest, low, None, sums))
            if j == 0:
                vec = between(vec, sums)
        back_flags = ending(flags, sums)
        return norms, [
            call(
                back_project_kernel, [[(size, 3 * width), LOW], [(size, 3 * width), LOW], full_low],
                [dqs[j], held[j], core(held[2 + j]), wq[layer], wkv[layer]], "back_project",
                2 * size * cols * 6 * width, 12, back_flags,
            )
            for j in pair
        ]

    top_tail = [out[1:] for out in top]
    feed_two_up = feed_up(1, feed_out_two, top_tail, after(s_up, top[1][5]))
    norm_two, back_two = attention_back(
        1, top_tail, feed_out_two, q_two, pieces_two, mixed_out_two, after(vecs[1], feed_two_up[1]),
        lambda vec, sums: vec, lambda flags, sums: flags,
    )
    sent = back_two[1][2]
    feed_two_down = feed_down(1, feed_out_two, top_tail, after(s_down, sent))
    low_two = [out[1] for out in second]
    mixed_two, send_mixed_two = mixed_first(
        1, low_two + [core(rows) for rows in low_two], back_two, mixed_out_two, norm_two, after(s_back, sent)
    )
    sums_two = total_over(
        jnp.concatenate([feed_two_up[1], feed_two_down[1], feed_two_up[2], send_mixed_two], axis=0), "dp"
    )
    under, under_flags = [], after(flags, feed_two_down[1], send_mixed_two)
    for j in pair:
        under.append(
            call(
                under_kernel, wide_outs,
                [
                    back_two[j][2], chip(back_two[j][2]), norm_two[j][0], set_grad[j], second[j][0],
                    vecs[0], feed_out_one[j][3], *feeds[0],
                ],
                "under", 8 * size * cols * units, 24, under_flags,
            )
        )
    feed_one_up = feed_up(0, feed_out_one, under, after(s_up, under[1][4]))
    feed_one_down = feed_down(0, feed_out_one, under, after(s_down, under[1][4]))
    m_feed_one, m_feed_two = (feed_one_up[0], feed_one_down[0]), (feed_two_up[0], feed_two_down[0])

    seconds_of_two = []

    def ending(flags, sums):
        sums_here = after(sums_two, sums)
        seconds_of_two.extend(feed_second(sums_here[:24], *m_feed_two))
        seconds_of_two.extend(mixed_second(sums_here[24:], mixed_two, width))
        return after(flags, seconds_of_two[1], seconds_of_two[3])

    norm_one, back_one = attention_back(
        0, under, feed_out_one, q_one, pieces_one, mixed_out_one,
        after(vecs[0], feed_one_up[1], feed_one_down[1]), lambda vec, sums: vec, ending,
    )
    last_flights = [chip(out[2][step:]) for out in back_one]

    sents = [out[2] for out in back_one]
    base_feed_two, second_feed_two, base_mixed_two, second_mixed_two = seconds_of_two
    last_two = Total(jnp.concatenate([second_feed_two, second_mixed_two], axis=0))
    last_two.step(*sents)
    mixed_one, send_mixed_one = mixed_first(
        0, set_in + whole_other, back_one, mixed_out_one, norm_one, s_back
    )
    total_one = jnp.concatenate([feed_one_up[1], feed_one_down[1], feed_one_up[2], send_mixed_one], axis=0)
    sums_one = total_over(total_one, "dp")
    sums_feed_one, sums_mixed_one = sums_one[:24], sums_one[24:]
    last_two.step(send_mixed_one)
    input_gradient = jnp.concatenate(
        [
            back_one[j][2][:step].astype(F32) + after(last_flights[j], send_mixed_one).astype(F32) + norm_one[j][0][:step]
            for j in pair
        ],
        axis=0,
    )
    seconds_two = last_two.rest()
    wide = jnp.concatenate([norm_sums(under, norm_one), norm_sums(top_tail, norm_two)], axis=0)
    wide = total_over(after(wide, send_mixed_one), "mp")
    base_feed_one, second_feed_one = feed_second(sums_feed_one, *m_feed_one)
    base_mixed_one, second_mixed_one = mixed_second(sums_mixed_one, mixed_one, width)
    seconds_one = total_over(jnp.concatenate([second_feed_one, second_mixed_one, wide], axis=0), "dp")
    seconds_feed_one, seconds_mixed_one, wide = seconds_one[:16], seconds_one[16:32], seconds_one[32:].reshape(2, 8, cols)
    gain_sum = jnp.concatenate([wide[:, 3:4], wide[:, 0:1]], axis=1)
    shift_sum = jnp.concatenate([wide[:, 5:6], wide[:, 4:5], wide[:, 2:3], wide[:, 1:2]], axis=1)
    held_feed = feed_error(base_feed_two, seconds_two[:16], *m_feed_two, 1, replicas, None)
    held_mixed = mixed_error(base_mixed_two, seconds_two[16:32], mixed_two, 1, replicas, None)
    new_e_in, new_e_out = feed_error(base_feed_one, seconds_feed_one, *m_feed_one, 0, replicas, held_feed)
    new_e_qkv, new_e_o = mixed_error(base_mixed_one, seconds_mixed_one, mixed_one, 0, replicas, held_mixed)
    member_errors = [flip(new_e_qkv), new_e_o, new_e_in, new_e_out]

    def unpack_bases(feed, mixed):
        return [mixed[:24].reshape(3, 8, -1), mixed[24:, :width], feed[:8], feed[8:16]]

    def unpack_seconds(feed, mixed):
        proj = jnp.stack([mixed[:8, 256 * member : 256 * member + width] for member in range(3)])
        return [proj, mixed[8:], feed[:8], feed[8:16]]

    bases = (unpack_bases(base_feed_one, base_mixed_one), unpack_bases(base_feed_two, base_mixed_two))
    seconds = (unpack_seconds(seconds_feed_one, seconds_mixed_one), unpack_seconds(seconds_two[:16], seconds_two[16:32]))
    scaled = [[second / replicas for second in seconds[layer]] for layer in range(2)]
    bias_rows = (sums_mixed_one[24], sums_two[48])
    bias_qv = jnp.stack([jnp.stack([row[256 : 256 + width], row[512 : 512 + width]]) for row in bias_rows])
    bias_in = jnp.stack([sums_feed_one[16], sums_two[16]])

    def part_of(value, axis):
        rows = value.shape[axis] // replicas
        return lax.dynamic_slice_in_dim(value, index * rows, rows, axis)

    def update_qkv(layer):
        base = part_of(bases[layer][0], 2)
        return jnp.einsum("jrm,jrn->jmn", base, scaled[layer][0], precision=HIGHEST)

    def update_o(layer):
        return dot(bases[layer][1], part_of(scaled[layer][1], 1), 0, 0, HIGHEST)

    def update_in(layer):
        return dot(part_of(bases[layer][2], 1), scaled[layer][2], 0, 0, HIGHEST)

    def update_out(layer):
        return flip(dot(part_of(scaled[layer][3], 1), bases[layer][3], 0, 0, HIGHEST))

    def renew(weight, moment, update):
        moment_new = MOMENTUM * moment + jnp.stack([update(0), update(1)])
        return weight - RATE * moment_new, moment_new

    new_w_qkv, new_m_qkv = renew(w_qkv, m_qkv, update_qkv)
    new_w_o, new_m_o = renew(w_o, m_o, update_o)
    new_w_in, new_m_in = renew(w_in, m_in, update_in)
    new_w_out, new_m_out = renew(w_out, m_out, update_out)
    new_m_qv = MOMENTUM * m_qv + bias_qv / replicas
    new_m_bin = MOMENTUM * m_bin + bias_in / replicas
    new_m_gain = MOMENTUM * m_gain + gain_sum / replicas
    new_m_shift = MOMENTUM * m_shift + shift_sum / replicas
    outer = [flip(jnp.stack([bases[0][member], bases[1][member]])) for member in range(4)]
    inner = [flip(jnp.stack([seconds[0][member], seconds[1][member]])) for member in range(4)]
    return (
        output, input_gradient, new_w_qkv, new_w_o, new_w_in, new_w_out,
        b_qv - RATE * new_m_qv, b_in - RATE * new_m_bin, ln_gain - RATE * new_m_gain, shifts - RATE * new_m_shift,
        new_m_qkv, new_m_o, new_m_in, new_m_out, new_m_qv, new_m_bin, new_m_gain, new_m_shift,
        *member_errors, *outer, *inner,
    )


def solution(mesh):
    in_specs = (
        P(("dp", "mp"), None), P(("dp", "mp"), None), P("dp", None), P("dp"),
        P(None, None, "dp", "mp"), P(None, "mp", "dp"), P(None, "dp", "mp"), P(None, "mp", "dp"),
        P(None, None, "mp"), P(None, "mp"), P(), P(),
        P(None, None, "dp", "mp"), P(None, "mp", "dp"), P(None, "dp", "mp"), P(None, "mp", "dp"),
        P(None, None, "mp"), P(None, "mp"), P(), P(),
        P("dp", None, None, None, "mp"), P("dp", None, "mp", None), P("dp", None, None, "mp"), P("dp", None, "mp", None),
        P(None, None, "mp", None), P(None, "mp", None), P(None, "mp", None), P(None, "mp", None),
    )
    out_specs = (
        P(("dp", "mp"), None), P(("dp", "mp"), None),
        P(None, None, "dp", "mp"), P(None, "mp", "dp"), P(None, "dp", "mp"), P(None, "mp", "dp"),
        P(None, None, "mp"), P(None, "mp"), P(), P(),
        P(None, None, "dp", "mp"), P(None, "mp", "dp"), P(None, "dp", "mp"), P(None, "mp", "dp"),
        P(None, None, "mp"), P(None, "mp"), P(), P(),
        P("dp", None, None, None, "mp"), P("dp", None, "mp", None), P("dp", None, None, "mp"), P("dp", None, "mp", None),
        P(None, None, "mp", None), P(None, "mp", None), P(None, "mp", None), P(None, "mp", None),
        P(None, None, "mp", None), P(None, "mp", None), P(None, "mp", None), P(None, "mp", None),
    )
    return jax.shard_map(per_device, mesh=mesh, in_specs=in_specs, out_specs=out_specs, check_vma=False)
```

```python
import jax
import jax.numpy as jnp
from jax import lax
from jax.experimental import pallas as pl
from jax.experimental.pallas import tpu as pltpu
from jax.sharding import PartitionSpec as P

HD = 64


NORM_EPS = 1e-05
ORTHO_EPS = 1e-06
MOMENTUM = 0.9
RATE = 0.05
MASKED = -1000000000.0
ROOT_HALF = 0.7071067811865476
INV_ROOT_TWO_PI = 0.3989422804014327
HIGHEST = lax.Precision.HIGHEST
LOW = jnp.bfloat16
F32 = jnp.float32


def dot(left, right, left_dim, right_dim, precision=None):
    return lax.dot_general(
        left,
        right,
        (((left_dim,), (right_dim,)), ((), ())),
        preferred_element_type=F32,
        precision=precision,
    )


def swap(value, axis, bit):
    size = lax.axis_size(axis)
    return lax.ppermute(value, axis, [(i, i ^ bit) for i in range(size)])


def gelu_parts(upper):
    cdf = 0.5 * (1.0 + lax.erf(upper * ROOT_HALF))
    slope = cdf + upper * jnp.exp(-0.5 * upper * upper) * INV_ROOT_TWO_PI
    return upper * cdf, slope


def after(value, *marks):
    return lax.optimization_barrier((value, *marks))[0]


def rows_sum(part, arrived):
    half = part.shape[0] // 2
    part, arrived = part.astype(F32), arrived.astype(F32)
    return jnp.concatenate([part[:half] + arrived[half:], part[half:] + arrived[:half]], axis=0)


def normal(rows_in):
    centred = rows_in - jnp.mean(rows_in, axis=-1, keepdims=True)
    inverse = lax.rsqrt(jnp.mean(centred * centred, axis=-1, keepdims=True) + NORM_EPS)
    return centred * inverse, inverse


def normal_back(grad, normed, inverse, gain):
    scaled = grad * gain
    inner = jnp.mean(scaled * normed, axis=-1, keepdims=True)
    return inverse * (scaled - jnp.mean(scaled, axis=-1, keepdims=True) - normed * inner)


class Arriving:
    def __init__(self, source, local, mark):
        self.local, self.shape, self.dtype, self.waited = local, local.shape, local.dtype, False
        self.copy = pltpu.make_async_copy(source, local, mark)
        self.copy.start()

    def __getitem__(self, index):
        self.settle()
        return self.local[index]

    def settle(self):
        if not self.waited:
            self.copy.wait()
            self.waited = True


class Leaving:
    def __init__(self, target, local, mark):
        self.local, self.shape, self.dtype, self.written = local, local.shape, local.dtype, 0
        self.copy = pltpu.make_async_copy(local, target, mark)

    def __setitem__(self, index, value):
        self.local[index] = value
        self.written += value.size
        if self.written == self.local.size:
            self.copy.start()

    def __getitem__(self, index):
        return self.local[index]

    def settle(self):
        assert self.written == self.local.size
        self.copy.wait()


def call(kernel, outs, args, name, flops, limit=24, scalars=None, far=(), far_outs=()):
    lead = 0 if scalars is None else 1
    inputs, results = len(args), len(outs)
    parts = {i: a[1] for i, a in enumerate(args) if isinstance(a, tuple)}
    kinds = [jax.ShapeDtypeStruct(a[2], a[0].dtype) if isinstance(a, tuple) else a for a in args]
    args = [a[0] if isinstance(a, tuple) else a for a in args]
    args = [pltpu.with_memory_space_constraint(a, pltpu.HBM) if i in far else a for i, a in enumerate(args)]
    moved_in, moved_out = [kinds[i] for i in far], [outs[i] for i in far_outs]

    def body(*refs):
        refs = list(refs)
        scratch = refs[lead + inputs + results :]
        late = []
        for spot, i in enumerate(far):
            source = refs[lead + i].at[parts[i]] if i in parts else refs[lead + i]
            refs[lead + i] = Arriving(source, scratch[spot], scratch[-1].at[spot])
            late.append(refs[lead + i])
        for spot, i in enumerate(far_outs):
            spot += len(far)
            at = lead + inputs + i
            refs[at] = Leaving(refs[at], scratch[spot], scratch[-1].at[spot])
            late.append(refs[at])
        kernel(*refs[: lead + inputs + results])
        for item in late:
            item.settle()

    near = lambda shape: pl.BlockSpec(shape, lambda n=len(shape): (0,) * n)
    elsewhere = pl.BlockSpec(memory_space=pltpu.HBM)
    specs = [elsewhere if i in far else near(a.shape) for i, a in enumerate(args)]
    out_specs = [elsewhere if i in far_outs else near(shape) for i, (shape, _) in enumerate(outs)]
    scratch = [pltpu.VMEM(a.shape, a.dtype) for a in moved_in] + [pltpu.VMEM(shape, kind) for shape, kind in moved_out]
    if scratch:
        scratch.append(pltpu.SemaphoreType.DMA((len(scratch),)))
    operands = list(args)
    if lead:
        specs = [pl.BlockSpec(memory_space=pltpu.SMEM)] + specs
        operands = [scalars] + operands
    shapes = [jax.ShapeDtypeStruct(shape, kind) for shape, kind in outs]
    made = [pltpu.HBM(shape, kind) if i in far_outs else shapes[i] for i, (shape, kind) in enumerate(outs)]
    moved = sum(a.size * a.dtype.itemsize for a in [*kinds, *shapes])
    return pl.pallas_call(
        body,
        in_specs=specs,
        out_specs=out_specs,
        out_shape=made,
        scratch_shapes=scratch,
        cost_estimate=cost(flops, moved),
        compiler_params=params(limit),
        name=name,
    )(*operands)


def join_kernel(order, flags_ref, own_ref, other_ref, q_ref, kv_ref, out_ref):
    width = q_ref.shape[1] // 2
    rows = own_ref.shape[0] // len(order)
    front = flags_ref[0] == 0
    for spot, v in enumerate(order):
        here = slice(spot * rows, (spot + 1) * rows)
        there = here if len(order) == 1 else pl.ds(pl.multiple_of((flags_ref[2] ^ v) * rows, 16), rows)
        groups = []
        for part in range(4):
            lanes = slice(part * width, (part + 1) * width)
            own, other = own_ref[here, lanes].astype(F32), other_ref[here, lanes].astype(F32)
            left, right = jnp.where(front, own, other), jnp.where(front, other, own)
            groups.append(jnp.concatenate([left, right], axis=1).astype(LOW))
        q_ref[there, :] = groups[0]
        kv_ref[there, : 2 * width] = groups[1]
        kv_ref[there, 2 * width :] = groups[2]
        out_ref[there, :] = groups[3]


def project(low, wq_ref, wkv_ref, bias_ref, q_ref, kv_ref):
    width = wq_ref.shape[1]
    q_ref[...] = (dot(low, wq_ref[...], 1, 0) + bias_ref[:, :width]).astype(LOW)
    kv_ref[...] = (dot(low, wkv_ref[...], 1, 0) + bias_ref[:, width:]).astype(LOW)


def project_kernel(x_ref, wq_ref, wkv_ref, bias_ref, q_ref, kv_ref):
    project(x_ref[...], wq_ref, wkv_ref, bias_ref, q_ref, kv_ref)


def first_norm(rows, vec_ref):
    return normal(rows)[0] * vec_ref[0:1, :] + vec_ref[2:3, :]


def second_norm(rows, vec_ref):
    return normal(rows)[0] * vec_ref[1:2, :] + vec_ref[3:4, :]


def norm_project_kernel(
    sent_ref, arrived_ref, rows_ref, vec_ref, wq_ref, wkv_ref, bias_ref, out_ref, low_ref, q_ref, kv_ref
):
    rows = rows_sum(sent_ref[...], arrived_ref[...]) + vec_ref[5:6, :] + first_norm(rows_ref[...], vec_ref)
    out_ref[...] = rows
    low = second_norm(rows, vec_ref).astype(LOW)
    low_ref[...] = low
    project(low, wq_ref, wkv_ref, bias_ref, q_ref, kv_ref)


def pick(flag, first, second):
    return jnp.where(flag, first.astype(F32), second.astype(F32)).astype(LOW)


def attend_kernel(flags_ref, q_ref, k0_ref, k1_ref, k2_ref, k3_ref, place_ref, bound_ref, wo_ref,
                  keep_ref, give_ref, logsum_ref, sent_ref):
    rows, width = q_ref.shape
    pieces = (k0_ref, k1_ref, k2_ref, k3_ref)
    lanes = lax.broadcasted_iota(jnp.int32, (1, 128), 1)
    low, high = bound_ref[:, :1], bound_ref[:, 1:2]
    masks = []
    for index, ref in enumerate(pieces):
        place = place_ref[:, index * ref.shape[0] : (index + 1) * ref.shape[0]]
        masks.append(jnp.where((place >= low) & (place < high), 0.0, MASKED))
    logsums = jnp.zeros((rows, 128), F32)
    tiles = []
    for tile in range(width // 128):
        cols = slice(tile * 128, tile * 128 + 128)
        other = slice(width + tile * 128, width + tile * 128 + 128)
        query = q_ref[:, cols]
        out = None
        for side in range(2):
            here = (lanes >= side * HD) & (lanes < side * HD + HD)
            lone = jnp.where(here, query.astype(F32) * HD ** (-0.5), 0.0).astype(LOW)
            scores = [dot(lone, ref[:, cols], 1, 1) + mask for ref, mask in zip(pieces, masks)]
            highest = jnp.max(scores[0], axis=-1, keepdims=True)
            for score in scores[1:]:
                highest = jnp.maximum(highest, jnp.max(score, axis=-1, keepdims=True))
            powers = [jnp.exp(score - highest) for score in scores]
            total = sum(jnp.sum(power, axis=-1, keepdims=True) for power in powers)
            inverse = 1.0 / total
            head = sum(dot((power * inverse).astype(LOW), ref[:, other], 1, 0) for power, ref in zip(powers, pieces))
            head = jnp.where(here, head, 0.0)
            out = head if out is None else out + head
            logsums = jnp.where(lanes == 2 * tile + side, highest + jnp.log(total), logsums)
        tiles.append(out.astype(LOW))
    logsum_ref[...] = logsums
    mixed = jnp.concatenate(tiles, axis=1)
    half = width // 2
    keep_ref[...] = pick(flags_ref[0] == 0, mixed[:, :half], mixed[:, half:])
    give_ref[...] = pick(flags_ref[0] == 0, mixed[:, half:], mixed[:, :half])
    sent_ref[...] = dot(mixed, wo_ref[...], 1, 1).astype(LOW)


def attend_all_kernel(flags_ref, kinds, *refs):
    pieces, place_ref, wo_ref, rest = refs[:4], refs[4], refs[5], refs[6:]
    chunks = len(rest) // (kinds + 2)
    for j in range(chunks):
        outs = rest[2 * chunks + j * kinds : 2 * chunks + (j + 1) * kinds]
        attend_kernel(flags_ref, rest[j], *pieces, place_ref, rest[chunks + j], wo_ref, *outs)


def attend_back_kernel(first, *refs):
    rows_ref, wo_ref, q_ref, k0_ref, k1_ref, k2_ref, k3_ref, logsum_ref, resid_ref = refs[:9]
    sent_ref, arrived_ref, vec_ref, place_ref, bound_ref = refs[9:14]
    held_refs = () if first else refs[14:18]
    rest_ref, low_ref, norm_sums_ref, dq_ref, *sums_refs = refs[14 + len(held_refs) :]
    grad = rows_sum(sent_ref[...], arrived_ref[...]) + resid_ref[...]
    normed, inverse = normal(rows_ref[...])
    back = normal_back(grad, normed, inverse, vec_ref[0:1, :])
    rest_ref[...] = back
    put_sums(norm_sums_ref, [grad * normed, grad, back], 3)
    low_back = back.astype(LOW)
    low_ref[...] = low_back
    mixed_grad = dot(low_back, wo_ref[...], 1, 0).astype(LOW).astype(F32)
    rows, width = q_ref.shape
    pieces = (k0_ref, k1_ref, k2_ref, k3_ref)
    lanes = lax.broadcasted_iota(jnp.int32, (1, 128), 1)
    low, high = bound_ref[:, :1], bound_ref[:, 1:2]
    scale = HD ** (-0.5)
    masks = []
    for index, ref in enumerate(pieces):
        place = place_ref[:, index * ref.shape[0] : (index + 1) * ref.shape[0]]
        masks.append(jnp.where((place >= low) & (place < high), 0.0, MASKED))
    for tile in range(width // 128):
        cols = slice(tile * 128, tile * 128 + 128)
        other = slice(width + tile * 128, width + tile * 128 + 128)
        query, grad = q_ref[:, cols].astype(F32), mixed_grad[:, cols]
        dq = None
        dk, dv = [None] * 4, [None] * 4
        for side in range(2):
            here = (lanes >= side * HD) & (lanes < side * HD + HD)
            lone = jnp.where(here, query * scale, 0.0).astype(LOW)
            lone_grad = jnp.where(here, grad, 0.0).astype(LOW)
            logsum = jnp.sum(jnp.where(lanes == 2 * tile + side, logsum_ref[...], 0.0), axis=-1, keepdims=True)
            probs, prob_grads = [], []
            inner = None
            for ref, mask in zip(pieces, masks):
                prob = jnp.exp(dot(lone, ref[:, cols], 1, 1) + mask - logsum)
                prob_grad = dot(lone_grad, ref[:, other], 1, 1)
                probs.append(prob)
                prob_grads.append(prob_grad)
                piece = jnp.sum(prob * prob_grad, axis=-1, keepdims=True)
                inner = piece if inner is None else inner + piece
            for index, ref in enumerate(pieces):
                score = (probs[index] * (prob_grads[index] - inner)).astype(LOW)
                back = dot(score, ref[:, cols], 1, 0)
                back = jnp.where(here, back * scale, 0.0)
                dq = back if dq is None else dq + back
                key = dot(score, lone, 0, 0)
                value = dot(probs[index].astype(LOW), lone_grad, 0, 0)
                dk[index] = key if dk[index] is None else dk[index] + key
                dv[index] = value if dv[index] is None else dv[index] + value
        dq_ref[:, cols] = dq.astype(LOW)
        for index in range(4):
            key, value = dk[index], dv[index]
            if held_refs:
                key = key + held_refs[index][:, cols]
                value = value + held_refs[index][:, other]
            sums_refs[index][:, cols] = key.astype(sums_refs[index].dtype)
            sums_refs[index][:, other] = value.astype(sums_refs[index].dtype)


def feed_kernel(is_first, sent_ref, arrived_ref, resid_ref, vec_ref, before_ref, feed0_ref, feed1_ref, bias_ref,
                rows_ref, give_ref, act_ref, slope_ref, out_ref):
    resid = resid_ref[...].astype(F32) if is_first else second_norm(resid_ref[...], before_ref)
    rows = rows_sum(sent_ref[...], arrived_ref[...]) + vec_ref[4:5, :] + resid
    rows_ref[...] = rows
    low = first_norm(rows, vec_ref).astype(LOW)
    cols = low.shape[1]
    units = feed0_ref.shape[0]
    top = feed0_ref.shape[1] - units
    base = top - units
    give_ref[:, :cols] = low
    act, slope = gelu_parts(dot(low, feed0_ref[:, base:top], 1, 0) + bias_ref[0:1, :])
    act = act.astype(LOW)
    act_ref[...] = act
    slope_ref[:, :units] = slope.astype(LOW)
    part = dot(act, feed0_ref[:, top:], 1, 1)
    act, slope = gelu_parts(dot(low, feed1_ref[:, base:top], 1, 0) + bias_ref[1:2, :])
    act = act.astype(LOW)
    give_ref[:, cols:] = act
    slope_ref[:, units:] = slope.astype(LOW)
    out_ref[...] = (part + dot(act, feed1_ref[:, top:], 1, 1)).astype(LOW)


def put_sums(sums_ref, lists, start):
    half = lists[0].shape[0] // 2
    sums_ref[...] = jnp.zeros(sums_ref.shape, F32)
    for index, rows in enumerate(lists):
        sums_ref[start + index : start + index + 1, :] = jnp.sum(rows[:half], axis=0, keepdims=True)


def back_feed(grad, normed, inverse, gain, slope_ref, feed0_ref, feed1_ref, rest_ref, give_ref, keep_ref, out_ref, sums_ref):
    back = normal_back(grad, normed, inverse, gain)
    rest_ref[...] = back
    put_sums(sums_ref, [grad * normed, grad, back], 0)
    low = back.astype(LOW)
    cols = low.shape[1]
    units = feed0_ref.shape[0]
    top = feed0_ref.shape[1] - units
    base = top - units
    give_ref[:, :cols] = low
    upper = (dot(low, feed0_ref[:, top:], 1, 0) * slope_ref[:, :units].astype(F32)).astype(LOW)
    keep_ref[...] = upper
    part = dot(upper, feed0_ref[:, base:top], 1, 1)
    upper = (dot(low, feed1_ref[:, top:], 1, 0) * slope_ref[:, units:].astype(F32)).astype(LOW)
    give_ref[:, cols:] = upper
    out_ref[...] = (part + dot(upper, feed1_ref[:, base:top], 1, 1)).astype(LOW)


def top_kernel(flags_ref, sent_ref, arrived_ref, rows_ref, grad_ref, before_rows_ref, before_ref, vec_ref, slope_ref,
               feed0_ref, feed1_ref, y_ref, rest_ref, give_ref, keep_ref, out_ref, sums_ref):
    rows = rows_sum(sent_ref[...], arrived_ref[...]) + vec_ref[5:6, :] + first_norm(rows_ref[...], vec_ref)
    normed, inverse = normal(rows)
    half = normed.shape[0] // 2
    y = normed[:half] * vec_ref[1:2, :] + vec_ref[3:4, :]
    on = flags_ref[1] > 0
    y_ref[...] = jnp.where(on, y, second_norm(before_rows_ref[:half, :], before_ref))
    grad = jnp.where(on, grad_ref[...].astype(F32), 0.0)
    back_feed(grad, normed, inverse, vec_ref[1:2, :], slope_ref, feed0_ref, feed1_ref,
              rest_ref, give_ref, keep_ref, out_ref, sums_ref)


def under_kernel(flags_ref, sent_ref, arrived_ref, resid_ref, grad_ref, rows_ref, vec_ref, slope_ref,
                 feed0_ref, feed1_ref, rest_ref, give_ref, keep_ref, out_ref, sums_ref):
    grad = rows_sum(sent_ref[...], arrived_ref[...]) + resid_ref[...]
    grad = jnp.where(flags_ref[1] > 0, grad, grad_ref[...].astype(F32))
    normed, inverse = normal(rows_ref[...])
    back_feed(grad, normed, inverse, vec_ref[1:2, :], slope_ref, feed0_ref, feed1_ref,
              rest_ref, give_ref, keep_ref, out_ref, sums_ref)


def back_project_kernel(flags_ref, dq_ref, own_ref, arrived_ref, wq_ref, wkv_ref, keep_ref, give_ref, sent_ref):
    dq = dq_ref[...]
    dkv = (own_ref[...] + arrived_ref[...].astype(F32)).astype(LOW)
    sent_ref[...] = (dot(dq, wq_ref[...], 1, 1) + dot(dkv, wkv_ref[...], 1, 1)).astype(LOW)
    half = dq.shape[1] // 2
    groups = (dq, dkv[:, : 2 * half], dkv[:, 2 * half :])
    front = flags_ref[0] == 0
    keep_ref[...] = jnp.concatenate([pick(front, g[:, :half], g[:, half:]) for g in groups], axis=1)
    give_ref[...] = jnp.concatenate([pick(front, g[:, half:], g[:, :half]) for g in groups], axis=1)

def split(value):
    high = value.astype(LOW)
    return high, (value - high.astype(F32)).astype(LOW)


def split_dot(small, large, small_dim, large_dim):
    high, rest = split(large)
    lead, tail = split(small)
    rows = small.shape[0]
    both = dot(jnp.concatenate([lead, tail], axis=0), high, small_dim, large_dim)
    return both[:rows] + both[rows:] + dot(lead, rest, small_dim, large_dim)


def dot_chunks(lefts, rights):
    total = None
    for left, right in zip(lefts, rights):
        part = dot(left[...], right[...], 0, 0)
        total = part if total is None else total + part
    return total


def rows_total_kernel(chunks, *refs):
    lefts, rights = refs[:chunks], refs[chunks : 2 * chunks]
    error_ref, start_ref, total_ref, first_ref, bias_ref = refs[2 * chunks :]
    total = dot_chunks(lefts, rights) + error_ref[...]
    total_ref[...] = total
    first_ref[...] = split_dot(start_ref[...], total, 1, 1)

    @pl.when(pl.program_id(0) == 0)
    def _():
        bias = sum(jnp.sum(ref[...].astype(F32), axis=0, keepdims=True) for ref in rights)
        bias_ref[...] = jnp.concatenate([bias, jnp.zeros((7, bias.shape[1]), F32)], axis=0)


def params(limit, **more):
    return pltpu.CompilerParams(vmem_limit_bytes=limit << 20, **more)


def cost(flops, moved):
    return pl.CostEstimate(flops=int(flops), bytes_accessed=int(moved), transcendentals=0)


def rows_total(lefts, rights, errors, starts, layer):
    rows, cols = errors.shape[-2:]
    tokens = lefts[0][0].shape[0]
    rank = starts.shape[1]
    step = 256
    chunks = len(lefts)
    return pl.pallas_call(
        lambda *refs: rows_total_kernel(chunks, *refs),
        grid=(rows // step,),
        in_specs=[pl.BlockSpec((tokens, step), lambda i, at=at: (0, i + at * (rows // step))) for _, at in lefts]
        + [pl.BlockSpec((tokens, cols), lambda i, at=at: (0, at)) for _, at in rights]
        + [
            pl.BlockSpec((None, None, step, cols), lambda i: (0, layer, i, 0)),
            pl.BlockSpec((None, rank, cols), lambda i: (layer, 0, 0)),
        ],
        out_specs=[
            pl.BlockSpec((step, cols), lambda i: (i, 0)),
            pl.BlockSpec((rank, step), lambda i: (0, i)),
            pl.BlockSpec((rank, cols), lambda i: (0, 0)),
        ],
        out_shape=[
            jax.ShapeDtypeStruct((rows, cols), F32),
            jax.ShapeDtypeStruct((rank, rows), F32),
            jax.ShapeDtypeStruct((rank, cols), F32),
        ],
        cost_estimate=cost(2 * chunks * tokens * rows * cols, 8 * rows * cols + 4 * chunks * tokens * rows),
        compiler_params=params(24),
        name="rows_total",
    )(*[array for array, _ in lefts], *[array for array, _ in rights], errors, starts)


def mixed_total_kernel(chunks, *refs):
    proj_refs, whole_refs = refs[:chunks], refs[chunks : 2 * chunks]
    attended_refs, piece_refs = refs[2 * chunks : 3 * chunks], refs[3 * chunks : 4 * chunks]
    e_proj_ref, e_back_ref, s_proj_ref, s_back_ref, total_ref, first_ref = refs[4 * chunks :]
    width = e_back_ref.shape[0]
    grads = dot_chunks(proj_refs, whole_refs)
    for member in range(3):
        rows = slice(member * width, (member + 1) * width)
        total = grads[rows] + e_proj_ref[member]
        total_ref[rows, :] = total
        first_ref[8 * member : 8 * member + 8, :] = split_dot(s_proj_ref[member], total, 1, 0)
    total = dot_chunks(attended_refs, piece_refs) + e_back_ref[...]
    total_ref[3 * width :, :] = total
    first_ref[24:, :] = jnp.zeros((8, total.shape[1]), F32)
    first_ref[24:, :width] = split_dot(s_back_ref[...], total, 1, 1)
    sums = sum(jnp.sum(ref[...].astype(F32), axis=0, keepdims=True) for ref in proj_refs)
    first_ref[24:25, 256 : 256 + width] = sums[:, :width]
    first_ref[24:25, 512 : 512 + width] = sums[:, 2 * width :]


def mixed_total(proj_low, whole_in, attended, piece, e_proj, e_back, s_proj, s_back, layer):
    tokens, width = attended[0].shape
    cols = whole_in[0].shape[1]
    rank = s_back.shape[1]
    chunks = len(attended)
    args = [*proj_low, *whole_in, *attended, *piece, (e_proj, (0, layer), e_proj.shape[2:]), (e_back, (0, layer), e_back.shape[2:]), s_proj[layer], s_back[layer]]
    return call(
        lambda *refs: mixed_total_kernel(chunks, *refs),
        [[(4 * width, cols), F32], [(4 * rank, cols), F32]],
        args, "mixed_total", 2 * chunks * tokens * 4 * width * cols, 24, None, range(4 * chunks + 2),
    )


def ortho_rows(factor):
    rank = factor.shape[0]
    index = lax.broadcasted_iota(jnp.int32, (rank, 1), 0)
    for row in range(rank):
        vector = factor[row : row + 1, :]
        inner = jnp.sum(factor * vector, axis=1, keepdims=True)
        scale = lax.rsqrt(inner[row : row + 1] + ORTHO_EPS)
        vector = vector * scale
        factor = jnp.where(
            index < row, factor, jnp.where(index == row, vector, factor - vector * (inner * scale))
        )
    return factor


def feed_second_kernel(sums_ref, up_ref, down_ref, base_ref, second_ref):
    for member, total_ref in enumerate((up_ref, down_ref)):
        rows = slice(8 * member, 8 * member + 8)
        base = ortho_rows(sums_ref[rows, :])
        base_ref[rows, :] = base
        second_ref[rows, :] = split_dot(base, total_ref[...], 1, 0)


def feed_second(sums, m_up, m_down):
    cols = m_up.shape[1]
    return pl.pallas_call(
        feed_second_kernel,
        out_shape=[jax.ShapeDtypeStruct((16, cols), F32)] * 2,
        cost_estimate=cost(96 * m_up.size, 8 * m_up.size),
        compiler_params=params(24),
        name="feed_second",
    )(sums, m_up, m_down)


def mixed_second_kernel(width, sums_ref, total_ref, base_ref, second_ref):
    second_ref[...] = jnp.zeros(second_ref.shape, F32)
    for member in range(3):
        rows = slice(8 * member, 8 * member + 8)
        base = ortho_rows(sums_ref[rows, :])
        base_ref[rows, :] = base
        second_ref[:8, 256 * member : 256 * member + width] = split_dot(
            base, total_ref[member * width : (member + 1) * width, :], 1, 1
        )
    base = ortho_rows(sums_ref[24:32, :width])
    base_ref[24:32, :width] = base
    second_ref[8:, :] = split_dot(base, total_ref[3 * width :, :], 1, 0)


def mixed_second(sums, m_mixed, width):
    cols = m_mixed.shape[1]
    return pl.pallas_call(
        lambda *refs: mixed_second_kernel(width, *refs),
        out_shape=[jax.ShapeDtypeStruct((32, cols), F32), jax.ShapeDtypeStruct((16, cols), F32)],
        cost_estimate=cost(48 * m_mixed.size, 4 * m_mixed.size),
        compiler_params=params(16),
        name="mixed_second",
    )(sums, m_mixed)


def low_rank(base, second):
    b_high, b_rest = split(base)
    s_high, s_rest = split(second)
    left = jnp.concatenate([b_high, b_rest, b_high], axis=0)
    right = jnp.concatenate([s_high, s_high, s_rest], axis=0)
    return dot(left, right, 0, 0)


def feed_error_kernel(layer, replicas, base_ref, second_ref, up_ref, down_ref, *refs):
    up_out, down_out = refs[-2:]
    seconds = second_ref[...] * (1.0 / replicas)
    up_out[...] = up_ref[...] - low_rank(base_ref[:8, :], seconds[:8])
    down_out[...] = down_ref[...] - low_rank(base_ref[8:16, :], seconds[8:16])


def feed_error(base, second, m_up, m_down, layer, replicas, held):
    rows, cols = m_up.shape
    rank2 = base.shape[0]
    step = 256
    shape = jax.ShapeDtypeStruct((1, 2, rows, cols), F32)
    out_spec = pl.BlockSpec((None, None, step, cols), lambda i: (0, layer, i, 0))
    extra = {} if held is None else {"input_output_aliases": {4: 0, 5: 1}}
    return pl.pallas_call(
        lambda *refs: feed_error_kernel(layer, replicas, *refs),
        grid=(rows // step,),
        in_specs=[
            pl.BlockSpec((rank2, step), lambda i: (0, i)),
            pl.BlockSpec((rank2, cols), lambda i: (0, 0)),
            pl.BlockSpec((step, cols), lambda i: (i, 0)),
            pl.BlockSpec((step, cols), lambda i: (i, 0)),
        ] + ([] if held is None else [pl.BlockSpec(memory_space=pl.ANY)] * 2),
        out_specs=[out_spec, out_spec],
        out_shape=[shape, shape],
        cost_estimate=cost(100 * m_up.size, 16 * m_up.size),
        compiler_params=params(16),
        name="feed_error",
        **extra,
    )(base, second, m_up, m_down, *(() if held is None else held))


def mixed_error_kernel(replicas, base_ref, second_ref, total_ref, *refs):
    proj_out, back_out = refs[-2:]
    width = back_out.shape[0]
    seconds = second_ref[...] * (1.0 / replicas)
    for member in range(3):
        approx = low_rank(seconds[:8, 256 * member : 256 * member + width], base_ref[8 * member : 8 * member + 8, :])
        proj_out[member] = total_ref[member * width : (member + 1) * width, :] - approx
    back_out[...] = total_ref[3 * width :, :] - low_rank(base_ref[24:32, :width], seconds[8:])


def mixed_error(base, second, m_mixed, layer, replicas, held):
    rows, cols = m_mixed.shape
    width = rows // 4
    extra = {} if held is None else {"input_output_aliases": {3: 0, 4: 1}}
    return pl.pallas_call(
        lambda *refs: mixed_error_kernel(replicas, *refs),
        grid=(1,),
        in_specs=[
            pl.BlockSpec(base.shape, lambda i: (0, 0)),
            pl.BlockSpec(second.shape, lambda i: (0, 0)),
            pl.BlockSpec((rows, cols), lambda i: (0, 0)),
        ] + ([] if held is None else [pl.BlockSpec(memory_space=pl.ANY)] * 2),
        out_specs=[
            pl.BlockSpec((None, None, 3, width, cols), lambda i: (0, layer, 0, 0, 0)),
            pl.BlockSpec((None, None, width, cols), lambda i: (0, layer, 0, 0)),
        ],
        out_shape=[
            jax.ShapeDtypeStruct((1, 2, 3, width, cols), F32), jax.ShapeDtypeStruct((1, 2, width, cols), F32)
        ],
        cost_estimate=cost(50 * m_mixed.size, 8 * m_mixed.size),
        compiler_params=params(24),
        name="mixed_error",
        **extra,
    )(base, second, m_mixed, *(() if held is None else held))


def flip(value):
    return jnp.swapaxes(value, -1, -2)


def per_device(
    x_in, out_grad, doc_lengths, keep_layer, w_qkv, w_o, w_in, w_out, b_qv, b_in, ln_gain, shifts,
    m_qkv, m_o, m_in, m_out, m_qv, m_bin, m_gain, m_shift, e_qkv, e_o, e_in, e_out, q_qkv, q_o, q_in, q_out,
):
    own_rows, cols = x_in.shape
    replicas = lax.axis_size("dp")
    index = lax.axis_index("dp")
    place = lax.axis_index("mp")
    width = w_o.shape[1]
    front = lax.rem(place, 2) == 0
    flags = jnp.stack([lax.rem(place, 2), keep_layer[0], index]).astype(jnp.int32)
    chunks = 2
    step = own_rows // chunks
    size = 2 * step
    pair = range(chunks)

    def core(value):
        return swap(value, "mp", 1)

    def chip(value):
        return swap(value, "mp", 2)

    def gather(piece):
        return lax.all_gather(piece, "dp", axis=0, tiled=True)

    def join(own, other, axis):
        return jnp.where(
            front, jnp.concatenate([own, other], axis=axis), jnp.concatenate([other, own], axis=axis)
        )

    def mixed_piece(layer):
        return jnp.concatenate(
            [w_qkv[layer, 0], w_qkv[layer, 1], w_qkv[layer, 2], flip(w_o[layer])], axis=1
        ).astype(LOW)

    def feed_piece(layer):
        return jnp.concatenate([w_in[layer], flip(w_out[layer])], axis=1).astype(LOW)

    def by_chunk(rows, arrived):
        return [
            jnp.concatenate([rows[j * step : (j + 1) * step], arrived[j * step : (j + 1) * step]], axis=0) for j in pair
        ]

    small = jnp.concatenate([b_qv.reshape(-1), b_in.reshape(-1)]).reshape(-1, 128)
    small = core(small).reshape(-1)
    other_qv = small[: b_qv.size].reshape(b_qv.shape)
    other_in = small[b_qv.size :].reshape(b_in.shape)

    ends = jnp.sum(
        jnp.where(
            jnp.arange(doc_lengths.shape[1])[:, None] <= jnp.arange(doc_lengths.shape[1])[None, :],
            doc_lengths[0][:, None], 0,
        ),
        axis=0,
    )

    def places_of(device, j):
        steps = jnp.arange(step, dtype=jnp.int32) + j * step
        return jnp.concatenate([device * own_rows + steps, (device ^ 2) * own_rows + steps])

    mine = [places_of(place, j) for j in pair]
    all_places = jnp.concatenate(mine + [places_of(place ^ 1, j) for j in pair])[None, :]

    def bounds_of(places):
        passed = places[:, None] >= ends[None, :]
        low = jnp.max(jnp.where(passed, ends[None, :], 0), axis=1)
        high = jnp.min(jnp.where(passed, 1 << 30, ends[None, :]), axis=1)
        return jnp.stack([low, high], axis=1)

    bounds = [bounds_of(places) for places in mine]

    vecs, feeds, proj_bias, feed_bias = [], [], [], []
    for layer in range(2):
        gain, shift = ln_gain[layer], shifts[layer]
        vecs.append(
            jnp.concatenate(
                [gain, shift[1:2], shift[3:4], shift[0:1], shift[2:3], jnp.zeros((2, cols), F32)], axis=0
            )
        )
        proj_bias.append(
            jnp.concatenate(
                [
                    join(b_qv[layer, 0], other_qv[layer, 0], 0),
                    jnp.zeros((2 * width,), F32),
                    join(b_qv[layer, 1], other_qv[layer, 1], 0),
                ]
            )[None]
        )
        feed_bias.append(jnp.stack([b_in[layer], other_in[layer]]))

    set_in = by_chunk(x_in, chip(x_in))
    order = [0]
    bits = [4, 2, 1] if replicas == 8 else []
    for bit in bits:
        order = order + [v ^ bit for v in order]
    if not bits:
        order = order[:1]

    def doubled(piece, bit):
        return jnp.concatenate([piece, swap(piece, "dp", bit)], axis=0)

    feed_whole = jnp.concatenate([mixed_piece(1), feed_piece(0)], axis=1)
    whole_mixed = mixed_piece(0)
    if bits:
        feed_whole = gather(feed_whole)
        set_grad = by_chunk(out_grad, chip(after(out_grad, *set_in)))
        whole_mixed = doubled(doubled(whole_mixed, 4), 2)
        whole_mixed, all_places, flags, *rest = lax.optimization_barrier(
            (whole_mixed, all_places, flags, *bounds, *vecs, *proj_bias, *feed_bias, *set_in, *set_grad)
        )
        bounds, vecs, proj_bias, feed_bias = rest[:2], rest[2:4], rest[4:6], rest[6:8]
        set_in, set_grad = rest[8:10], rest[10:12]
        whole_mixed = doubled(whole_mixed, 1)
    else:
        set_grad = by_chunk(out_grad, chip(out_grad))
        whole_mixed = gather(whole_mixed)
        feed_whole = gather(feed_whole)
    feed_late, *set_in = lax.optimization_barrier((feed_piece(1), *set_in))
    feed_late = gather(feed_late)
    whole_other = [core(rows) for rows in set_in]

    full = [(size, cols), F32]
    full_low = [(size, cols), LOW]
    thin = [(size, 128), F32]
    half_low = [(size, 2 * width), LOW]
    one_low = [(size, width), LOW]
    kv_low = [(size, 4 * width), LOW]
    units = cols

    def mixed_weights(own, other, order):
        return call(
            lambda *refs: join_kernel(order, *refs), [[(cols, 2 * width), LOW], [(cols, 4 * width), LOW], [(cols, 2 * width), LOW]],
            [(own, (slice(None), pl.ds(0, cols)), (cols, cols)), (other, (slice(None), pl.ds(0, cols)), (cols, cols))],
            "join", 0, 16, flags, (0, 1), (0, 1, 2),
        )

    def attention(layer, q, kv):
        pieces = kv + [core(part) for part in kv]
        kinds = [one_low, one_low, thin, full_low]
        outs = call(
            lambda flags_ref, *refs: attend_all_kernel(flags_ref, len(kinds), *refs), kinds * chunks,
            [*pieces, all_places, wo[layer], *q, *bounds], "attend",
            chunks * (2 * size * (4 * size) * 4 * width + 2 * size * 2 * width * cols), 20, flags, (6, 7, 0, 1, 2, 3, 5), (0, 1, 2, 4, 5, 6),
        )
        return pieces, [outs[j * len(kinds) : (j + 1) * len(kinds)] for j in pair]

    def feed_all(layer, outs, resid):
        return [
            call(
                lambda *refs: feed_kernel(layer == 0, *refs),
                [full, [(size, cols + units), LOW], [(size, units), LOW], [(size, 2 * units), LOW], full_low],
                [outs[j][3], chip(outs[j][3]), resid[j], vecs[layer], vecs[0], *feeds[layer], feed_bias[layer]],
                "feed", 8 * size * cols * units, 26, None, (2, 5, 6), (0, 1, 2, 3),
            )
            for j in pair
        ]

    e_proj, s_proj = flip(e_qkv), flip(q_qkv)
    e_proj, e_back, e_up, e_down = (
        pltpu.with_memory_space_constraint(value, pltpu.HBM) for value in (e_proj, e_o, e_in, e_out)
    )
    s_back, s_up, s_down = flip(q_o), flip(q_in), flip(q_out)

    def feed_up(layer, feed_out, tails, start):
        give_up = [out[1] for out in feed_out]
        give_down = [out[1] for out in tails]
        return rows_total(
            [(rows, 0) for rows in give_up + [core(rows) for rows in give_up]],
            [(out[2], 0) for out in tails] + [(core(rows), 1) for rows in give_down], e_up, start, layer,
        )

    def feed_down(layer, feed_out, tails, start):
        give_up = [out[1] for out in feed_out]
        give_down = [out[1] for out in tails]
        return rows_total(
            [(out[2], 0) for out in feed_out] + [(core(rows), 1) for rows in give_up],
            [(rows, 0) for rows in give_down + [core(rows) for rows in give_down]], e_down, start, layer,
        )

    def mixed_first(layer, low, back, mixed, norm, start):
        return mixed_total(
            [out[0] for out in back] + [core(out[1]) for out in back],
            low,
            [out[0] for out in mixed] + [core(out[1]) for out in mixed],
            [out[1] for out in norm] + [core(out[1]) for out in norm],
            e_proj, e_back, s_proj, start, layer,
        )

    def total_over(value, axis):
        bit = 1
        while bit < lax.axis_size(axis):
            value = value + swap(value, axis, bit)
            bit = 2 * bit
        return value

    class Total:
        def __init__(self, value):
            self.value, self.bit = value, 1

        def step(self, *marks):
            if self.bit < replicas:
                self.value = self.value + after(swap(self.value, "dp", self.bit), *marks)
                self.bit = 2 * self.bit

        def rest(self):
            while self.bit < replicas:
                self.value = self.value + swap(self.value, "dp", self.bit)
                self.bit = 2 * self.bit
            return self.value

    def norm_sums(tails, norm):
        return sum(out[4] for out in tails) + sum(out[3] for out in norm)

    wq, wkv, wo = ([part] for part in mixed_weights(whole_mixed, core(whole_mixed), order))
    first = [
        call(
            project_kernel, [half_low, kv_low], [set_in[j], wq[0], wkv[0], proj_bias[0]],
            "project", 2 * size * cols * 6 * width, 10, None, (1, 2), (0, 1),
        )
        for j in pair
    ]
    q_one = [out[0] for out in first]
    pieces_one, mixed_out_one = attention(0, q_one, [out[1] for out in first])
    feed_whole = after(feed_whole, mixed_out_one[0][3])
    other_whole = core(feed_whole)
    spot = ((slice(None), pl.ds(cols, 2 * cols)), (cols, 2 * cols))
    feeds.append(((feed_whole, *spot), (other_whole, *spot)))
    feed_out_one = feed_all(0, mixed_out_one, set_in)
    own_late = after(feed_whole, feed_out_one[1][4])
    for held, part in zip((wq, wkv, wo), mixed_weights(own_late, other_whole, [0])):
        held.append(part)
    second = [
        call(
            norm_project_kernel, [full, full_low, half_low, kv_low],
            [feed_out_one[j][4], chip(feed_out_one[j][4]), feed_out_one[j][0], vecs[0], wq[1], wkv[1], proj_bias[1]],
            "norm_project", 2 * size * cols * 6 * width, 12, None, (2, 4, 5), (0, 1, 2, 3),
        )
        for j in pair
    ]
    q_two = [out[2] for out in second]
    pieces_two, mixed_out_two = attention(1, q_two, [out[3] for out in second])
    feed_late = after(feed_late, mixed_out_two[1][3])
    other_late = core(feed_late)
    feeds.append((feed_late, other_late))
    feed_out_two = feed_all(1, mixed_out_two, [out[0] for out in second])

    wide_outs = [full, [(size, cols + units), LOW], [(size, units), LOW], full_low, [(8, cols), F32]]
    top = [
        call(
            top_kernel, [[(step, cols), F32]] + wide_outs,
            [
                feed_out_two[j][4], chip(feed_out_two[j][4]), feed_out_two[j][0], set_grad[j], second[j][0], vecs[0],
                vecs[1], feed_out_two[j][3], *feeds[1],
            ],
            "top", 8 * size * cols * units, 28, flags, (2, 3, 4, 8, 9, 7), (0, 1, 2, 3),
        )
        for j in pair
    ]
    output = jnp.concatenate([out[0] for out in top], axis=0)

    def attention_back(layer, outs, feed_out, q, pieces, mixed, vec, between, ending):
        held, dqs, norms = [], [], []
        for j in pair:
            kinds = [full] * 4 if j + 1 < chunks else [full, full, full_low, full_low]
            rest, low, sums, dq, *held = call(
                lambda *refs, j=j: attend_back_kernel(j == 0, *refs),
                [full, full_low, [(8, cols), F32], half_low] + kinds,
                [
                    feed_out[j][0], wo[layer], q[j], *pieces, mixed[j][2], outs[j][0],
                    outs[j][3], chip(outs[j][3]), vec, all_places, bounds[j], *held,
                ],
                "attend_back", 5 * size * (4 * size) * 4 * width, 28, None, (8, 0, 1, 2, 3, 4, 5, 6, 7), (0, 1, 3) if j + 1 < chunks else (0, 1, 3, 4, 5),
            )
            dqs.append(dq)
            norms.append((rest, low, None, sums))
            if j == 0:
                vec = between(vec, sums)
        back_flags = ending(flags, sums)
        return norms, [
            call(
                back_project_kernel, [[(size, 3 * width), LOW], [(size, 3 * width), LOW], full_low],
                [dqs[j], held[j], core(held[2 + j]), wq[layer], wkv[layer]], "back_project",
                2 * size * cols * 6 * width, 16, back_flags, (0, 3, 1, 4), (0, 1),
            )
            for j in pair
        ]

    top_tail = [out[1:] for out in top]
    feed_two_up = feed_up(1, feed_out_two, top_tail, after(s_up, top[1][5]))
    norm_two, back_two = attention_back(
        1, top_tail, feed_out_two, q_two, pieces_two, mixed_out_two, after(vecs[1], feed_two_up[1]),
        lambda vec, sums: vec, lambda flags, sums: flags,
    )
    sent = back_two[1][2]
    feed_two_down = feed_down(1, feed_out_two, top_tail, after(s_down, sent))
    low_two = [out[1] for out in second]
    mixed_two, send_mixed_two = mixed_first(
        1, low_two + [core(rows) for rows in low_two], back_two, mixed_out_two, norm_two, after(s_back, sent)
    )
    total_two = Total(jnp.concatenate([feed_two_up[1], feed_two_down[1], feed_two_up[2], send_mixed_two], axis=0))
    under, under_flags = [], after(flags, feed_two_down[1], send_mixed_two)
    for j in pair:
        under.append(
            call(
                under_kernel, wide_outs,
                [
                    back_two[j][2], chip(back_two[j][2]), norm_two[j][0], set_grad[j], second[j][0],
                    vecs[0], feed_out_one[j][3], *feeds[0],
                ],
                "under", 8 * size * cols * units, 28, under_flags, (2, 3, 4, 7, 8, 6), (0, 1, 2),
            )
        )
    feed_one_up = feed_up(0, feed_out_one, under, after(s_up, under[1][4]))
    feed_one_down = feed_down(0, feed_out_one, under, after(s_down, under[1][4]))
    m_feed_one, m_feed_two = (feed_one_up[0], feed_one_down[0]), (feed_two_up[0], feed_two_down[0])

    total_two.step(feed_one_up[1], feed_one_down[1])

    def between(vec, sums):
        total_two.step(sums)
        return after(vec, total_two.value)

    def ending(flags, sums):
        return after(flags, total_two.value)

    norm_one, back_one = attention_back(
        0, under, feed_out_one, q_one, pieces_one, mixed_out_one,
        after(vecs[0], feed_one_up[1], feed_one_down[1]), between, ending,
    )
    last_flights = [chip(out[2][step:]) for out in back_one]

    sents = [out[2] for out in back_one]
    mixed_one, send_mixed_one = mixed_first(
        0, set_in + whole_other, back_one, mixed_out_one, norm_one, s_back
    )
    total_one = jnp.concatenate([feed_one_up[1], feed_one_down[1], feed_one_up[2], send_mixed_one], axis=0)
    sums_one = total_over(total_one, "dp")
    sums_feed_one, sums_mixed_one = sums_one[:24], sums_one[24:]
    total_two.step(send_mixed_one)
    sums_two = after(total_two.rest(), send_mixed_one)
    base_feed_two, second_feed_two = feed_second(sums_two[:24], *m_feed_two)
    base_mixed_two, second_mixed_two = mixed_second(sums_two[24:], mixed_two, width)
    last_two = Total(jnp.concatenate([second_feed_two, second_mixed_two], axis=0))
    input_gradient = jnp.concatenate(
        [
            back_one[j][2][:step].astype(F32) + after(last_flights[j], send_mixed_one).astype(F32) + norm_one[j][0][:step]
            for j in pair
        ],
        axis=0,
    )
    seconds_two = last_two.rest()
    wide = jnp.concatenate([norm_sums(under, norm_one), norm_sums(top_tail, norm_two)], axis=0)
    wide = total_over(after(wide, send_mixed_one), "mp")
    base_feed_one, second_feed_one = feed_second(sums_feed_one, *m_feed_one)
    base_mixed_one, second_mixed_one = mixed_second(sums_mixed_one, mixed_one, width)
    seconds_one = total_over(jnp.concatenate([second_feed_one, second_mixed_one, wide], axis=0), "dp")
    seconds_feed_one, seconds_mixed_one, wide = seconds_one[:16], seconds_one[16:32], seconds_one[32:].reshape(2, 8, cols)
    gain_sum = jnp.concatenate([wide[:, 3:4], wide[:, 0:1]], axis=1)
    shift_sum = jnp.concatenate([wide[:, 5:6], wide[:, 4:5], wide[:, 2:3], wide[:, 1:2]], axis=1)
    held_feed = feed_error(base_feed_two, seconds_two[:16], *m_feed_two, 1, replicas, None)
    held_mixed = mixed_error(base_mixed_two, seconds_two[16:32], mixed_two, 1, replicas, None)
    new_e_in, new_e_out = feed_error(base_feed_one, seconds_feed_one, *m_feed_one, 0, replicas, held_feed)
    new_e_qkv, new_e_o = mixed_error(base_mixed_one, seconds_mixed_one, mixed_one, 0, replicas, held_mixed)
    member_errors = [flip(new_e_qkv), new_e_o, new_e_in, new_e_out]

    def unpack_bases(feed, mixed):
        return [mixed[:24].reshape(3, 8, -1), mixed[24:, :width], feed[:8], feed[8:16]]

    def unpack_seconds(feed, mixed):
        proj = jnp.stack([mixed[:8, 256 * member : 256 * member + width] for member in range(3)])
        return [proj, mixed[8:], feed[:8], feed[8:16]]

    bases = (unpack_bases(base_feed_one, base_mixed_one), unpack_bases(base_feed_two, base_mixed_two))
    seconds = (unpack_seconds(seconds_feed_one, seconds_mixed_one), unpack_seconds(seconds_two[:16], seconds_two[16:32]))
    scaled = [[second / replicas for second in seconds[layer]] for layer in range(2)]
    bias_rows = (sums_mixed_one[24], sums_two[48])
    bias_qv = jnp.stack([jnp.stack([row[256 : 256 + width], row[512 : 512 + width]]) for row in bias_rows])
    bias_in = jnp.stack([sums_feed_one[16], sums_two[16]])

    def part_of(value, axis):
        rows = value.shape[axis] // replicas
        return lax.dynamic_slice_in_dim(value, index * rows, rows, axis)

    def update_qkv(layer):
        base = part_of(bases[layer][0], 2)
        return jnp.einsum("jrm,jrn->jmn", base, scaled[layer][0], precision=HIGHEST)

    def update_o(layer):
        return dot(bases[layer][1], part_of(scaled[layer][1], 1), 0, 0, HIGHEST)

    def update_in(layer):
        return dot(part_of(bases[layer][2], 1), scaled[layer][2], 0, 0, HIGHEST)

    def update_out(layer):
        return flip(dot(part_of(scaled[layer][3], 1), bases[layer][3], 0, 0, HIGHEST))

    def renew(weight, moment, update):
        moment_new = MOMENTUM * moment + jnp.stack([update(0), update(1)])
        return weight - RATE * moment_new, moment_new

    new_w_qkv, new_m_qkv = renew(w_qkv, m_qkv, update_qkv)
    new_w_o, new_m_o = renew(w_o, m_o, update_o)
    new_w_in, new_m_in = renew(w_in, m_in, update_in)
    new_w_out, new_m_out = renew(w_out, m_out, update_out)
    new_m_qv = MOMENTUM * m_qv + bias_qv / replicas
    new_m_bin = MOMENTUM * m_bin + bias_in / replicas
    new_m_gain = MOMENTUM * m_gain + gain_sum / replicas
    new_m_shift = MOMENTUM * m_shift + shift_sum / replicas
    outer = [flip(jnp.stack([bases[0][member], bases[1][member]])) for member in range(4)]
    inner = [flip(jnp.stack([seconds[0][member], seconds[1][member]])) for member in range(4)]
    return (
        output, input_gradient, new_w_qkv, new_w_o, new_w_in, new_w_out,
        b_qv - RATE * new_m_qv, b_in - RATE * new_m_bin, ln_gain - RATE * new_m_gain, shifts - RATE * new_m_shift,
        new_m_qkv, new_m_o, new_m_in, new_m_out, new_m_qv, new_m_bin, new_m_gain, new_m_shift,
        *member_errors, *outer, *inner,
    )


def solution(mesh):
    in_specs = (
        P(("dp", "mp"), None), P(("dp", "mp"), None), P("dp", None), P("dp"),
        P(None, None, "dp", "mp"), P(None, "mp", "dp"), P(None, "dp", "mp"), P(None, "mp", "dp"),
        P(None, None, "mp"), P(None, "mp"), P(), P(),
        P(None, None, "dp", "mp"), P(None, "mp", "dp"), P(None, "dp", "mp"), P(None, "mp", "dp"),
        P(None, None, "mp"), P(None, "mp"), P(), P(),
        P("dp", None, None, None, "mp"), P("dp", None, "mp", None), P("dp", None, None, "mp"), P("dp", None, "mp", None),
        P(None, None, "mp", None), P(None, "mp", None), P(None, "mp", None), P(None, "mp", None),
    )
    out_specs = (
        P(("dp", "mp"), None), P(("dp", "mp"), None),
        P(None, None, "dp", "mp"), P(None, "mp", "dp"), P(None, "dp", "mp"), P(None, "mp", "dp"),
        P(None, None, "mp"), P(None, "mp"), P(), P(),
        P(None, None, "dp", "mp"), P(None, "mp", "dp"), P(None, "dp", "mp"), P(None, "mp", "dp"),
        P(None, None, "mp"), P(None, "mp"), P(), P(),
        P("dp", None, None, None, "mp"), P("dp", None, "mp", None), P("dp", None, None, "mp"), P("dp", None, "mp", None),
        P(None, None, "mp", None), P(None, "mp", None), P(None, "mp", None), P(None, "mp", None),
        P(None, None, "mp", None), P(None, "mp", None), P(None, "mp", None), P(None, "mp", None),
    )
    return jax.shard_map(per_device, mesh=mesh, in_specs=in_specs, out_specs=out_specs, check_vma=False)
```

```python
import jax
import jax.numpy as jnp
from jax import lax
from jax.experimental import pallas as pl
from jax.experimental.pallas import tpu as pltpu
from jax.sharding import PartitionSpec as P

HD = 64


NORM_EPS = 1e-05
ORTHO_EPS = 1e-06
MOMENTUM = 0.9
RATE = 0.05
MASKED = -1000000000.0
ROOT_HALF = 0.7071067811865476
INV_ROOT_TWO_PI = 0.3989422804014327
HIGHEST = lax.Precision.HIGHEST
LOW = jnp.bfloat16
F32 = jnp.float32


def dot(left, right, left_dim, right_dim, precision=None):
    return lax.dot_general(
        left,
        right,
        (((left_dim,), (right_dim,)), ((), ())),
        preferred_element_type=F32,
        precision=precision,
    )


def swap(value, axis, bit):
    size = lax.axis_size(axis)
    return lax.ppermute(value, axis, [(i, i ^ bit) for i in range(size)])


def gelu_parts(upper):
    cdf = 0.5 * (1.0 + lax.erf(upper * ROOT_HALF))
    slope = cdf + upper * jnp.exp(-0.5 * upper * upper) * INV_ROOT_TWO_PI
    return upper * cdf, slope


def after(value, *marks):
    return lax.optimization_barrier((value, *marks))[0]


def rows_sum(part, arrived):
    half = part.shape[0] // 2
    part, arrived = part.astype(F32), arrived.astype(F32)
    return jnp.concatenate([part[:half] + arrived[half:], part[half:] + arrived[:half]], axis=0)


def normal(rows_in):
    centred = rows_in - jnp.mean(rows_in, axis=-1, keepdims=True)
    inverse = lax.rsqrt(jnp.mean(centred * centred, axis=-1, keepdims=True) + NORM_EPS)
    return centred * inverse, inverse


def normal_back(grad, normed, inverse, gain):
    scaled = grad * gain
    inner = jnp.mean(scaled * normed, axis=-1, keepdims=True)
    return inverse * (scaled - jnp.mean(scaled, axis=-1, keepdims=True) - normed * inner)


class Arriving:
    def __init__(self, source, local, mark):
        self.local, self.shape, self.dtype, self.waited = local, local.shape, local.dtype, False
        self.copy = pltpu.make_async_copy(source, local, mark)
        self.copy.start()

    def __getitem__(self, index):
        self.settle()
        return self.local[index]

    def settle(self):
        if not self.waited:
            self.copy.wait()
            self.waited = True


class Leaving:
    def __init__(self, target, local, mark):
        self.local, self.shape, self.dtype, self.written = local, local.shape, local.dtype, 0
        self.copy = pltpu.make_async_copy(local, target, mark)

    def __setitem__(self, index, value):
        self.local[index] = value
        self.written += value.size
        if self.written == self.local.size:
            self.copy.start()

    def __getitem__(self, index):
        return self.local[index]

    def settle(self):
        assert self.written == self.local.size
        self.copy.wait()


def call(kernel, outs, args, name, flops, limit=24, scalars=None, far=(), far_outs=()):
    lead = 0 if scalars is None else 1
    inputs, results = len(args), len(outs)
    parts = {i: a[1] for i, a in enumerate(args) if isinstance(a, tuple)}
    kinds = [jax.ShapeDtypeStruct(a[2], a[0].dtype) if isinstance(a, tuple) else a for a in args]
    args = [a[0] if isinstance(a, tuple) else a for a in args]
    args = [pltpu.with_memory_space_constraint(a, pltpu.HBM) if i in far else a for i, a in enumerate(args)]
    moved_in, moved_out = [kinds[i] for i in far], [outs[i] for i in far_outs]

    def body(*refs):
        refs = list(refs)
        scratch = refs[lead + inputs + results :]
        late = []
        for spot, i in enumerate(far):
            source = refs[lead + i].at[parts[i]] if i in parts else refs[lead + i]
            refs[lead + i] = Arriving(source, scratch[spot], scratch[-1].at[spot])
            late.append(refs[lead + i])
        for spot, i in enumerate(far_outs):
            spot += len(far)
            at = lead + inputs + i
            refs[at] = Leaving(refs[at], scratch[spot], scratch[-1].at[spot])
            late.append(refs[at])
        kernel(*refs[: lead + inputs + results])
        for item in late:
            item.settle()

    near = lambda shape: pl.BlockSpec(shape, lambda n=len(shape): (0,) * n)
    elsewhere = pl.BlockSpec(memory_space=pltpu.HBM)
    specs = [elsewhere if i in far else near(a.shape) for i, a in enumerate(args)]
    out_specs = [elsewhere if i in far_outs else near(shape) for i, (shape, _) in enumerate(outs)]
    scratch = [pltpu.VMEM(a.shape, a.dtype) for a in moved_in] + [pltpu.VMEM(shape, kind) for shape, kind in moved_out]
    if scratch:
        scratch.append(pltpu.SemaphoreType.DMA((len(scratch),)))
    operands = list(args)
    if lead:
        specs = [pl.BlockSpec(memory_space=pltpu.SMEM)] + specs
        operands = [scalars] + operands
    shapes = [jax.ShapeDtypeStruct(shape, kind) for shape, kind in outs]
    made = [pltpu.HBM(shape, kind) if i in far_outs else shapes[i] for i, (shape, kind) in enumerate(outs)]
    moved = sum(a.size * a.dtype.itemsize for a in [*kinds, *shapes])
    return pl.pallas_call(
        body,
        in_specs=specs,
        out_specs=out_specs,
        out_shape=made,
        scratch_shapes=scratch,
        cost_estimate=cost(flops, moved),
        compiler_params=params(limit),
        name=name,
    )(*operands)


def join_kernel(order, flags_ref, own_ref, other_ref, q_ref, kv_ref, out_ref):
    width = q_ref.shape[1] // 2
    rows = own_ref.shape[0] // len(order)
    front = flags_ref[0] == 0
    for spot, v in enumerate(order):
        here = slice(spot * rows, (spot + 1) * rows)
        there = here if len(order) == 1 else pl.ds(pl.multiple_of((flags_ref[2] ^ v) * rows, 16), rows)
        groups = []
        for part in range(4):
            lanes = slice(part * width, (part + 1) * width)
            own, other = own_ref[here, lanes].astype(F32), other_ref[here, lanes].astype(F32)
            left, right = jnp.where(front, own, other), jnp.where(front, other, own)
            groups.append(jnp.concatenate([left, right], axis=1).astype(LOW))
        q_ref[there, :] = groups[0]
        kv_ref[there, : 2 * width] = groups[1]
        kv_ref[there, 2 * width :] = groups[2]
        out_ref[there, :] = groups[3]


def project(low, wq_ref, wkv_ref, bias_ref, q_ref, kv_ref):
    width = wq_ref.shape[1]
    q_ref[...] = (dot(low, wq_ref[...], 1, 0) + bias_ref[:, :width]).astype(LOW)
    kv_ref[...] = (dot(low, wkv_ref[...], 1, 0) + bias_ref[:, width:]).astype(LOW)


def project_kernel(x_ref, wq_ref, wkv_ref, bias_ref, q_ref, kv_ref):
    project(x_ref[...], wq_ref, wkv_ref, bias_ref, q_ref, kv_ref)


def first_norm(rows, vec_ref):
    return normal(rows)[0] * vec_ref[0:1, :] + vec_ref[2:3, :]


def second_norm(rows, vec_ref):
    return normal(rows)[0] * vec_ref[1:2, :] + vec_ref[3:4, :]


def norm_project_kernel(
    sent_ref, arrived_ref, rows_ref, vec_ref, wq_ref, wkv_ref, bias_ref, out_ref, low_ref, q_ref, kv_ref
):
    rows = rows_sum(sent_ref[...], arrived_ref[...]) + vec_ref[5:6, :] + first_norm(rows_ref[...], vec_ref)
    out_ref[...] = rows
    low = second_norm(rows, vec_ref).astype(LOW)
    low_ref[...] = low
    project(low, wq_ref, wkv_ref, bias_ref, q_ref, kv_ref)


def pick(flag, first, second):
    return jnp.where(flag, first.astype(F32), second.astype(F32)).astype(LOW)


def attend_kernel(flags_ref, q_ref, k0_ref, k1_ref, k2_ref, k3_ref, place_ref, bound_ref, wo_ref,
                  keep_ref, give_ref, logsum_ref, sent_ref):
    rows, width = q_ref.shape
    pieces = (k0_ref, k1_ref, k2_ref, k3_ref)
    lanes = lax.broadcasted_iota(jnp.int32, (1, 128), 1)
    low, high = bound_ref[:, :1], bound_ref[:, 1:2]
    masks = []
    for index, ref in enumerate(pieces):
        place = place_ref[:, index * ref.shape[0] : (index + 1) * ref.shape[0]]
        masks.append(jnp.where((place >= low) & (place < high), 0.0, MASKED))
    logsums = jnp.zeros((rows, 128), F32)
    tiles = []
    for tile in range(width // 128):
        cols = slice(tile * 128, tile * 128 + 128)
        other = slice(width + tile * 128, width + tile * 128 + 128)
        query = q_ref[:, cols]
        out = None
        for side in range(2):
            here = (lanes >= side * HD) & (lanes < side * HD + HD)
            lone = jnp.where(here, query.astype(F32) * HD ** (-0.5), 0.0).astype(LOW)
            scores = [dot(lone, ref[:, cols], 1, 1) + mask for ref, mask in zip(pieces, masks)]
            highest = jnp.max(scores[0], axis=-1, keepdims=True)
            for score in scores[1:]:
                highest = jnp.maximum(highest, jnp.max(score, axis=-1, keepdims=True))
            powers = [jnp.exp(score - highest) for score in scores]
            total = sum(jnp.sum(power, axis=-1, keepdims=True) for power in powers)
            inverse = 1.0 / total
            head = sum(dot((power * inverse).astype(LOW), ref[:, other], 1, 0) for power, ref in zip(powers, pieces))
            head = jnp.where(here, head, 0.0)
            out = head if out is None else out + head
            logsums = jnp.where(lanes == 2 * tile + side, highest + jnp.log(total), logsums)
        tiles.append(out.astype(LOW))
    logsum_ref[...] = logsums
    mixed = jnp.concatenate(tiles, axis=1)
    half = width // 2
    keep_ref[...] = pick(flags_ref[0] == 0, mixed[:, :half], mixed[:, half:])
    give_ref[...] = pick(flags_ref[0] == 0, mixed[:, half:], mixed[:, :half])
    sent_ref[...] = dot(mixed, wo_ref[...], 1, 1).astype(LOW)


def attend_all_kernel(flags_ref, kinds, *refs):
    pieces, place_ref, wo_ref, rest = refs[:4], refs[4], refs[5], refs[6:]
    chunks = len(rest) // (kinds + 2)
    for j in range(chunks):
        outs = rest[2 * chunks + j * kinds : 2 * chunks + (j + 1) * kinds]
        attend_kernel(flags_ref, rest[j], *pieces, place_ref, rest[chunks + j], wo_ref, *outs)


def attend_back_kernel(first, *refs):
    rows_ref, wo_ref, q_ref, k0_ref, k1_ref, k2_ref, k3_ref, logsum_ref, resid_ref = refs[:9]
    sent_ref, arrived_ref, vec_ref, place_ref, bound_ref = refs[9:14]
    held_refs = () if first else refs[14:18]
    rest_ref, low_ref, norm_sums_ref, dq_ref, *sums_refs = refs[14 + len(held_refs) :]
    grad = rows_sum(sent_ref[...], arrived_ref[...]) + resid_ref[...]
    normed, inverse = normal(rows_ref[...])
    back = normal_back(grad, normed, inverse, vec_ref[0:1, :])
    rest_ref[...] = back
    put_sums(norm_sums_ref, [grad * normed, grad, back], 3)
    low_back = back.astype(LOW)
    low_ref[...] = low_back
    mixed_grad = dot(low_back, wo_ref[...], 1, 0).astype(LOW).astype(F32)
    rows, width = q_ref.shape
    pieces = (k0_ref, k1_ref, k2_ref, k3_ref)
    lanes = lax.broadcasted_iota(jnp.int32, (1, 128), 1)
    low, high = bound_ref[:, :1], bound_ref[:, 1:2]
    scale = HD ** (-0.5)
    masks = []
    for index, ref in enumerate(pieces):
        place = place_ref[:, index * ref.shape[0] : (index + 1) * ref.shape[0]]
        masks.append(jnp.where((place >= low) & (place < high), 0.0, MASKED))
    for tile in range(width // 128):
        cols = slice(tile * 128, tile * 128 + 128)
        other = slice(width + tile * 128, width + tile * 128 + 128)
        query, grad = q_ref[:, cols].astype(F32), mixed_grad[:, cols]
        dq = None
        dk, dv = [None] * 4, [None] * 4
        for side in range(2):
            here = (lanes >= side * HD) & (lanes < side * HD + HD)
            lone = jnp.where(here, query * scale, 0.0).astype(LOW)
            lone_grad = jnp.where(here, grad, 0.0).astype(LOW)
            logsum = jnp.sum(jnp.where(lanes == 2 * tile + side, logsum_ref[...], 0.0), axis=-1, keepdims=True)
            probs, prob_grads = [], []
            inner = None
            for ref, mask in zip(pieces, masks):
                prob = jnp.exp(dot(lone, ref[:, cols], 1, 1) + mask - logsum)
                prob_grad = dot(lone_grad, ref[:, other], 1, 1)
                probs.append(prob)
                prob_grads.append(prob_grad)
                piece = jnp.sum(prob * prob_grad, axis=-1, keepdims=True)
                inner = piece if inner is None else inner + piece
            for index, ref in enumerate(pieces):
                score = (probs[index] * (prob_grads[index] - inner)).astype(LOW)
                back = dot(score, ref[:, cols], 1, 0)
                back = jnp.where(here, back * scale, 0.0)
                dq = back if dq is None else dq + back
                key = dot(score, lone, 0, 0)
                value = dot(probs[index].astype(LOW), lone_grad, 0, 0)
                dk[index] = key if dk[index] is None else dk[index] + key
                dv[index] = value if dv[index] is None else dv[index] + value
        dq_ref[:, cols] = dq.astype(LOW)
        for index in range(4):
            key, value = dk[index], dv[index]
            if held_refs:
                key = key + held_refs[index][:, cols]
                value = value + held_refs[index][:, other]
            sums_refs[index][:, cols] = key.astype(sums_refs[index].dtype)
            sums_refs[index][:, other] = value.astype(sums_refs[index].dtype)


def feed_kernel(is_first, sent_ref, arrived_ref, resid_ref, vec_ref, before_ref, feed0_ref, feed1_ref, bias_ref,
                rows_ref, give_ref, act_ref, slope_ref, out_ref):
    resid = resid_ref[...].astype(F32) if is_first else second_norm(resid_ref[...], before_ref)
    rows = rows_sum(sent_ref[...], arrived_ref[...]) + vec_ref[4:5, :] + resid
    rows_ref[...] = rows
    low = first_norm(rows, vec_ref).astype(LOW)
    cols = low.shape[1]
    units = feed0_ref.shape[0]
    top = feed0_ref.shape[1] - units
    base = top - units
    give_ref[:, :cols] = low
    act, slope = gelu_parts(dot(low, feed0_ref[:, base:top], 1, 0) + bias_ref[0:1, :])
    act = act.astype(LOW)
    act_ref[...] = act
    slope_ref[:, :units] = slope.astype(LOW)
    part = dot(act, feed0_ref[:, top:], 1, 1)
    act, slope = gelu_parts(dot(low, feed1_ref[:, base:top], 1, 0) + bias_ref[1:2, :])
    act = act.astype(LOW)
    give_ref[:, cols:] = act
    slope_ref[:, units:] = slope.astype(LOW)
    out_ref[...] = (part + dot(act, feed1_ref[:, top:], 1, 1)).astype(LOW)


def put_sums(sums_ref, lists, start):
    half = lists[0].shape[0] // 2
    sums_ref[...] = jnp.zeros(sums_ref.shape, F32)
    for index, rows in enumerate(lists):
        sums_ref[start + index : start + index + 1, :] = jnp.sum(rows[:half], axis=0, keepdims=True)


def back_feed(grad, normed, inverse, gain, slope_ref, feed0_ref, feed1_ref, rest_ref, give_ref, keep_ref, out_ref, sums_ref):
    back = normal_back(grad, normed, inverse, gain)
    rest_ref[...] = back
    put_sums(sums_ref, [grad * normed, grad, back], 0)
    low = back.astype(LOW)
    cols = low.shape[1]
    units = feed0_ref.shape[0]
    top = feed0_ref.shape[1] - units
    base = top - units
    give_ref[:, :cols] = low
    upper = (dot(low, feed0_ref[:, top:], 1, 0) * slope_ref[:, :units].astype(F32)).astype(LOW)
    keep_ref[...] = upper
    part = dot(upper, feed0_ref[:, base:top], 1, 1)
    upper = (dot(low, feed1_ref[:, top:], 1, 0) * slope_ref[:, units:].astype(F32)).astype(LOW)
    give_ref[:, cols:] = upper
    out_ref[...] = (part + dot(upper, feed1_ref[:, base:top], 1, 1)).astype(LOW)


def top_kernel(flags_ref, sent_ref, arrived_ref, rows_ref, grad_ref, before_rows_ref, before_ref, vec_ref, slope_ref,
               feed0_ref, feed1_ref, y_ref, rest_ref, give_ref, keep_ref, out_ref, sums_ref):
    rows = rows_sum(sent_ref[...], arrived_ref[...]) + vec_ref[5:6, :] + first_norm(rows_ref[...], vec_ref)
    normed, inverse = normal(rows)
    half = normed.shape[0] // 2
    y = normed[:half] * vec_ref[1:2, :] + vec_ref[3:4, :]
    on = flags_ref[1] > 0
    y_ref[...] = jnp.where(on, y, second_norm(before_rows_ref[:half, :], before_ref))
    grad = jnp.where(on, grad_ref[...].astype(F32), 0.0)
    back_feed(grad, normed, inverse, vec_ref[1:2, :], slope_ref, feed0_ref, feed1_ref,
              rest_ref, give_ref, keep_ref, out_ref, sums_ref)


def under_kernel(flags_ref, sent_ref, arrived_ref, resid_ref, grad_ref, rows_ref, vec_ref, slope_ref,
                 feed0_ref, feed1_ref, rest_ref, give_ref, keep_ref, out_ref, sums_ref):
    grad = rows_sum(sent_ref[...], arrived_ref[...]) + resid_ref[...]
    grad = jnp.where(flags_ref[1] > 0, grad, grad_ref[...].astype(F32))
    normed, inverse = normal(rows_ref[...])
    back_feed(grad, normed, inverse, vec_ref[1:2, :], slope_ref, feed0_ref, feed1_ref,
              rest_ref, give_ref, keep_ref, out_ref, sums_ref)


def renew_kernel(replicas, flags_ref, *refs):
    bases, seconds, state, outs = refs[:4], refs[4:7], refs[7:15], refs[15:]
    rows = state[2].shape[2]
    cols = bases[0].shape[1]
    pick_rows = lax.broadcasted_iota(jnp.int32, (cols, rows), 0)
    pick_cols = lax.broadcasted_iota(jnp.int32, (cols, rows), 1)
    chosen = jnp.where(pick_rows == pick_cols + flags_ref[2] * rows, 1.0, 0.0).astype(LOW)

    def part(value):
        high, rest = split(value)
        return dot(high, chosen, 1, 0) + dot(rest, chosen, 1, 0)

    def write(index, spot, update):
        weight, moment = state[2 * index], state[2 * index + 1]
        fresh = MOMENTUM * moment[spot] + update
        outs[2 * index + 1][spot] = fresh
        outs[2 * index][spot] = weight[spot] - RATE * fresh

    for layer in range(2):
        base_feed, base_mixed = bases[2 * layer][...], bases[2 * layer + 1][...]
        width = state[2].shape[1]
        scale = 1.0 / replicas
        if layer == 0:
            feed, mixed = seconds[0][...], seconds[1][...]
        else:
            feed, mixed = seconds[2][:16, :], seconds[2][16:, :]
        for member in range(3):
            outs[8][(layer, member)] = base_mixed[8 * member : 8 * member + 8]
            outs[12][(layer, member)] = mixed[:8, 256 * member : 256 * member + width]
        outs[9][(layer,)] = base_mixed[24:32, :width]
        outs[13][(layer,)] = mixed[8:]
        for member in range(2):
            outs[10 + member][(layer,)] = base_feed[8 * member : 8 * member + 8]
            outs[14 + member][(layer,)] = feed[8 * member : 8 * member + 8]
        feed, mixed = feed * scale, mixed * scale
        for member in range(3):
            update = low_rank(part(base_mixed[8 * member : 8 * member + 8]), mixed[:8, 256 * member : 256 * member + width])
            write(0, (layer, member), update)
        write(1, (layer,), low_rank(base_mixed[24:32, :width], part(mixed[8:])))
        write(2, (layer,), low_rank(part(base_feed[:8]), feed[:8]))
        write(3, (layer,), low_rank(part(feed[8:]), base_feed[8:16]))


def back_project_kernel(flags_ref, dq_ref, own_ref, arrived_ref, wq_ref, wkv_ref, keep_ref, give_ref, sent_ref):
    dq = dq_ref[...]
    dkv = (own_ref[...] + arrived_ref[...].astype(F32)).astype(LOW)
    sent_ref[...] = (dot(dq, wq_ref[...], 1, 1) + dot(dkv, wkv_ref[...], 1, 1)).astype(LOW)
    half = dq.shape[1] // 2
    groups = (dq, dkv[:, : 2 * half], dkv[:, 2 * half :])
    front = flags_ref[0] == 0
    keep_ref[...] = jnp.concatenate([pick(front, g[:, :half], g[:, half:]) for g in groups], axis=1)
    give_ref[...] = jnp.concatenate([pick(front, g[:, half:], g[:, :half]) for g in groups], axis=1)

def split(value):
    high = value.astype(LOW)
    return high, (value - high.astype(F32)).astype(LOW)


def split_dot(small, large, small_dim, large_dim):
    high, rest = split(large)
    lead, tail = split(small)
    rows = small.shape[0]
    both = dot(jnp.concatenate([lead, tail], axis=0), high, small_dim, large_dim)
    return both[:rows] + both[rows:] + dot(lead, rest, small_dim, large_dim)


def dot_chunks(lefts, rights):
    total = None
    for left, right in zip(lefts, rights):
        part = dot(left[...], right[...], 0, 0)
        total = part if total is None else total + part
    return total


def rows_total_kernel(chunks, *refs):
    lefts, rights = refs[:chunks], refs[chunks : 2 * chunks]
    error_ref, start_ref, total_ref, first_ref, bias_ref = refs[2 * chunks :]
    total = dot_chunks(lefts, rights) + error_ref[...]
    total_ref[...] = total
    first_ref[...] = split_dot(start_ref[...], total, 1, 1)

    @pl.when(pl.program_id(0) == 0)
    def _():
        bias = sum(jnp.sum(ref[...].astype(F32), axis=0, keepdims=True) for ref in rights)
        bias_ref[...] = jnp.concatenate([bias, jnp.zeros((7, bias.shape[1]), F32)], axis=0)


def params(limit, **more):
    return pltpu.CompilerParams(vmem_limit_bytes=limit << 20, **more)


def cost(flops, moved):
    return pl.CostEstimate(flops=int(flops), bytes_accessed=int(moved), transcendentals=0)


def rows_total(lefts, rights, errors, starts, layer):
    rows, cols = errors.shape[-2:]
    tokens = lefts[0][0].shape[0]
    rank = starts.shape[1]
    step = 256
    chunks = len(lefts)
    return pl.pallas_call(
        lambda *refs: rows_total_kernel(chunks, *refs),
        grid=(rows // step,),
        in_specs=[pl.BlockSpec((tokens, step), lambda i, at=at: (0, i + at * (rows // step))) for _, at in lefts]
        + [pl.BlockSpec((tokens, cols), lambda i, at=at: (0, at)) for _, at in rights]
        + [
            pl.BlockSpec((None, None, step, cols), lambda i: (0, layer, i, 0)),
            pl.BlockSpec((None, rank, cols), lambda i: (layer, 0, 0)),
        ],
        out_specs=[
            pl.BlockSpec((step, cols), lambda i: (i, 0)),
            pl.BlockSpec((rank, step), lambda i: (0, i)),
            pl.BlockSpec((rank, cols), lambda i: (0, 0)),
        ],
        out_shape=[
            jax.ShapeDtypeStruct((rows, cols), F32),
            jax.ShapeDtypeStruct((rank, rows), F32),
            jax.ShapeDtypeStruct((rank, cols), F32),
        ],
        cost_estimate=cost(2 * chunks * tokens * rows * cols, 8 * rows * cols + 4 * chunks * tokens * rows),
        compiler_params=params(24),
        name="rows_total",
    )(*[array for array, _ in lefts], *[array for array, _ in rights], errors, starts)


def mixed_total_kernel(chunks, *refs):
    proj_refs, whole_refs = refs[:chunks], refs[chunks : 2 * chunks]
    attended_refs, piece_refs = refs[2 * chunks : 3 * chunks], refs[3 * chunks : 4 * chunks]
    e_proj_ref, e_back_ref, s_proj_ref, s_back_ref, total_ref, first_ref = refs[4 * chunks :]
    width = e_back_ref.shape[0]
    grads = dot_chunks(proj_refs, whole_refs)
    for member in range(3):
        rows = slice(member * width, (member + 1) * width)
        total = grads[rows] + e_proj_ref[member]
        total_ref[rows, :] = total
        first_ref[8 * member : 8 * member + 8, :] = split_dot(s_proj_ref[member], total, 1, 0)
    total = dot_chunks(attended_refs, piece_refs) + e_back_ref[...]
    total_ref[3 * width :, :] = total
    first_ref[24:, :] = jnp.zeros((8, total.shape[1]), F32)
    first_ref[24:, :width] = split_dot(s_back_ref[...], total, 1, 1)
    sums = sum(jnp.sum(ref[...].astype(F32), axis=0, keepdims=True) for ref in proj_refs)
    first_ref[24:25, 256 : 256 + width] = sums[:, :width]
    first_ref[24:25, 512 : 512 + width] = sums[:, 2 * width :]


def mixed_total(proj_low, whole_in, attended, piece, e_proj, e_back, s_proj, s_back, layer):
    tokens, width = attended[0].shape
    cols = whole_in[0].shape[1]
    rank = s_back.shape[1]
    chunks = len(attended)
    args = [*proj_low, *whole_in, *attended, *piece, (e_proj, (0, layer), e_proj.shape[2:]), (e_back, (0, layer), e_back.shape[2:]), s_proj[layer], s_back[layer]]
    return call(
        lambda *refs: mixed_total_kernel(chunks, *refs),
        [[(4 * width, cols), F32], [(4 * rank, cols), F32]],
        args, "mixed_total", 2 * chunks * tokens * 4 * width * cols, 24, None, range(4 * chunks + 2),
    )


def ortho_rows(factor):
    rank = factor.shape[0]
    index = lax.broadcasted_iota(jnp.int32, (rank, 1), 0)
    for row in range(rank):
        vector = factor[row : row + 1, :]
        inner = jnp.sum(factor * vector, axis=1, keepdims=True)
        scale = lax.rsqrt(inner[row : row + 1] + ORTHO_EPS)
        vector = vector * scale
        factor = jnp.where(
            index < row, factor, jnp.where(index == row, vector, factor - vector * (inner * scale))
        )
    return factor


def feed_second_kernel(sums_ref, up_ref, down_ref, base_ref, second_ref):
    for member, total_ref in enumerate((up_ref, down_ref)):
        rows = slice(8 * member, 8 * member + 8)
        base = ortho_rows(sums_ref[rows, :])
        base_ref[rows, :] = base
        second_ref[rows, :] = split_dot(base, total_ref[...], 1, 0)


def feed_second(sums, m_up, m_down):
    cols = m_up.shape[1]
    return pl.pallas_call(
        feed_second_kernel,
        out_shape=[jax.ShapeDtypeStruct((16, cols), F32)] * 2,
        cost_estimate=cost(96 * m_up.size, 8 * m_up.size),
        compiler_params=params(24),
        name="feed_second",
    )(sums, m_up, m_down)


def mixed_second_kernel(width, sums_ref, total_ref, base_ref, second_ref):
    second_ref[...] = jnp.zeros(second_ref.shape, F32)
    for member in range(3):
        rows = slice(8 * member, 8 * member + 8)
        base = ortho_rows(sums_ref[rows, :])
        base_ref[rows, :] = base
        second_ref[:8, 256 * member : 256 * member + width] = split_dot(
            base, total_ref[member * width : (member + 1) * width, :], 1, 1
        )
    base = ortho_rows(sums_ref[24:32, :width])
    base_ref[24:32, :width] = base
    second_ref[8:, :] = split_dot(base, total_ref[3 * width :, :], 1, 0)


def mixed_second(sums, m_mixed, width):
    cols = m_mixed.shape[1]
    return pl.pallas_call(
        lambda *refs: mixed_second_kernel(width, *refs),
        out_shape=[jax.ShapeDtypeStruct((32, cols), F32), jax.ShapeDtypeStruct((16, cols), F32)],
        cost_estimate=cost(48 * m_mixed.size, 4 * m_mixed.size),
        compiler_params=params(16),
        name="mixed_second",
    )(sums, m_mixed)


def low_rank(base, second):
    b_high, b_rest = split(base)
    s_high, s_rest = split(second)
    left = jnp.concatenate([b_high, b_rest, b_high], axis=0)
    right = jnp.concatenate([s_high, s_high, s_rest], axis=0)
    return dot(left, right, 0, 0)


def feed_error_kernel(layer, replicas, base_ref, second_ref, up_ref, down_ref, *refs):
    up_out, down_out = refs[-2:]
    seconds = second_ref[...] * (1.0 / replicas)
    up_out[...] = up_ref[...] - low_rank(base_ref[:8, :], seconds[:8])
    down_out[...] = down_ref[...] - low_rank(base_ref[8:16, :], seconds[8:16])


def feed_error(base, second, m_up, m_down, layer, replicas, held):
    rows, cols = m_up.shape
    rank2 = base.shape[0]
    step = 256
    shape = jax.ShapeDtypeStruct((1, 2, rows, cols), F32)
    out_spec = pl.BlockSpec((None, None, step, cols), lambda i: (0, layer, i, 0))
    extra = {} if held is None else {"input_output_aliases": {4: 0, 5: 1}}
    return pl.pallas_call(
        lambda *refs: feed_error_kernel(layer, replicas, *refs),
        grid=(rows // step,),
        in_specs=[
            pl.BlockSpec((rank2, step), lambda i: (0, i)),
            pl.BlockSpec((rank2, cols), lambda i: (0, 0)),
            pl.BlockSpec((step, cols), lambda i: (i, 0)),
            pl.BlockSpec((step, cols), lambda i: (i, 0)),
        ] + ([] if held is None else [pl.BlockSpec(memory_space=pl.ANY)] * 2),
        out_specs=[out_spec, out_spec],
        out_shape=[shape, shape],
        cost_estimate=cost(100 * m_up.size, 16 * m_up.size),
        compiler_params=params(16),
        name="feed_error",
        **extra,
    )(base, second, m_up, m_down, *(() if held is None else held))


def mixed_error_kernel(replicas, base_ref, second_ref, total_ref, *refs):
    proj_out, back_out = refs[-2:]
    width = back_out.shape[0]
    seconds = second_ref[...] * (1.0 / replicas)
    for member in range(3):
        approx = low_rank(seconds[:8, 256 * member : 256 * member + width], base_ref[8 * member : 8 * member + 8, :])
        proj_out[member] = total_ref[member * width : (member + 1) * width, :] - approx
    back_out[...] = total_ref[3 * width :, :] - low_rank(base_ref[24:32, :width], seconds[8:])


def mixed_error(base, second, m_mixed, layer, replicas, held):
    rows, cols = m_mixed.shape
    width = rows // 4
    extra = {} if held is None else {"input_output_aliases": {3: 0, 4: 1}}
    return pl.pallas_call(
        lambda *refs: mixed_error_kernel(replicas, *refs),
        grid=(1,),
        in_specs=[
            pl.BlockSpec(base.shape, lambda i: (0, 0)),
            pl.BlockSpec(second.shape, lambda i: (0, 0)),
            pl.BlockSpec((rows, cols), lambda i: (0, 0)),
        ] + ([] if held is None else [pl.BlockSpec(memory_space=pl.ANY)] * 2),
        out_specs=[
            pl.BlockSpec((None, None, 3, width, cols), lambda i: (0, layer, 0, 0, 0)),
            pl.BlockSpec((None, None, width, cols), lambda i: (0, layer, 0, 0)),
        ],
        out_shape=[
            jax.ShapeDtypeStruct((1, 2, 3, width, cols), F32), jax.ShapeDtypeStruct((1, 2, width, cols), F32)
        ],
        cost_estimate=cost(50 * m_mixed.size, 8 * m_mixed.size),
        compiler_params=params(24),
        name="mixed_error",
        **extra,
    )(base, second, m_mixed, *(() if held is None else held))


def flip(value):
    return jnp.swapaxes(value, -1, -2)


def per_device(
    x_in, out_grad, doc_lengths, keep_layer, w_qkv, w_o, w_in, w_out, b_qv, b_in, ln_gain, shifts,
    m_qkv, m_o, m_in, m_out, m_qv, m_bin, m_gain, m_shift, e_qkv, e_o, e_in, e_out, q_qkv, q_o, q_in, q_out,
):
    own_rows, cols = x_in.shape
    replicas = lax.axis_size("dp")
    index = lax.axis_index("dp")
    place = lax.axis_index("mp")
    width = w_o.shape[1]
    front = lax.rem(place, 2) == 0
    flags = jnp.stack([lax.rem(place, 2), keep_layer[0], index]).astype(jnp.int32)
    chunks = 2
    step = own_rows // chunks
    size = 2 * step
    pair = range(chunks)

    def core(value):
        return swap(value, "mp", 1)

    def chip(value):
        return swap(value, "mp", 2)

    def gather(piece):
        return lax.all_gather(piece, "dp", axis=0, tiled=True)

    def join(own, other, axis):
        return jnp.where(
            front, jnp.concatenate([own, other], axis=axis), jnp.concatenate([other, own], axis=axis)
        )

    def mixed_piece(layer):
        return jnp.concatenate(
            [w_qkv[layer, 0], w_qkv[layer, 1], w_qkv[layer, 2], flip(w_o[layer])], axis=1
        ).astype(LOW)

    def feed_piece(layer):
        return jnp.concatenate([w_in[layer], flip(w_out[layer])], axis=1).astype(LOW)

    def by_chunk(rows, arrived):
        return [
            jnp.concatenate([rows[j * step : (j + 1) * step], arrived[j * step : (j + 1) * step]], axis=0) for j in pair
        ]

    small = jnp.concatenate([b_qv.reshape(-1), b_in.reshape(-1)]).reshape(-1, 128)
    small = core(small).reshape(-1)
    other_qv = small[: b_qv.size].reshape(b_qv.shape)
    other_in = small[b_qv.size :].reshape(b_in.shape)

    ends = jnp.sum(
        jnp.where(
            jnp.arange(doc_lengths.shape[1])[:, None] <= jnp.arange(doc_lengths.shape[1])[None, :],
            doc_lengths[0][:, None], 0,
        ),
        axis=0,
    )

    def places_of(device, j):
        steps = jnp.arange(step, dtype=jnp.int32) + j * step
        return jnp.concatenate([device * own_rows + steps, (device ^ 2) * own_rows + steps])

    mine = [places_of(place, j) for j in pair]
    all_places = jnp.concatenate(mine + [places_of(place ^ 1, j) for j in pair])[None, :]

    def bounds_of(places):
        passed = places[:, None] >= ends[None, :]
        low = jnp.max(jnp.where(passed, ends[None, :], 0), axis=1)
        high = jnp.min(jnp.where(passed, 1 << 30, ends[None, :]), axis=1)
        return jnp.stack([low, high], axis=1)

    bounds = [bounds_of(places) for places in mine]

    vecs, feeds, proj_bias, feed_bias = [], [], [], []
    for layer in range(2):
        gain, shift = ln_gain[layer], shifts[layer]
        vecs.append(
            jnp.concatenate(
                [gain, shift[1:2], shift[3:4], shift[0:1], shift[2:3], jnp.zeros((2, cols), F32)], axis=0
            )
        )
        proj_bias.append(
            jnp.concatenate(
                [
                    join(b_qv[layer, 0], other_qv[layer, 0], 0),
                    jnp.zeros((2 * width,), F32),
                    join(b_qv[layer, 1], other_qv[layer, 1], 0),
                ]
            )[None]
        )
        feed_bias.append(jnp.stack([b_in[layer], other_in[layer]]))

    set_in = by_chunk(x_in, chip(x_in))
    order = [0]
    bits = [4, 2, 1] if replicas == 8 else []
    for bit in bits:
        order = order + [v ^ bit for v in order]
    if not bits:
        order = order[:1]

    def doubled(piece, bit):
        return jnp.concatenate([piece, swap(piece, "dp", bit)], axis=0)

    feed_whole = jnp.concatenate([mixed_piece(1), feed_piece(0)], axis=1)
    whole_mixed = mixed_piece(0)
    if bits:
        feed_whole = gather(feed_whole)
        set_grad = by_chunk(out_grad, chip(after(out_grad, *set_in)))
        whole_mixed = doubled(doubled(whole_mixed, 4), 2)
        whole_mixed, all_places, flags, *rest = lax.optimization_barrier(
            (whole_mixed, all_places, flags, *bounds, *vecs, *proj_bias, *feed_bias, *set_in, *set_grad)
        )
        bounds, vecs, proj_bias, feed_bias = rest[:2], rest[2:4], rest[4:6], rest[6:8]
        set_in, set_grad = rest[8:10], rest[10:12]
        whole_mixed = doubled(whole_mixed, 1)
    else:
        set_grad = by_chunk(out_grad, chip(out_grad))
        whole_mixed = gather(whole_mixed)
        feed_whole = gather(feed_whole)
    feed_late, *set_in = lax.optimization_barrier((feed_piece(1), *set_in))
    feed_late = gather(feed_late)
    whole_other = [core(rows) for rows in set_in]

    full = [(size, cols), F32]
    full_low = [(size, cols), LOW]
    thin = [(size, 128), F32]
    half_low = [(size, 2 * width), LOW]
    one_low = [(size, width), LOW]
    kv_low = [(size, 4 * width), LOW]
    units = cols

    def mixed_weights(own, other, order):
        return call(
            lambda *refs: join_kernel(order, *refs), [[(cols, 2 * width), LOW], [(cols, 4 * width), LOW], [(cols, 2 * width), LOW]],
            [(own, (slice(None), pl.ds(0, cols)), (cols, cols)), (other, (slice(None), pl.ds(0, cols)), (cols, cols))],
            "join", 0, 16, flags, (0, 1), (0, 1, 2),
        )

    def attention(layer, q, kv):
        pieces = kv + [core(part) for part in kv]
        kinds = [one_low, one_low, thin, full_low]
        outs = call(
            lambda flags_ref, *refs: attend_all_kernel(flags_ref, len(kinds), *refs), kinds * chunks,
            [*pieces, all_places, wo[layer], *q, *bounds], "attend",
            chunks * (2 * size * (4 * size) * 4 * width + 2 * size * 2 * width * cols), 20, flags, (6, 7, 0, 1, 2, 3, 5), (0, 1, 2, 4, 5, 6),
        )
        return pieces, [outs[j * len(kinds) : (j + 1) * len(kinds)] for j in pair]

    def feed_all(layer, outs, resid):
        return [
            call(
                lambda *refs: feed_kernel(layer == 0, *refs),
                [full, [(size, cols + units), LOW], [(size, units), LOW], [(size, 2 * units), LOW], full_low],
                [outs[j][3], chip(outs[j][3]), resid[j], vecs[layer], vecs[0], *feeds[layer], feed_bias[layer]],
                "feed", 8 * size * cols * units, 26, None, (2, 5, 6), (0, 1, 2, 3),
            )
            for j in pair
        ]

    e_proj, s_proj = flip(e_qkv), flip(q_qkv)
    e_proj, e_back, e_up, e_down = (
        pltpu.with_memory_space_constraint(value, pltpu.HBM) for value in (e_proj, e_o, e_in, e_out)
    )
    s_back, s_up, s_down = flip(q_o), flip(q_in), flip(q_out)

    def feed_up(layer, feed_out, tails, start):
        give_up = [out[1] for out in feed_out]
        give_down = [out[1] for out in tails]
        return rows_total(
            [(rows, 0) for rows in give_up + [core(rows) for rows in give_up]],
            [(out[2], 0) for out in tails] + [(core(rows), 1) for rows in give_down], e_up, start, layer,
        )

    def feed_down(layer, feed_out, tails, start):
        give_up = [out[1] for out in feed_out]
        give_down = [out[1] for out in tails]
        return rows_total(
            [(out[2], 0) for out in feed_out] + [(core(rows), 1) for rows in give_up],
            [(rows, 0) for rows in give_down + [core(rows) for rows in give_down]], e_down, start, layer,
        )

    def mixed_first(layer, low, back, mixed, norm, start):
        return mixed_total(
            [out[0] for out in back] + [core(out[1]) for out in back],
            low,
            [out[0] for out in mixed] + [core(out[1]) for out in mixed],
            [out[1] for out in norm] + [core(out[1]) for out in norm],
            e_proj, e_back, s_proj, start, layer,
        )

    def total_over(value, axis):
        bit = 1
        while bit < lax.axis_size(axis):
            value = value + swap(value, axis, bit)
            bit = 2 * bit
        return value

    class Total:
        def __init__(self, value):
            self.value, self.bit = value, 1

        def step(self, *marks):
            if self.bit < replicas:
                self.value = self.value + after(swap(self.value, "dp", self.bit), *marks)
                self.bit = 2 * self.bit

        def rest(self):
            while self.bit < replicas:
                self.value = self.value + swap(self.value, "dp", self.bit)
                self.bit = 2 * self.bit
            return self.value

    def norm_sums(tails, norm):
        return sum(out[4] for out in tails) + sum(out[3] for out in norm)

    wq, wkv, wo = ([part] for part in mixed_weights(whole_mixed, core(whole_mixed), order))
    first = [
        call(
            project_kernel, [half_low, kv_low], [set_in[j], wq[0], wkv[0], proj_bias[0]],
            "project", 2 * size * cols * 6 * width, 10, None, (1, 2), (0, 1),
        )
        for j in pair
    ]
    q_one = [out[0] for out in first]
    pieces_one, mixed_out_one = attention(0, q_one, [out[1] for out in first])
    feed_whole = after(feed_whole, mixed_out_one[0][3])
    other_whole = core(feed_whole)
    spot = ((slice(None), pl.ds(cols, 2 * cols)), (cols, 2 * cols))
    feeds.append(((feed_whole, *spot), (other_whole, *spot)))
    feed_out_one = feed_all(0, mixed_out_one, set_in)
    own_late = after(feed_whole, feed_out_one[1][4])
    for held, part in zip((wq, wkv, wo), mixed_weights(own_late, other_whole, [0])):
        held.append(part)
    second = [
        call(
            norm_project_kernel, [full, full_low, half_low, kv_low],
            [feed_out_one[j][4], chip(feed_out_one[j][4]), feed_out_one[j][0], vecs[0], wq[1], wkv[1], proj_bias[1]],
            "norm_project", 2 * size * cols * 6 * width, 12, None, (2, 4, 5), (0, 1, 2, 3),
        )
        for j in pair
    ]
    q_two = [out[2] for out in second]
    pieces_two, mixed_out_two = attention(1, q_two, [out[3] for out in second])
    feed_late = after(feed_late, mixed_out_two[1][3])
    other_late = core(feed_late)
    feeds.append((feed_late, other_late))
    feed_out_two = feed_all(1, mixed_out_two, [out[0] for out in second])

    wide_outs = [full, [(size, cols + units), LOW], [(size, units), LOW], full_low, [(8, cols), F32]]
    top = [
        call(
            top_kernel, [[(step, cols), F32]] + wide_outs,
            [
                feed_out_two[j][4], chip(feed_out_two[j][4]), feed_out_two[j][0], set_grad[j], second[j][0], vecs[0],
                vecs[1], feed_out_two[j][3], *feeds[1],
            ],
            "top", 8 * size * cols * units, 28, flags, (2, 3, 4, 8, 9, 7), (0, 1, 2, 3),
        )
        for j in pair
    ]
    output = jnp.concatenate([out[0] for out in top], axis=0)

    def attention_back(layer, outs, feed_out, q, pieces, mixed, vec, between, ending):
        held, dqs, norms = [], [], []
        for j in pair:
            kinds = [full] * 4 if j + 1 < chunks else [full, full, full_low, full_low]
            rest, low, sums, dq, *held = call(
                lambda *refs, j=j: attend_back_kernel(j == 0, *refs),
                [full, full_low, [(8, cols), F32], half_low] + kinds,
                [
                    feed_out[j][0], wo[layer], q[j], *pieces, mixed[j][2], outs[j][0],
                    outs[j][3], chip(outs[j][3]), vec, all_places, bounds[j], *held,
                ],
                "attend_back", 5 * size * (4 * size) * 4 * width, 28, None, (8, 0, 1, 2, 3, 4, 5, 6, 7), (0, 1, 3) if j + 1 < chunks else (0, 1, 3, 4, 5),
            )
            dqs.append(dq)
            norms.append((rest, low, None, sums))
            if j == 0:
                vec = between(vec, sums)
        back_flags = ending(flags, sums)
        return norms, [
            call(
                back_project_kernel, [[(size, 3 * width), LOW], [(size, 3 * width), LOW], full_low],
                [dqs[j], held[j], core(held[2 + j]), wq[layer], wkv[layer]], "back_project",
                2 * size * cols * 6 * width, 16, back_flags, (0, 3, 1, 4), (0, 1),
            )
            for j in pair
        ]

    top_tail = [out[1:] for out in top]
    feed_two_up = feed_up(1, feed_out_two, top_tail, after(s_up, top[1][5]))
    norm_two, back_two = attention_back(
        1, top_tail, feed_out_two, q_two, pieces_two, mixed_out_two, after(vecs[1], feed_two_up[1]),
        lambda vec, sums: vec, lambda flags, sums: flags,
    )
    sent = back_two[1][2]
    feed_two_down = feed_down(1, feed_out_two, top_tail, after(s_down, sent))
    low_two = [out[1] for out in second]
    mixed_two, send_mixed_two = mixed_first(
        1, low_two + [core(rows) for rows in low_two], back_two, mixed_out_two, norm_two, after(s_back, sent)
    )
    total_two = Total(jnp.concatenate([feed_two_up[1], feed_two_down[1], feed_two_up[2], send_mixed_two], axis=0))
    under, under_flags = [], after(flags, feed_two_down[1], send_mixed_two)
    for j in pair:
        under.append(
            call(
                under_kernel, wide_outs,
                [
                    back_two[j][2], chip(back_two[j][2]), norm_two[j][0], set_grad[j], second[j][0],
                    vecs[0], feed_out_one[j][3], *feeds[0],
                ],
                "under", 8 * size * cols * units, 28, under_flags, (2, 3, 4, 7, 8, 6), (0, 1, 2),
            )
        )
    feed_one_up = feed_up(0, feed_out_one, under, after(s_up, under[1][4]))
    feed_one_down = feed_down(0, feed_out_one, under, after(s_down, under[1][4]))
    m_feed_one, m_feed_two = (feed_one_up[0], feed_one_down[0]), (feed_two_up[0], feed_two_down[0])

    total_two.step(feed_one_up[1], feed_one_down[1])

    def between(vec, sums):
        total_two.step(sums)
        return after(vec, total_two.value)

    def ending(flags, sums):
        return after(flags, total_two.value)

    norm_one, back_one = attention_back(
        0, under, feed_out_one, q_one, pieces_one, mixed_out_one,
        after(vecs[0], feed_one_up[1], feed_one_down[1]), between, ending,
    )
    last_flights = [chip(out[2][step:]) for out in back_one]

    sents = [out[2] for out in back_one]
    mixed_one, send_mixed_one = mixed_first(
        0, set_in + whole_other, back_one, mixed_out_one, norm_one, s_back
    )
    total_one = jnp.concatenate([feed_one_up[1], feed_one_down[1], feed_one_up[2], send_mixed_one], axis=0)
    sums_one = total_over(total_one, "dp")
    sums_feed_one, sums_mixed_one = sums_one[:24], sums_one[24:]
    total_two.step(send_mixed_one)
    sums_two = after(total_two.rest(), send_mixed_one)
    base_feed_two, second_feed_two = feed_second(sums_two[:24], *m_feed_two)
    base_mixed_two, second_mixed_two = mixed_second(sums_two[24:], mixed_two, width)
    last_two = Total(jnp.concatenate([second_feed_two, second_mixed_two], axis=0))
    input_gradient = jnp.concatenate(
        [
            back_one[j][2][:step].astype(F32) + after(last_flights[j], send_mixed_one).astype(F32) + norm_one[j][0][:step]
            for j in pair
        ],
        axis=0,
    )
    seconds_two = last_two.rest()
    wide = jnp.concatenate([norm_sums(under, norm_one), norm_sums(top_tail, norm_two)], axis=0)
    wide = total_over(after(wide, send_mixed_one), "mp")
    base_feed_one, second_feed_one = feed_second(sums_feed_one, *m_feed_one)
    base_mixed_one, second_mixed_one = mixed_second(sums_mixed_one, mixed_one, width)
    seconds_one = total_over(jnp.concatenate([second_feed_one, second_mixed_one, wide], axis=0), "dp")
    seconds_feed_one, seconds_mixed_one, wide = seconds_one[:16], seconds_one[16:32], seconds_one[32:].reshape(2, 8, cols)
    gain_sum = jnp.concatenate([wide[:, 3:4], wide[:, 0:1]], axis=1)
    shift_sum = jnp.concatenate([wide[:, 5:6], wide[:, 4:5], wide[:, 2:3], wide[:, 1:2]], axis=1)
    held_feed = feed_error(base_feed_two, seconds_two[:16], *m_feed_two, 1, replicas, None)
    held_mixed = mixed_error(base_mixed_two, seconds_two[16:32], mixed_two, 1, replicas, None)
    new_e_in, new_e_out = feed_error(base_feed_one, seconds_feed_one, *m_feed_one, 0, replicas, held_feed)
    new_e_qkv, new_e_o = mixed_error(base_mixed_one, seconds_mixed_one, mixed_one, 0, replicas, held_mixed)
    member_errors = [flip(new_e_qkv), new_e_o, new_e_in, new_e_out]

    bias_rows = (sums_mixed_one[24], sums_two[48])
    bias_qv = jnp.stack([jnp.stack([row[256 : 256 + width], row[512 : 512 + width]]) for row in bias_rows])
    bias_in = jnp.stack([sums_feed_one[16], sums_two[16]])

    rank = q_in.shape[2]
    kept = []
    for weight, moment in ((w_qkv, m_qkv), (w_o, m_o), (w_in, m_in), (flip(w_out), flip(m_out))):
        kept.extend([weight, moment])
    factors = [(2, 3, rank, cols), (2, rank, width), (2, rank, cols), (2, rank, cols)]
    factors += [(2, 3, rank, width), (2, rank, cols), (2, rank, cols), (2, rank, cols)]
    new_w_qkv, new_m_qkv, new_w_o, new_m_o, new_w_in, new_m_in, new_w_out, new_m_out, *factors = call(
        lambda *refs: renew_kernel(replicas, *refs), [[a.shape, F32] for a in kept] + [[shape, F32] for shape in factors],
        [
            base_feed_one, base_mixed_one, base_feed_two, base_mixed_two,
            seconds_feed_one, seconds_mixed_one, seconds_two, *kept,
        ],
        "renew", 1 << 24, 24, flags, range(7, 15), range(16),
    )
    new_w_out, new_m_out = flip(new_w_out), flip(new_m_out)
    new_m_qv = MOMENTUM * m_qv + bias_qv / replicas
    new_m_bin = MOMENTUM * m_bin + bias_in / replicas
    new_m_gain = MOMENTUM * m_gain + gain_sum / replicas
    new_m_shift = MOMENTUM * m_shift + shift_sum / replicas
    outer = [flip(value) for value in factors[:4]]
    inner = [flip(value) for value in factors[4:]]
    return (
        output, input_gradient, new_w_qkv, new_w_o, new_w_in, new_w_out,
        b_qv - RATE * new_m_qv, b_in - RATE * new_m_bin, ln_gain - RATE * new_m_gain, shifts - RATE * new_m_shift,
        new_m_qkv, new_m_o, new_m_in, new_m_out, new_m_qv, new_m_bin, new_m_gain, new_m_shift,
        *member_errors, *outer, *inner,
    )


def solution(mesh):
    in_specs = (
        P(("dp", "mp"), None), P(("dp", "mp"), None), P("dp", None), P("dp"),
        P(None, None, "dp", "mp"), P(None, "mp", "dp"), P(None, "dp", "mp"), P(None, "mp", "dp"),
        P(None, None, "mp"), P(None, "mp"), P(), P(),
        P(None, None, "dp", "mp"), P(None, "mp", "dp"), P(None, "dp", "mp"), P(None, "mp", "dp"),
        P(None, None, "mp"), P(None, "mp"), P(), P(),
        P("dp", None, None, None, "mp"), P("dp", None, "mp", None), P("dp", None, None, "mp"), P("dp", None, "mp", None),
        P(None, None, "mp", None), P(None, "mp", None), P(None, "mp", None), P(None, "mp", None),
    )
    out_specs = (
        P(("dp", "mp"), None), P(("dp", "mp"), None),
        P(None, None, "dp", "mp"), P(None, "mp", "dp"), P(None, "dp", "mp"), P(None, "mp", "dp"),
        P(None, None, "mp"), P(None, "mp"), P(), P(),
        P(None, None, "dp", "mp"), P(None, "mp", "dp"), P(None, "dp", "mp"), P(None, "mp", "dp"),
        P(None, None, "mp"), P(None, "mp"), P(), P(),
        P("dp", None, None, None, "mp"), P("dp", None, "mp", None), P("dp", None, None, "mp"), P("dp", None, "mp", None),
        P(None, None, "mp", None), P(None, "mp", None), P(None, "mp", None), P(None, "mp", None),
        P(None, None, "mp", None), P(None, "mp", None), P(None, "mp", None), P(None, "mp", None),
    )
    return jax.shard_map(per_device, mesh=mesh, in_specs=in_specs, out_specs=out_specs, check_vma=False)
```

```python
import jax
import jax.numpy as jnp
from jax import lax
from jax.experimental import pallas as pl
from jax.experimental.pallas import tpu as pltpu
from jax.sharding import PartitionSpec as P

HD = 64


NORM_EPS = 1e-05
ORTHO_EPS = 1e-06
MOMENTUM = 0.9
RATE = 0.05
MASKED = -1000000000.0
ROOT_HALF = 0.7071067811865476
INV_ROOT_TWO_PI = 0.3989422804014327
HIGHEST = lax.Precision.HIGHEST
LOW = jnp.bfloat16
F32 = jnp.float32


def dot(left, right, left_dim, right_dim, precision=None):
    return lax.dot_general(
        left,
        right,
        (((left_dim,), (right_dim,)), ((), ())),
        preferred_element_type=F32,
        precision=precision,
    )


def swap(value, axis, bit):
    size = lax.axis_size(axis)
    return lax.ppermute(value, axis, [(i, i ^ bit) for i in range(size)])


def gelu_parts(upper):
    cdf = 0.5 * (1.0 + lax.erf(upper * ROOT_HALF))
    slope = cdf + upper * jnp.exp(-0.5 * upper * upper) * INV_ROOT_TWO_PI
    return upper * cdf, slope


def after(value, *marks):
    return lax.optimization_barrier((value, *marks))[0]


def rows_sum(part, arrived):
    half = part.shape[0] // 2
    part, arrived = part.astype(F32), arrived.astype(F32)
    return jnp.concatenate([part[:half] + arrived[half:], part[half:] + arrived[:half]], axis=0)


def normal(rows_in):
    centred = rows_in - jnp.mean(rows_in, axis=-1, keepdims=True)
    inverse = lax.rsqrt(jnp.mean(centred * centred, axis=-1, keepdims=True) + NORM_EPS)
    return centred * inverse, inverse


def normal_back(grad, normed, inverse, gain):
    scaled = grad * gain
    inner = jnp.mean(scaled * normed, axis=-1, keepdims=True)
    return inverse * (scaled - jnp.mean(scaled, axis=-1, keepdims=True) - normed * inner)


class Arriving:
    def __init__(self, source, local, mark):
        self.local, self.shape, self.dtype, self.waited = local, local.shape, local.dtype, False
        self.copy = pltpu.make_async_copy(source, local, mark)
        self.copy.start()

    def __getitem__(self, index):
        self.settle()
        return self.local[index]

    def settle(self):
        if not self.waited:
            self.copy.wait()
            self.waited = True


class Leaving:
    def __init__(self, target, local, mark):
        self.local, self.shape, self.dtype, self.written = local, local.shape, local.dtype, 0
        self.copy = pltpu.make_async_copy(local, target, mark)

    def __setitem__(self, index, value):
        self.local[index] = value
        self.written += value.size
        if self.written == self.local.size:
            self.copy.start()

    def __getitem__(self, index):
        return self.local[index]

    def settle(self):
        assert self.written == self.local.size
        self.copy.wait()


def call(kernel, outs, args, name, flops, limit=24, scalars=None, far=(), far_outs=()):
    lead = 0 if scalars is None else 1
    inputs, results = len(args), len(outs)
    parts = {i: a[1] for i, a in enumerate(args) if isinstance(a, tuple)}
    kinds = [jax.ShapeDtypeStruct(a[2], a[0].dtype) if isinstance(a, tuple) else a for a in args]
    args = [a[0] if isinstance(a, tuple) else a for a in args]
    args = [pltpu.with_memory_space_constraint(a, pltpu.HBM) if i in far else a for i, a in enumerate(args)]
    moved_in, moved_out = [kinds[i] for i in far], [outs[i] for i in far_outs]

    def body(*refs):
        refs = list(refs)
        scratch = refs[lead + inputs + results :]
        late = []
        for spot, i in enumerate(far):
            source = refs[lead + i].at[parts[i]] if i in parts else refs[lead + i]
            refs[lead + i] = Arriving(source, scratch[spot], scratch[-1].at[spot])
            late.append(refs[lead + i])
        for spot, i in enumerate(far_outs):
            spot += len(far)
            at = lead + inputs + i
            refs[at] = Leaving(refs[at], scratch[spot], scratch[-1].at[spot])
            late.append(refs[at])
        kernel(*refs[: lead + inputs + results])
        for item in late:
            item.settle()

    near = lambda shape: pl.BlockSpec(shape, lambda n=len(shape): (0,) * n)
    elsewhere = pl.BlockSpec(memory_space=pltpu.HBM)
    specs = [elsewhere if i in far else near(a.shape) for i, a in enumerate(args)]
    out_specs = [elsewhere if i in far_outs else near(shape) for i, (shape, _) in enumerate(outs)]
    scratch = [pltpu.VMEM(a.shape, a.dtype) for a in moved_in] + [pltpu.VMEM(shape, kind) for shape, kind in moved_out]
    if scratch:
        scratch.append(pltpu.SemaphoreType.DMA((len(scratch),)))
    operands = list(args)
    if lead:
        specs = [pl.BlockSpec(memory_space=pltpu.SMEM)] + specs
        operands = [scalars] + operands
    shapes = [jax.ShapeDtypeStruct(shape, kind) for shape, kind in outs]
    made = [pltpu.HBM(shape, kind) if i in far_outs else shapes[i] for i, (shape, kind) in enumerate(outs)]
    moved = sum(a.size * a.dtype.itemsize for a in [*kinds, *shapes])
    return pl.pallas_call(
        body,
        in_specs=specs,
        out_specs=out_specs,
        out_shape=made,
        scratch_shapes=scratch,
        cost_estimate=cost(flops, moved),
        compiler_params=params(limit),
        name=name,
    )(*operands)


def join_kernel(order, flags_ref, own_ref, other_ref, q_ref, kv_ref, out_ref):
    width = q_ref.shape[1] // 2
    rows = own_ref.shape[0] // len(order)
    front = flags_ref[0] == 0
    for spot, v in enumerate(order):
        here = slice(spot * rows, (spot + 1) * rows)
        there = here if len(order) == 1 else pl.ds(pl.multiple_of((flags_ref[2] ^ v) * rows, 16), rows)
        groups = []
        for part in range(4):
            lanes = slice(part * width, (part + 1) * width)
            own, other = own_ref[here, lanes].astype(F32), other_ref[here, lanes].astype(F32)
            left, right = jnp.where(front, own, other), jnp.where(front, other, own)
            groups.append(jnp.concatenate([left, right], axis=1).astype(LOW))
        q_ref[there, :] = groups[0]
        kv_ref[there, : 2 * width] = groups[1]
        kv_ref[there, 2 * width :] = groups[2]
        out_ref[there, :] = groups[3]


def project(low, wq_ref, wkv_ref, bias_ref, q_ref, kv_ref):
    width = wq_ref.shape[1]
    q_ref[...] = (dot(low, wq_ref[...], 1, 0) + bias_ref[:, :width]).astype(LOW)
    kv_ref[...] = (dot(low, wkv_ref[...], 1, 0) + bias_ref[:, width:]).astype(LOW)


def project_kernel(x_ref, wq_ref, wkv_ref, bias_ref, q_ref, kv_ref):
    project(x_ref[...], wq_ref, wkv_ref, bias_ref, q_ref, kv_ref)


def first_norm(rows, vec_ref):
    return normal(rows)[0] * vec_ref[0:1, :] + vec_ref[2:3, :]


def second_norm(rows, vec_ref):
    return normal(rows)[0] * vec_ref[1:2, :] + vec_ref[3:4, :]


def norm_project_kernel(
    sent_ref, arrived_ref, rows_ref, vec_ref, wq_ref, wkv_ref, bias_ref, out_ref, low_ref, q_ref, kv_ref
):
    rows = rows_sum(sent_ref[...], arrived_ref[...]) + vec_ref[5:6, :] + first_norm(rows_ref[...], vec_ref)
    out_ref[...] = rows
    low = second_norm(rows, vec_ref).astype(LOW)
    low_ref[...] = low
    project(low, wq_ref, wkv_ref, bias_ref, q_ref, kv_ref)


def pick(flag, first, second):
    return jnp.where(flag, first.astype(F32), second.astype(F32)).astype(LOW)


def attend_kernel(flags_ref, q_ref, k0_ref, k1_ref, k2_ref, k3_ref, place_ref, bound_ref, wo_ref,
                  keep_ref, give_ref, logsum_ref, sent_ref):
    rows, width = q_ref.shape
    pieces = (k0_ref, k1_ref, k2_ref, k3_ref)
    lanes = lax.broadcasted_iota(jnp.int32, (1, 128), 1)
    low, high = bound_ref[:, :1], bound_ref[:, 1:2]
    masks = []
    for index, ref in enumerate(pieces):
        place = place_ref[:, index * ref.shape[0] : (index + 1) * ref.shape[0]]
        masks.append(jnp.where((place >= low) & (place < high), 0.0, MASKED))
    logsums = jnp.zeros((rows, 128), F32)
    tiles = []
    for tile in range(width // 128):
        cols = slice(tile * 128, tile * 128 + 128)
        other = slice(width + tile * 128, width + tile * 128 + 128)
        query = q_ref[:, cols]
        out = None
        for side in range(2):
            here = (lanes >= side * HD) & (lanes < side * HD + HD)
            lone = jnp.where(here, query.astype(F32) * HD ** (-0.5), 0.0).astype(LOW)
            scores = [dot(lone, ref[:, cols], 1, 1) + mask for ref, mask in zip(pieces, masks)]
            highest = jnp.max(scores[0], axis=-1, keepdims=True)
            for score in scores[1:]:
                highest = jnp.maximum(highest, jnp.max(score, axis=-1, keepdims=True))
            powers = [jnp.exp(score - highest) for score in scores]
            total = sum(jnp.sum(power, axis=-1, keepdims=True) for power in powers)
            inverse = 1.0 / total
            head = sum(dot((power * inverse).astype(LOW), ref[:, other], 1, 0) for power, ref in zip(powers, pieces))
            head = jnp.where(here, head, 0.0)
            out = head if out is None else out + head
            logsums = jnp.where(lanes == 2 * tile + side, highest + jnp.log(total), logsums)
        tiles.append(out.astype(LOW))
    logsum_ref[...] = logsums
    mixed = jnp.concatenate(tiles, axis=1)
    half = width // 2
    keep_ref[...] = pick(flags_ref[0] == 0, mixed[:, :half], mixed[:, half:])
    give_ref[...] = pick(flags_ref[0] == 0, mixed[:, half:], mixed[:, :half])
    sent_ref[...] = dot(mixed, wo_ref[...], 1, 1).astype(LOW)


def attend_all_kernel(flags_ref, kinds, *refs):
    pieces, place_ref, wo_ref, rest = refs[:4], refs[4], refs[5], refs[6:]
    chunks = len(rest) // (kinds + 2)
    for j in range(chunks):
        outs = rest[2 * chunks + j * kinds : 2 * chunks + (j + 1) * kinds]
        attend_kernel(flags_ref, rest[j], *pieces, place_ref, rest[chunks + j], wo_ref, *outs)


def attend_back_kernel(first, *refs):
    rows_ref, wo_ref, q_ref, k0_ref, k1_ref, k2_ref, k3_ref, logsum_ref, resid_ref = refs[:9]
    sent_ref, arrived_ref, vec_ref, place_ref, bound_ref = refs[9:14]
    held_refs = () if first else refs[14:18]
    rest_ref, low_ref, norm_sums_ref, dq_ref, *sums_refs = refs[14 + len(held_refs) :]
    grad = rows_sum(sent_ref[...], arrived_ref[...]) + resid_ref[...]
    normed, inverse = normal(rows_ref[...])
    back = normal_back(grad, normed, inverse, vec_ref[0:1, :])
    rest_ref[...] = back
    put_sums(norm_sums_ref, [grad * normed, grad, back], 3)
    low_back = back.astype(LOW)
    low_ref[...] = low_back
    mixed_grad = dot(low_back, wo_ref[...], 1, 0).astype(LOW).astype(F32)
    rows, width = q_ref.shape
    pieces = (k0_ref, k1_ref, k2_ref, k3_ref)
    lanes = lax.broadcasted_iota(jnp.int32, (1, 128), 1)
    low, high = bound_ref[:, :1], bound_ref[:, 1:2]
    scale = HD ** (-0.5)
    masks = []
    for index, ref in enumerate(pieces):
        place = place_ref[:, index * ref.shape[0] : (index + 1) * ref.shape[0]]
        masks.append(jnp.where((place >= low) & (place < high), 0.0, MASKED))
    for tile in range(width // 128):
        cols = slice(tile * 128, tile * 128 + 128)
        other = slice(width + tile * 128, width + tile * 128 + 128)
        query, grad = q_ref[:, cols].astype(F32), mixed_grad[:, cols]
        dq = None
        dk, dv = [None] * 4, [None] * 4
        for side in range(2):
            here = (lanes >= side * HD) & (lanes < side * HD + HD)
            lone = jnp.where(here, query * scale, 0.0).astype(LOW)
            lone_grad = jnp.where(here, grad, 0.0).astype(LOW)
            logsum = jnp.sum(jnp.where(lanes == 2 * tile + side, logsum_ref[...], 0.0), axis=-1, keepdims=True)
            probs, prob_grads = [], []
            inner = None
            for ref, mask in zip(pieces, masks):
                prob = jnp.exp(dot(lone, ref[:, cols], 1, 1) + mask - logsum)
                prob_grad = dot(lone_grad, ref[:, other], 1, 1)
                probs.append(prob)
                prob_grads.append(prob_grad)
                piece = jnp.sum(prob * prob_grad, axis=-1, keepdims=True)
                inner = piece if inner is None else inner + piece
            for index, ref in enumerate(pieces):
                score = (probs[index] * (prob_grads[index] - inner)).astype(LOW)
                back = dot(score, ref[:, cols], 1, 0)
                back = jnp.where(here, back * scale, 0.0)
                dq = back if dq is None else dq + back
                key = dot(score, lone, 0, 0)
                value = dot(probs[index].astype(LOW), lone_grad, 0, 0)
                dk[index] = key if dk[index] is None else dk[index] + key
                dv[index] = value if dv[index] is None else dv[index] + value
        dq_ref[:, cols] = dq.astype(LOW)
        for index in range(4):
            key, value = dk[index], dv[index]
            if held_refs:
                key = key + held_refs[index][:, cols]
                value = value + held_refs[index][:, other]
            sums_refs[index][:, cols] = key.astype(sums_refs[index].dtype)
            sums_refs[index][:, other] = value.astype(sums_refs[index].dtype)


def feed_kernel(is_first, sent_ref, arrived_ref, resid_ref, vec_ref, before_ref, feed0_ref, feed1_ref, bias_ref,
                rows_ref, give_ref, act_ref, slope_ref, out_ref):
    resid = resid_ref[...].astype(F32) if is_first else second_norm(resid_ref[...], before_ref)
    rows = rows_sum(sent_ref[...], arrived_ref[...]) + vec_ref[4:5, :] + resid
    rows_ref[...] = rows
    low = first_norm(rows, vec_ref).astype(LOW)
    cols = low.shape[1]
    units = feed0_ref.shape[0]
    top = feed0_ref.shape[1] - units
    base = top - units
    give_ref[:, :cols] = low
    act, slope = gelu_parts(dot(low, feed0_ref[:, base:top], 1, 0) + bias_ref[0:1, :])
    act = act.astype(LOW)
    act_ref[...] = act
    slope_ref[:, :units] = slope.astype(LOW)
    part = dot(act, feed0_ref[:, top:], 1, 1)
    act, slope = gelu_parts(dot(low, feed1_ref[:, base:top], 1, 0) + bias_ref[1:2, :])
    act = act.astype(LOW)
    give_ref[:, cols:] = act
    slope_ref[:, units:] = slope.astype(LOW)
    out_ref[...] = (part + dot(act, feed1_ref[:, top:], 1, 1)).astype(LOW)


def put_sums(sums_ref, lists, start):
    half = lists[0].shape[0] // 2
    sums_ref[...] = jnp.zeros(sums_ref.shape, F32)
    for index, rows in enumerate(lists):
        sums_ref[start + index : start + index + 1, :] = jnp.sum(rows[:half], axis=0, keepdims=True)


def back_feed(grad, normed, inverse, gain, slope_ref, feed0_ref, feed1_ref, rest_ref, give_ref, keep_ref, out_ref, sums_ref):
    back = normal_back(grad, normed, inverse, gain)
    rest_ref[...] = back
    put_sums(sums_ref, [grad * normed, grad, back], 0)
    low = back.astype(LOW)
    cols = low.shape[1]
    units = feed0_ref.shape[0]
    top = feed0_ref.shape[1] - units
    base = top - units
    give_ref[:, :cols] = low
    upper = (dot(low, feed0_ref[:, top:], 1, 0) * slope_ref[:, :units].astype(F32)).astype(LOW)
    keep_ref[...] = upper
    part = dot(upper, feed0_ref[:, base:top], 1, 1)
    upper = (dot(low, feed1_ref[:, top:], 1, 0) * slope_ref[:, units:].astype(F32)).astype(LOW)
    give_ref[:, cols:] = upper
    out_ref[...] = (part + dot(upper, feed1_ref[:, base:top], 1, 1)).astype(LOW)


def top_kernel(flags_ref, sent_ref, arrived_ref, rows_ref, grad_ref, before_rows_ref, before_ref, vec_ref, slope_ref,
               feed0_ref, feed1_ref, y_ref, rest_ref, give_ref, keep_ref, out_ref, sums_ref):
    rows = rows_sum(sent_ref[...], arrived_ref[...]) + vec_ref[5:6, :] + first_norm(rows_ref[...], vec_ref)
    normed, inverse = normal(rows)
    half = normed.shape[0] // 2
    y = normed[:half] * vec_ref[1:2, :] + vec_ref[3:4, :]
    on = flags_ref[1] > 0
    y_ref[...] = jnp.where(on, y, second_norm(before_rows_ref[:half, :], before_ref))
    grad = jnp.where(on, grad_ref[...].astype(F32), 0.0)
    back_feed(grad, normed, inverse, vec_ref[1:2, :], slope_ref, feed0_ref, feed1_ref,
              rest_ref, give_ref, keep_ref, out_ref, sums_ref)


def under_kernel(flags_ref, sent_ref, arrived_ref, resid_ref, grad_ref, rows_ref, vec_ref, slope_ref,
                 feed0_ref, feed1_ref, rest_ref, give_ref, keep_ref, out_ref, sums_ref):
    grad = rows_sum(sent_ref[...], arrived_ref[...]) + resid_ref[...]
    grad = jnp.where(flags_ref[1] > 0, grad, grad_ref[...].astype(F32))
    normed, inverse = normal(rows_ref[...])
    back_feed(grad, normed, inverse, vec_ref[1:2, :], slope_ref, feed0_ref, feed1_ref,
              rest_ref, give_ref, keep_ref, out_ref, sums_ref)


def renew_kernel(replicas, flags_ref, *refs):
    bases, seconds, state, outs = refs[:4], refs[4:7], refs[7:15], refs[15:]
    rows = state[2].shape[2]
    cols = bases[0].shape[1]
    pick_rows = lax.broadcasted_iota(jnp.int32, (cols, rows), 0)
    pick_cols = lax.broadcasted_iota(jnp.int32, (cols, rows), 1)
    chosen = jnp.where(pick_rows == pick_cols + flags_ref[2] * rows, 1.0, 0.0).astype(LOW)

    def part(value):
        high, rest = split(value)
        return dot(high, chosen, 1, 0) + dot(rest, chosen, 1, 0)

    def write(index, spot, update):
        weight, moment = state[2 * index], state[2 * index + 1]
        fresh = MOMENTUM * moment[spot] + update
        outs[2 * index + 1][spot] = fresh
        outs[2 * index][spot] = weight[spot] - RATE * fresh

    for layer in range(2):
        base_feed, base_mixed = bases[2 * layer][...], bases[2 * layer + 1][...]
        width = state[2].shape[1]
        scale = 1.0 / replicas
        if layer == 0:
            feed, mixed = seconds[0][...], seconds[1][...]
        else:
            feed, mixed = seconds[2][:16, :], seconds[2][16:, :]
        for member in range(3):
            outs[8][(layer, member)] = base_mixed[8 * member : 8 * member + 8]
            outs[12][(layer, member)] = mixed[:8, 256 * member : 256 * member + width]
        outs[9][(layer,)] = base_mixed[24:32, :width]
        outs[13][(layer,)] = mixed[8:]
        for member in range(2):
            outs[10 + member][(layer,)] = base_feed[8 * member : 8 * member + 8]
            outs[14 + member][(layer,)] = feed[8 * member : 8 * member + 8]
        feed, mixed = feed * scale, mixed * scale
        for member in range(3):
            update = low_rank(part(base_mixed[8 * member : 8 * member + 8]), mixed[:8, 256 * member : 256 * member + width])
            write(0, (layer, member), update)
        write(1, (layer,), low_rank(base_mixed[24:32, :width], part(mixed[8:])))
        write(2, (layer,), low_rank(part(base_feed[:8]), feed[:8]))
        write(3, (layer,), low_rank(part(feed[8:]), base_feed[8:16]))


def back_project_kernel(flags_ref, dq_ref, own_ref, arrived_ref, wq_ref, wkv_ref, keep_ref, give_ref, sent_ref):
    dq = dq_ref[...]
    dkv = (own_ref[...] + arrived_ref[...].astype(F32)).astype(LOW)
    sent_ref[...] = (dot(dq, wq_ref[...], 1, 1) + dot(dkv, wkv_ref[...], 1, 1)).astype(LOW)
    half = dq.shape[1] // 2
    groups = (dq, dkv[:, : 2 * half], dkv[:, 2 * half :])
    front = flags_ref[0] == 0
    keep_ref[...] = jnp.concatenate([pick(front, g[:, :half], g[:, half:]) for g in groups], axis=1)
    give_ref[...] = jnp.concatenate([pick(front, g[:, half:], g[:, :half]) for g in groups], axis=1)

def split(value):
    high = value.astype(LOW)
    return high, (value - high.astype(F32)).astype(LOW)


def split_dot(small, large, small_dim, large_dim):
    high, rest = split(large)
    lead, tail = split(small)
    rows = small.shape[0]
    both = dot(jnp.concatenate([lead, tail], axis=0), high, small_dim, large_dim)
    return both[:rows] + both[rows:] + dot(lead, rest, small_dim, large_dim)


def dot_chunks(lefts, rights):
    total = None
    for left, right in zip(lefts, rights):
        part = dot(left[...], right[...], 0, 0)
        total = part if total is None else total + part
    return total


def rows_total_kernel(chunks, *refs):
    lefts, rights = refs[:chunks], refs[chunks : 2 * chunks]
    error_ref, start_ref, total_ref, first_ref, bias_ref = refs[2 * chunks :]
    total = dot_chunks(lefts, rights) + error_ref[...]
    total_ref[...] = total
    first_ref[...] = split_dot(start_ref[...], total, 1, 1)

    @pl.when(pl.program_id(0) == 0)
    def _():
        bias = sum(jnp.sum(ref[...].astype(F32), axis=0, keepdims=True) for ref in rights)
        bias_ref[...] = jnp.concatenate([bias, jnp.zeros((7, bias.shape[1]), F32)], axis=0)


def params(limit, **more):
    return pltpu.CompilerParams(vmem_limit_bytes=limit << 20, **more)


def cost(flops, moved):
    return pl.CostEstimate(flops=int(flops), bytes_accessed=int(moved), transcendentals=0)


def rows_total(lefts, rights, errors, starts, layer):
    rows, cols = errors.shape[-2:]
    tokens = lefts[0][0].shape[0]
    rank = starts.shape[1]
    step = 256
    chunks = len(lefts)
    return pl.pallas_call(
        lambda *refs: rows_total_kernel(chunks, *refs),
        grid=(rows // step,),
        in_specs=[pl.BlockSpec((tokens, step), lambda i, at=at: (0, i + at * (rows // step))) for _, at in lefts]
        + [pl.BlockSpec((tokens, cols), lambda i, at=at: (0, at)) for _, at in rights]
        + [
            pl.BlockSpec((None, None, step, cols), lambda i: (0, layer, i, 0)),
            pl.BlockSpec((None, rank, cols), lambda i: (layer, 0, 0)),
        ],
        out_specs=[
            pl.BlockSpec((step, cols), lambda i: (i, 0)),
            pl.BlockSpec((rank, step), lambda i: (0, i)),
            pl.BlockSpec((rank, cols), lambda i: (0, 0)),
        ],
        out_shape=[
            jax.ShapeDtypeStruct((rows, cols), F32),
            jax.ShapeDtypeStruct((rank, rows), F32),
            jax.ShapeDtypeStruct((rank, cols), F32),
        ],
        cost_estimate=cost(2 * chunks * tokens * rows * cols, 8 * rows * cols + 4 * chunks * tokens * rows),
        compiler_params=params(24),
        name="rows_total",
    )(*[array for array, _ in lefts], *[array for array, _ in rights], errors, starts)


def mixed_total_kernel(chunks, *refs):
    proj_refs, whole_refs = refs[:chunks], refs[chunks : 2 * chunks]
    attended_refs, piece_refs = refs[2 * chunks : 3 * chunks], refs[3 * chunks : 4 * chunks]
    e_proj_ref, e_back_ref, s_proj_ref, s_back_ref, total_ref, first_ref = refs[4 * chunks :]
    width = e_back_ref.shape[0]
    grads = dot_chunks(proj_refs, whole_refs)
    for member in range(3):
        rows = slice(member * width, (member + 1) * width)
        total = grads[rows] + e_proj_ref[member]
        total_ref[rows, :] = total
        first_ref[8 * member : 8 * member + 8, :] = split_dot(s_proj_ref[member], total, 1, 0)
    total = dot_chunks(attended_refs, piece_refs) + e_back_ref[...]
    total_ref[3 * width :, :] = total
    first_ref[24:, :] = jnp.zeros((8, total.shape[1]), F32)
    first_ref[24:, :width] = split_dot(s_back_ref[...], total, 1, 1)
    sums = sum(jnp.sum(ref[...].astype(F32), axis=0, keepdims=True) for ref in proj_refs)
    first_ref[24:25, 256 : 256 + width] = sums[:, :width]
    first_ref[24:25, 512 : 512 + width] = sums[:, 2 * width :]


def mixed_total(proj_low, whole_in, attended, piece, e_proj, e_back, s_proj, s_back, layer):
    tokens, width = attended[0].shape
    cols = whole_in[0].shape[1]
    rank = s_back.shape[1]
    chunks = len(attended)
    args = [*proj_low, *whole_in, *attended, *piece, (e_proj, (0, layer), e_proj.shape[2:]), (e_back, (0, layer), e_back.shape[2:]), s_proj[layer], s_back[layer]]
    return call(
        lambda *refs: mixed_total_kernel(chunks, *refs),
        [[(4 * width, cols), F32], [(4 * rank, cols), F32]],
        args, "mixed_total", 2 * chunks * tokens * 4 * width * cols, 24, None, range(4 * chunks + 2),
    )


def ortho_rows(factor):
    rank = factor.shape[0]
    index = lax.broadcasted_iota(jnp.int32, (rank, 1), 0)
    for row in range(rank):
        vector = factor[row : row + 1, :]
        inner = jnp.sum(factor * vector, axis=1, keepdims=True)
        scale = lax.rsqrt(inner[row : row + 1] + ORTHO_EPS)
        vector = vector * scale
        factor = jnp.where(
            index < row, factor, jnp.where(index == row, vector, factor - vector * (inner * scale))
        )
    return factor


def feed_second_kernel(sums_ref, up_ref, down_ref, base_ref, second_ref):
    for member, total_ref in enumerate((up_ref, down_ref)):
        rows = slice(8 * member, 8 * member + 8)
        base = ortho_rows(sums_ref[rows, :])
        base_ref[rows, :] = base
        second_ref[rows, :] = split_dot(base, total_ref[...], 1, 0)


def feed_second(sums, m_up, m_down):
    cols = m_up.shape[1]
    return pl.pallas_call(
        feed_second_kernel,
        out_shape=[jax.ShapeDtypeStruct((16, cols), F32)] * 2,
        cost_estimate=cost(96 * m_up.size, 8 * m_up.size),
        compiler_params=params(24),
        name="feed_second",
    )(sums, m_up, m_down)


def mixed_second_kernel(width, sums_ref, total_ref, base_ref, second_ref):
    second_ref[...] = jnp.zeros(second_ref.shape, F32)
    for member in range(3):
        rows = slice(8 * member, 8 * member + 8)
        base = ortho_rows(sums_ref[rows, :])
        base_ref[rows, :] = base
        second_ref[:8, 256 * member : 256 * member + width] = split_dot(
            base, total_ref[member * width : (member + 1) * width, :], 1, 1
        )
    base = ortho_rows(sums_ref[24:32, :width])
    base_ref[24:32, :width] = base
    second_ref[8:, :] = split_dot(base, total_ref[3 * width :, :], 1, 0)


def mixed_second(sums, m_mixed, width):
    cols = m_mixed.shape[1]
    return pl.pallas_call(
        lambda *refs: mixed_second_kernel(width, *refs),
        out_shape=[jax.ShapeDtypeStruct((32, cols), F32), jax.ShapeDtypeStruct((16, cols), F32)],
        cost_estimate=cost(48 * m_mixed.size, 4 * m_mixed.size),
        compiler_params=params(16),
        name="mixed_second",
    )(sums, m_mixed)


def low_rank(base, second):
    b_high, b_rest = split(base)
    s_high, s_rest = split(second)
    left = jnp.concatenate([b_high, b_rest, b_high], axis=0)
    right = jnp.concatenate([s_high, s_high, s_rest], axis=0)
    return dot(left, right, 0, 0)


def feed_error_kernel(layer, replicas, base_ref, second_ref, up_ref, down_ref, *refs):
    up_out, down_out = refs[-2:]
    seconds = second_ref[...] * (1.0 / replicas)
    up_out[...] = up_ref[...] - low_rank(base_ref[:8, :], seconds[:8])
    down_out[...] = down_ref[...] - low_rank(base_ref[8:16, :], seconds[8:16])


def feed_error(base, second, m_up, m_down, layer, replicas, held):
    rows, cols = m_up.shape
    rank2 = base.shape[0]
    step = 256
    shape = jax.ShapeDtypeStruct((1, 2, rows, cols), F32)
    out_spec = pl.BlockSpec((None, None, step, cols), lambda i: (0, layer, i, 0))
    extra = {} if held is None else {"input_output_aliases": {4: 0, 5: 1}}
    return pl.pallas_call(
        lambda *refs: feed_error_kernel(layer, replicas, *refs),
        grid=(rows // step,),
        in_specs=[
            pl.BlockSpec((rank2, step), lambda i: (0, i)),
            pl.BlockSpec((rank2, cols), lambda i: (0, 0)),
            pl.BlockSpec((step, cols), lambda i: (i, 0)),
            pl.BlockSpec((step, cols), lambda i: (i, 0)),
        ] + ([] if held is None else [pl.BlockSpec(memory_space=pl.ANY)] * 2),
        out_specs=[out_spec, out_spec],
        out_shape=[shape, shape],
        cost_estimate=cost(100 * m_up.size, 16 * m_up.size),
        compiler_params=params(16),
        name="feed_error",
        **extra,
    )(base, second, m_up, m_down, *(() if held is None else held))


def mixed_error_kernel(replicas, base_ref, second_ref, total_ref, *refs):
    proj_out, back_out = refs[-2:]
    width = back_out.shape[0]
    seconds = second_ref[...] * (1.0 / replicas)
    for member in range(3):
        approx = low_rank(seconds[:8, 256 * member : 256 * member + width], base_ref[8 * member : 8 * member + 8, :])
        proj_out[member] = total_ref[member * width : (member + 1) * width, :] - approx
    back_out[...] = total_ref[3 * width :, :] - low_rank(base_ref[24:32, :width], seconds[8:])


def mixed_error(base, second, m_mixed, layer, replicas, held):
    rows, cols = m_mixed.shape
    width = rows // 4
    extra = {} if held is None else {"input_output_aliases": {3: 0, 4: 1}}
    return pl.pallas_call(
        lambda *refs: mixed_error_kernel(replicas, *refs),
        grid=(1,),
        in_specs=[
            pl.BlockSpec(base.shape, lambda i: (0, 0)),
            pl.BlockSpec(second.shape, lambda i: (0, 0)),
            pl.BlockSpec((rows, cols), lambda i: (0, 0)),
        ] + ([] if held is None else [pl.BlockSpec(memory_space=pl.ANY)] * 2),
        out_specs=[
            pl.BlockSpec((None, None, 3, width, cols), lambda i: (0, layer, 0, 0, 0)),
            pl.BlockSpec((None, None, width, cols), lambda i: (0, layer, 0, 0)),
        ],
        out_shape=[
            jax.ShapeDtypeStruct((1, 2, 3, width, cols), F32), jax.ShapeDtypeStruct((1, 2, width, cols), F32)
        ],
        cost_estimate=cost(50 * m_mixed.size, 8 * m_mixed.size),
        compiler_params=params(24),
        name="mixed_error",
        **extra,
    )(base, second, m_mixed, *(() if held is None else held))


def flip(value):
    return jnp.swapaxes(value, -1, -2)


def per_device(
    x_in, out_grad, doc_lengths, keep_layer, w_qkv, w_o, w_in, w_out, b_qv, b_in, ln_gain, shifts,
    m_qkv, m_o, m_in, m_out, m_qv, m_bin, m_gain, m_shift, e_qkv, e_o, e_in, e_out, q_qkv, q_o, q_in, q_out,
):
    own_rows, cols = x_in.shape
    replicas = lax.axis_size("dp")
    index = lax.axis_index("dp")
    place = lax.axis_index("mp")
    width = w_o.shape[1]
    front = lax.rem(place, 2) == 0
    flags = jnp.stack([lax.rem(place, 2), keep_layer[0], index]).astype(jnp.int32)
    chunks = 2
    step = own_rows // chunks
    size = 2 * step
    pair = range(chunks)

    def core(value):
        return swap(value, "mp", 1)

    def chip(value):
        return swap(value, "mp", 2)

    def gather(piece):
        return lax.all_gather(piece, "dp", axis=0, tiled=True)

    def join(own, other, axis):
        return jnp.where(
            front, jnp.concatenate([own, other], axis=axis), jnp.concatenate([other, own], axis=axis)
        )

    def mixed_piece(layer):
        return jnp.concatenate(
            [w_qkv[layer, 0], w_qkv[layer, 1], w_qkv[layer, 2], flip(w_o[layer])], axis=1
        ).astype(LOW)

    def feed_piece(layer):
        return jnp.concatenate([w_in[layer], flip(w_out[layer])], axis=1).astype(LOW)

    def by_chunk(rows, arrived):
        return [
            jnp.concatenate([rows[j * step : (j + 1) * step], arrived[j * step : (j + 1) * step]], axis=0) for j in pair
        ]

    small = jnp.concatenate([b_qv.reshape(-1), b_in.reshape(-1)]).reshape(-1, 128)
    small = core(small).reshape(-1)
    other_qv = small[: b_qv.size].reshape(b_qv.shape)
    other_in = small[b_qv.size :].reshape(b_in.shape)

    ends = jnp.sum(
        jnp.where(
            jnp.arange(doc_lengths.shape[1])[:, None] <= jnp.arange(doc_lengths.shape[1])[None, :],
            doc_lengths[0][:, None], 0,
        ),
        axis=0,
    )

    def places_of(device, j):
        steps = jnp.arange(step, dtype=jnp.int32) + j * step
        return jnp.concatenate([device * own_rows + steps, (device ^ 2) * own_rows + steps])

    mine = [places_of(place, j) for j in pair]
    all_places = jnp.concatenate(mine + [places_of(place ^ 1, j) for j in pair])[None, :]

    def bounds_of(places):
        passed = places[:, None] >= ends[None, :]
        low = jnp.max(jnp.where(passed, ends[None, :], 0), axis=1)
        high = jnp.min(jnp.where(passed, 1 << 30, ends[None, :]), axis=1)
        return jnp.stack([low, high], axis=1)

    bounds = [bounds_of(places) for places in mine]

    vecs, feeds, proj_bias, feed_bias = [], [], [], []
    for layer in range(2):
        gain, shift = ln_gain[layer], shifts[layer]
        vecs.append(
            jnp.concatenate(
                [gain, shift[1:2], shift[3:4], shift[0:1], shift[2:3], jnp.zeros((2, cols), F32)], axis=0
            )
        )
        proj_bias.append(
            jnp.concatenate(
                [
                    join(b_qv[layer, 0], other_qv[layer, 0], 0),
                    jnp.zeros((2 * width,), F32),
                    join(b_qv[layer, 1], other_qv[layer, 1], 0),
                ]
            )[None]
        )
        feed_bias.append(jnp.stack([b_in[layer], other_in[layer]]))

    set_in = by_chunk(x_in, chip(x_in))
    order = [0]
    bits = [4, 2, 1] if replicas == 8 else []
    for bit in bits:
        order = order + [v ^ bit for v in order]
    if not bits:
        order = order[:1]

    def doubled(piece, bit):
        return jnp.concatenate([piece, swap(piece, "dp", bit)], axis=0)

    feed_whole = jnp.concatenate([mixed_piece(1), feed_piece(0)], axis=1)
    whole_mixed = mixed_piece(0)
    if bits:
        feed_whole = gather(feed_whole)
        set_grad = by_chunk(out_grad, chip(after(out_grad, *set_in)))
        whole_mixed = doubled(doubled(whole_mixed, 4), 2)
        whole_mixed, all_places, flags, *rest = lax.optimization_barrier(
            (whole_mixed, all_places, flags, *bounds, *vecs, *proj_bias, *feed_bias, *set_in, *set_grad)
        )
        bounds, vecs, proj_bias, feed_bias = rest[:2], rest[2:4], rest[4:6], rest[6:8]
        set_in, set_grad = rest[8:10], rest[10:12]
        whole_mixed = doubled(whole_mixed, 1)
    else:
        set_grad = by_chunk(out_grad, chip(out_grad))
        whole_mixed = gather(whole_mixed)
        feed_whole = gather(feed_whole)
    feed_late, *set_in = lax.optimization_barrier((feed_piece(1), *set_in))
    feed_late = gather(feed_late)
    whole_other = [core(rows) for rows in set_in]

    full = [(size, cols), F32]
    full_low = [(size, cols), LOW]
    thin = [(size, 128), F32]
    half_low = [(size, 2 * width), LOW]
    one_low = [(size, width), LOW]
    kv_low = [(size, 4 * width), LOW]
    units = cols

    def mixed_weights(own, other, order):
        return call(
            lambda *refs: join_kernel(order, *refs), [[(cols, 2 * width), LOW], [(cols, 4 * width), LOW], [(cols, 2 * width), LOW]],
            [(own, (slice(None), pl.ds(0, cols)), (cols, cols)), (other, (slice(None), pl.ds(0, cols)), (cols, cols))],
            "join", 0, 16, flags, (0, 1), (0, 1, 2),
        )

    def attention(layer, q, kv):
        pieces = kv + [core(part) for part in kv]
        kinds = [one_low, one_low, thin, full_low]
        outs = call(
            lambda flags_ref, *refs: attend_all_kernel(flags_ref, len(kinds), *refs), kinds * chunks,
            [*pieces, all_places, wo[layer], *q, *bounds], "attend",
            chunks * (2 * size * (4 * size) * 4 * width + 2 * size * 2 * width * cols), 20, flags, (6, 7, 0, 1, 2, 3, 5), (0, 1, 2, 4, 5, 6),
        )
        return pieces, [outs[j * len(kinds) : (j + 1) * len(kinds)] for j in pair]

    def feed_all(layer, outs, resid):
        return [
            call(
                lambda *refs: feed_kernel(layer == 0, *refs),
                [full, [(size, cols + units), LOW], [(size, units), LOW], [(size, 2 * units), LOW], full_low],
                [outs[j][3], chip(outs[j][3]), resid[j], vecs[layer], vecs[0], *feeds[layer], feed_bias[layer]],
                "feed", 8 * size * cols * units, 26, None, (2, 5, 6), (0, 1, 2, 3),
            )
            for j in pair
        ]

    e_proj, s_proj = flip(e_qkv), flip(q_qkv)
    e_proj, e_back, e_up, e_down = (
        pltpu.with_memory_space_constraint(value, pltpu.HBM) for value in (e_proj, e_o, e_in, e_out)
    )
    s_back, s_up, s_down = flip(q_o), flip(q_in), flip(q_out)

    def feed_up(layer, feed_out, tails, start):
        give_up = [out[1] for out in feed_out]
        give_down = [out[1] for out in tails]
        return rows_total(
            [(rows, 0) for rows in give_up + [core(rows) for rows in give_up]],
            [(out[2], 0) for out in tails] + [(core(rows), 1) for rows in give_down], e_up, start, layer,
        )

    def feed_down(layer, feed_out, tails, start):
        give_up = [out[1] for out in feed_out]
        give_down = [out[1] for out in tails]
        return rows_total(
            [(out[2], 0) for out in feed_out] + [(core(rows), 1) for rows in give_up],
            [(rows, 0) for rows in give_down + [core(rows) for rows in give_down]], e_down, start, layer,
        )

    def mixed_first(layer, low, back, mixed, norm, start):
        return mixed_total(
            [out[0] for out in back] + [core(out[1]) for out in back],
            low,
            [out[0] for out in mixed] + [core(out[1]) for out in mixed],
            [out[1] for out in norm] + [core(out[1]) for out in norm],
            e_proj, e_back, s_proj, start, layer,
        )

    def total_over(value, axis):
        bit = 1
        while bit < lax.axis_size(axis):
            value = value + swap(value, axis, bit)
            bit = 2 * bit
        return value

    class Total:
        def __init__(self, value):
            self.value, self.bit = value, 1

        def step(self, *marks):
            if self.bit < replicas:
                self.value = self.value + after(swap(self.value, "dp", self.bit), *marks)
                self.bit = 2 * self.bit

        def rest(self):
            while self.bit < replicas:
                self.value = self.value + swap(self.value, "dp", self.bit)
                self.bit = 2 * self.bit
            return self.value

    def norm_sums(tails, norm):
        return sum(out[4] for out in tails) + sum(out[3] for out in norm)

    wq, wkv, wo = ([part] for part in mixed_weights(whole_mixed, core(whole_mixed), order))
    first = [
        call(
            project_kernel, [half_low, kv_low], [set_in[j], wq[0], wkv[0], proj_bias[0]],
            "project", 2 * size * cols * 6 * width, 10, None, (1, 2), (0, 1),
        )
        for j in pair
    ]
    q_one = [out[0] for out in first]
    pieces_one, mixed_out_one = attention(0, q_one, [out[1] for out in first])
    feed_whole = after(feed_whole, mixed_out_one[0][3])
    other_whole = core(feed_whole)
    spot = ((slice(None), pl.ds(cols, 2 * cols)), (cols, 2 * cols))
    feeds.append(((feed_whole, *spot), (other_whole, *spot)))
    feed_out_one = feed_all(0, mixed_out_one, set_in)
    own_late = after(feed_whole, feed_out_one[1][4])
    for held, part in zip((wq, wkv, wo), mixed_weights(own_late, other_whole, [0])):
        held.append(part)
    second = [
        call(
            norm_project_kernel, [full, full_low, half_low, kv_low],
            [feed_out_one[j][4], chip(feed_out_one[j][4]), feed_out_one[j][0], vecs[0], wq[1], wkv[1], proj_bias[1]],
            "norm_project", 2 * size * cols * 6 * width, 12, None, (2, 4, 5), (0, 1, 2, 3),
        )
        for j in pair
    ]
    q_two = [out[2] for out in second]
    pieces_two, mixed_out_two = attention(1, q_two, [out[3] for out in second])
    feed_late = after(feed_late, mixed_out_two[1][3])
    other_late = core(feed_late)
    feeds.append((feed_late, other_late))
    feed_out_two = feed_all(1, mixed_out_two, [out[0] for out in second])

    wide_outs = [full, [(size, cols + units), LOW], [(size, units), LOW], full_low, [(8, cols), F32]]
    top = [
        call(
            top_kernel, [[(step, cols), F32]] + wide_outs,
            [
                feed_out_two[j][4], chip(feed_out_two[j][4]), feed_out_two[j][0], set_grad[j], second[j][0], vecs[0],
                vecs[1], feed_out_two[j][3], *feeds[1],
            ],
            "top", 8 * size * cols * units, 28, flags, (2, 3, 4, 8, 9, 7), (0, 1, 2, 3),
        )
        for j in pair
    ]
    output = jnp.concatenate([out[0] for out in top], axis=0)

    def attention_back(layer, outs, feed_out, q, pieces, mixed, vec, between, ending):
        held, dqs, norms = [], [], []
        for j in pair:
            kinds = [full] * 4 if j + 1 < chunks else [full, full, full_low, full_low]
            rest, low, sums, dq, *held = call(
                lambda *refs, j=j: attend_back_kernel(j == 0, *refs),
                [full, full_low, [(8, cols), F32], half_low] + kinds,
                [
                    feed_out[j][0], wo[layer], q[j], *pieces, mixed[j][2], outs[j][0],
                    outs[j][3], chip(outs[j][3]), vec, all_places, bounds[j], *held,
                ],
                "attend_back", 5 * size * (4 * size) * 4 * width, 28, None, (8, 0, 1, 2, 3, 4, 5, 6, 7), (0, 1, 3) if j + 1 < chunks else (0, 1, 3, 4, 5),
            )
            dqs.append(dq)
            norms.append((rest, low, None, sums))
            if j == 0:
                vec = between(vec, sums)
        back_flags = ending(flags, sums)
        return norms, [
            call(
                back_project_kernel, [[(size, 3 * width), LOW], [(size, 3 * width), LOW], full_low],
                [dqs[j], held[j], core(held[2 + j]), wq[layer], wkv[layer]], "back_project",
                2 * size * cols * 6 * width, 16, back_flags, (0, 3, 1, 4), (0, 1),
            )
            for j in pair
        ]

    top_tail = [out[1:] for out in top]
    feed_two_up = feed_up(1, feed_out_two, top_tail, after(s_up, top[1][5]))
    norm_two, back_two = attention_back(
        1, top_tail, feed_out_two, q_two, pieces_two, mixed_out_two, after(vecs[1], feed_two_up[1]),
        lambda vec, sums: vec, lambda flags, sums: flags,
    )
    sent = back_two[1][2]
    feed_two_down = feed_down(1, feed_out_two, top_tail, after(s_down, sent))
    low_two = [out[1] for out in second]
    mixed_two, send_mixed_two = mixed_first(
        1, low_two + [core(rows) for rows in low_two], back_two, mixed_out_two, norm_two, after(s_back, sent)
    )
    total_two = Total(jnp.concatenate([feed_two_up[1], feed_two_down[1], feed_two_up[2], send_mixed_two], axis=0))
    under, under_flags = [], after(flags, feed_two_down[1], send_mixed_two)
    for j in pair:
        under.append(
            call(
                under_kernel, wide_outs,
                [
                    back_two[j][2], chip(back_two[j][2]), norm_two[j][0], set_grad[j], second[j][0],
                    vecs[0], feed_out_one[j][3], *feeds[0],
                ],
                "under", 8 * size * cols * units, 28, under_flags, (2, 3, 4, 7, 8, 6), (0, 1, 2),
            )
        )
    feed_one_up = feed_up(0, feed_out_one, under, after(s_up, under[1][4]))
    feed_one_down = feed_down(0, feed_out_one, under, after(s_down, under[1][4]))
    m_feed_one, m_feed_two = (feed_one_up[0], feed_one_down[0]), (feed_two_up[0], feed_two_down[0])

    total_two.step(feed_one_up[1], feed_one_down[1])

    def between(vec, sums):
        total_two.step(sums)
        return after(vec, total_two.value)

    def ending(flags, sums):
        return after(flags, total_two.value)

    norm_one, back_one = attention_back(
        0, under, feed_out_one, q_one, pieces_one, mixed_out_one,
        after(vecs[0], feed_one_up[1], feed_one_down[1]), between, ending,
    )
    last_flights = [chip(out[2][step:]) for out in back_one]

    sents = [out[2] for out in back_one]
    mixed_one, send_mixed_one = mixed_first(
        0, set_in + whole_other, back_one, mixed_out_one, norm_one, s_back
    )
    total_one = jnp.concatenate([feed_one_up[1], feed_one_down[1], feed_one_up[2], send_mixed_one], axis=0)
    sums_one = total_over(total_one, "dp")
    sums_feed_one, sums_mixed_one = sums_one[:24], sums_one[24:]
    total_two.step(send_mixed_one)
    sums_two = after(total_two.rest(), send_mixed_one)
    base_feed_two, second_feed_two = feed_second(sums_two[:24], *m_feed_two)
    base_mixed_two, second_mixed_two = mixed_second(sums_two[24:], mixed_two, width)
    wide = jnp.concatenate([norm_sums(under, norm_one), norm_sums(top_tail, norm_two)], axis=0)
    wide = total_over(after(wide, send_mixed_one), "mp")
    last_two = Total(jnp.concatenate([second_feed_two, second_mixed_two, wide], axis=0))
    input_gradient = jnp.concatenate(
        [
            back_one[j][2][:step].astype(F32) + after(last_flights[j], send_mixed_one).astype(F32) + norm_one[j][0][:step]
            for j in pair
        ],
        axis=0,
    )
    seconds_two = last_two.rest()
    seconds_two, wide = seconds_two[:32], seconds_two[32:].reshape(2, 8, cols)
    base_feed_one, second_feed_one = feed_second(sums_feed_one, *m_feed_one)
    base_mixed_one, second_mixed_one = mixed_second(sums_mixed_one, mixed_one, width)
    seconds_one = total_over(jnp.concatenate([second_feed_one, second_mixed_one], axis=0), "dp")
    seconds_feed_one, seconds_mixed_one = seconds_one[:16], seconds_one[16:]
    gain_sum = jnp.concatenate([wide[:, 3:4], wide[:, 0:1]], axis=1)
    shift_sum = jnp.concatenate([wide[:, 5:6], wide[:, 4:5], wide[:, 2:3], wide[:, 1:2]], axis=1)
    held_feed = feed_error(base_feed_two, seconds_two[:16], *m_feed_two, 1, replicas, None)
    held_mixed = mixed_error(base_mixed_two, seconds_two[16:32], mixed_two, 1, replicas, None)
    new_e_in, new_e_out = feed_error(base_feed_one, seconds_feed_one, *m_feed_one, 0, replicas, held_feed)
    new_e_qkv, new_e_o = mixed_error(base_mixed_one, seconds_mixed_one, mixed_one, 0, replicas, held_mixed)
    member_errors = [flip(new_e_qkv), new_e_o, new_e_in, new_e_out]

    bias_rows = (sums_mixed_one[24], sums_two[48])
    bias_qv = jnp.stack([jnp.stack([row[256 : 256 + width], row[512 : 512 + width]]) for row in bias_rows])
    bias_in = jnp.stack([sums_feed_one[16], sums_two[16]])

    rank = q_in.shape[2]
    kept = []
    for weight, moment in ((w_qkv, m_qkv), (w_o, m_o), (w_in, m_in), (flip(w_out), flip(m_out))):
        kept.extend([weight, moment])
    factors = [(2, 3, rank, cols), (2, rank, width), (2, rank, cols), (2, rank, cols)]
    factors += [(2, 3, rank, width), (2, rank, cols), (2, rank, cols), (2, rank, cols)]
    new_w_qkv, new_m_qkv, new_w_o, new_m_o, new_w_in, new_m_in, new_w_out, new_m_out, *factors = call(
        lambda *refs: renew_kernel(replicas, *refs), [[a.shape, F32] for a in kept] + [[shape, F32] for shape in factors],
        [
            base_feed_one, base_mixed_one, base_feed_two, base_mixed_two,
            seconds_feed_one, seconds_mixed_one, seconds_two, *kept,
        ],
        "renew", 1 << 24, 24, flags, range(7, 15), range(16),
    )
    new_w_out, new_m_out = flip(new_w_out), flip(new_m_out)
    new_m_qv = MOMENTUM * m_qv + bias_qv / replicas
    new_m_bin = MOMENTUM * m_bin + bias_in / replicas
    new_m_gain = MOMENTUM * m_gain + gain_sum / replicas
    new_m_shift = MOMENTUM * m_shift + shift_sum / replicas
    outer = [flip(value) for value in factors[:4]]
    inner = [flip(value) for value in factors[4:]]
    return (
        output, input_gradient, new_w_qkv, new_w_o, new_w_in, new_w_out,
        b_qv - RATE * new_m_qv, b_in - RATE * new_m_bin, ln_gain - RATE * new_m_gain, shifts - RATE * new_m_shift,
        new_m_qkv, new_m_o, new_m_in, new_m_out, new_m_qv, new_m_bin, new_m_gain, new_m_shift,
        *member_errors, *outer, *inner,
    )


def solution(mesh):
    in_specs = (
        P(("dp", "mp"), None), P(("dp", "mp"), None), P("dp", None), P("dp"),
        P(None, None, "dp", "mp"), P(None, "mp", "dp"), P(None, "dp", "mp"), P(None, "mp", "dp"),
        P(None, None, "mp"), P(None, "mp"), P(), P(),
        P(None, None, "dp", "mp"), P(None, "mp", "dp"), P(None, "dp", "mp"), P(None, "mp", "dp"),
        P(None, None, "mp"), P(None, "mp"), P(), P(),
        P("dp", None, None, None, "mp"), P("dp", None, "mp", None), P("dp", None, None, "mp"), P("dp", None, "mp", None),
        P(None, None, "mp", None), P(None, "mp", None), P(None, "mp", None), P(None, "mp", None),
    )
    out_specs = (
        P(("dp", "mp"), None), P(("dp", "mp"), None),
        P(None, None, "dp", "mp"), P(None, "mp", "dp"), P(None, "dp", "mp"), P(None, "mp", "dp"),
        P(None, None, "mp"), P(None, "mp"), P(), P(),
        P(None, None, "dp", "mp"), P(None, "mp", "dp"), P(None, "dp", "mp"), P(None, "mp", "dp"),
        P(None, None, "mp"), P(None, "mp"), P(), P(),
        P("dp", None, None, None, "mp"), P("dp", None, "mp", None), P("dp", None, None, "mp"), P("dp", None, "mp", None),
        P(None, None, "mp", None), P(None, "mp", None), P(None, "mp", None), P(None, "mp", None),
        P(None, None, "mp", None), P(None, "mp", None), P(None, "mp", None), P(None, "mp", None),
    )
    return jax.shard_map(per_device, mesh=mesh, in_specs=in_specs, out_specs=out_specs, check_vma=False)
```
